128 devices in a mesh: dp: 2 (over core), pipe: 2 (over x_hi), expert: 32 (over z, y, x_lo).
Axes of the slice: x: 4 (x_hi: 2, x_lo: 2; x = x_hi * 2 + x_lo), y: 4, z: 4, core: 2. Of those that a mesh axis runs over, the one named last changes fastest.
Arguments:
- saved_inputs: bfloat16 [2, 4, 128, 3072], P('pipe', None, 'dp'), may hold values from -6 to 6
- top_grad: bfloat16 [4, 128, 3072], P(None, 'dp'), may hold values from -6 to 6
- routes: int32 [2, 4, 128, 2], P('pipe', None, 'dp'), may hold values from 0 to 3, all different within a row; in each aligned block of 64 rows (0 to 63, 64 to 127, ..., all dimensions but the last counted through in order) at most 48 rows name the same one
- mix_weights: float32 [2, 4, 128, 2], P('pipe', None, 'dp'), may hold values from 0.2 to 0.8
- w_gate: bfloat16 [2, 32, 1, 3072, 1024], P('pipe', 'expert', None, None, 'dp'), may hold values from -0.109375 to 0.109375
- w_up: bfloat16 [2, 32, 1, 3072, 1024], P('pipe', 'expert', None, None, 'dp'), may hold values from -0.109375 to 0.109375
- w_down: bfloat16 [2, 32, 1, 1024, 3072], P('pipe', 'expert', None, 'dp'), may hold values from -0.0625 to 0.0625
- q_prev: float32 [2, 32, 1, 3, 1024, 64], P('pipe', 'expert', None, None, 'dp'), may hold values from -6 to 6
Outputs:
- input_grads: bfloat16 [2, 4, 128, 3072], P('pipe', None, 'dp')
- basis: float32 [2, 32, 1, 3072, 64], P('pipe', 'expert', None, 'dp')
- q_next: float32 [2, 32, 1, 3, 1024, 64], P('pipe', 'expert', None, None, 'dp')
The draws below stay inside these ranges and needn't reach their ends.
Inputs may be any that keep to these rules, and one draw needn't show every extreme that they name: For every section, microbatch and aligned block of 64 tokens (the tokens of one index of dp), each expert is named by at most 48 routes, a bound that some block reaches; a token's 2 routes name different experts.
All inputs are finite; a program needn't handle non-finite values.
Results may differ from the reference program's by a relative error of at most 0.015.
Values may be sent and summed in bfloat16 or wider, within the bound.
No kernel may reach another device: no remote copies, remote signals or barrier semaphores. Data moves between devices by JAX's collectives and lax.ppermute only.
A program may use at most 128 MiB of HBM per device.

```python
import math
import jax
import jax.numpy as jnp
import numpy as np
from jax import lax

D = 3072
EXPERTS = 4
F = 8192
TOP = 2
R = 64
MICRO = 4
TOK_DEV = 64
EXP_DEV = 1
COPY = 8
FSLICE = 1024
CAP = 48
TOKENS = 128
SECTIONS = 2
N_DP = 2
N_PIPE = 2
N_EXPERT = 32


def block_levels(stream_key, extent, cuts, smallest, largest):
    factor_of, own = 1.0, jax.random.fold_in(stream_key, 6)
    for position, blocks in cuts:
        heights = jnp.exp(jax.random.uniform(jax.random.fold_in(own, position), (blocks,), jnp.float32, smallest / len(cuts), largest / len(cuts)))
        factor_of = factor_of * jnp.repeat(heights, extent[position] // blocks).reshape([-1 if axis == position else 1 for axis in range(len(extent))])
    return factor_of


def shared_out(own_key, own, number, rows, number_of, top, reach, lean):
    sequence = jax.random.permutation(own_key, number_of)
    heavy_load, ordinary = load_shares(number_of, rows * top, reach, lean, True), load_shares(number_of, rows * top, reach, lean, False)
    places = jnp.arange(number_of)

    def named(sizes, turn):
        used = int((sizes > 0).sum())
        fixed = max(1, used // 4)
        passed = fixed + (places - fixed + turn * (used - fixed)) % max(1, number_of - fixed)
        return jnp.zeros((number_of,), jnp.int32).at[sequence[jnp.where(places < fixed, places, passed)]].set(jnp.asarray(sizes, jnp.int32))

    sizes = jnp.where(number % 4 == 0, named(heavy_load, number // 4), named(ordinary, number - number // 4 - 1))
    mixed = jax.random.permutation(jax.random.fold_in(own, 3), number_of)
    donor, sink = mixed[0:number_of // 2 * 2:2], mixed[1:number_of // 2 * 2:2]
    slack = jnp.minimum(sizes[donor] - 1, reach - sizes[sink]) // 2
    slack = jnp.where((donor == sequence[0]) | (sink == sequence[0]) | (sizes[sink] == 0), 0, jnp.maximum(slack, 0))
    passed = jax.random.randint(jax.random.fold_in(own, 4), (number_of // 2,), 0, 1 << 20) % (slack + 1)
    sizes = sizes.at[donor].add(-passed).at[sink].add(passed)
    items = jnp.searchsorted(jnp.cumsum(sizes), jnp.arange(rows * top), side="right").astype(jnp.int32)
    listing = items.reshape(top, rows).T
    listing = listing[jax.random.permutation(jax.random.fold_in(own, 1), rows)]
    turn = jax.random.randint(jax.random.fold_in(own, 2), (rows, 1), 0, top)
    return jnp.take_along_axis(listing, (jnp.arange(top)[None, :] + turn) % top, axis=1)


def load_shares(number_of, total, reach, lean, full):
    loads = [(1 << 20) // math.isqrt(rank ** lean) + 1 for rank in range(1, number_of + 1)]
    largest = reach if full else min(reach, max(-(-total // number_of), total * loads[0] // sum(loads)))
    least = 1 if total - largest >= number_of - 1 else 0
    holding, surplus = [largest] + [least] * (number_of - 1), total - largest - least * (number_of - 1)
    while surplus > 0:
        movable = [i for i in range(1, number_of) if holding[i] < largest] or [i for i in range(1, number_of) if holding[i] < reach]
        whole, remaining = sum([loads[i] for i in movable]), surplus
        for i in movable:
            addition = min(reach - holding[i], max(1, remaining * loads[i] // whole), surplus)
            holding[i] = holding[i] + addition
            surplus = surplus - addition
    return np.array(holding)


def centred(rng, shape, spread, reach, pieces=(), held_as=jnp.bfloat16):
    values = jax.random.normal(rng, shape, jnp.float32) * spread
    if len(pieces) > 0:
        values = block_levels(rng, shape, pieces, -0.22, 0.18) * values
    return jnp.clip(values, min=-reach, max=reach).astype(held_as)


def setup_inputs(seed: int = 0) -> dict:
    keys = jax.random.split(jax.random.key(seed), 9)
    saved_inputs = centred(keys[0], (SECTIONS, MICRO, TOKENS, D), 1.0, 6.0, ((0, 2), (2, 2)))
    top_grad = centred(keys[1], (MICRO, TOKENS, D), 1.0, 6.0, ((1, 2),))
    routes_keys = jax.random.split(jax.random.fold_in(keys[2], 1), SECTIONS * MICRO * TOKENS // TOK_DEV)
    routes_turns = jax.random.permutation(jax.random.fold_in(keys[2], 3), SECTIONS * MICRO * TOKENS // TOK_DEV)
    routes = jax.vmap(lambda own, number: shared_out(jax.random.fold_in(keys[2], 2), own, number, TOK_DEV, EXPERTS, TOP, CAP, 2))(routes_keys, routes_turns).reshape((SECTIONS, MICRO, TOKENS, TOP))
    mix_weights = jnp.clip(0.2 + 0.6 * jax.random.uniform(keys[3], (SECTIONS, MICRO, TOKENS, TOP), jnp.float32) ** block_levels(keys[3], (SECTIONS, MICRO, TOKENS, TOP), ((0, 2), (2, 2)), -0.2, 0.2), 0.2, 0.8)
    w_gate = centred(keys[4], (SECTIONS, N_EXPERT, EXP_DEV, D, FSLICE), D ** -0.5, 0.109375, ((0, 2), (1, 32), (4, 2)))
    w_up = centred(keys[5], (SECTIONS, N_EXPERT, EXP_DEV, D, FSLICE), D ** -0.5, 0.109375, ((0, 2), (1, 32), (4, 2)))
    w_down = centred(keys[6], (SECTIONS, N_EXPERT, EXP_DEV, FSLICE, D), F ** -0.5, 0.0625, ((0, 2), (1, 32), (3, 2)))
    q_prev = centred(keys[7], (SECTIONS, N_EXPERT, EXP_DEV, 3, FSLICE, R), 1.0, 6.0, ((0, 2), (1, 32), (4, 2)), jnp.float32)
    return dict(saved_inputs=saved_inputs, top_grad=top_grad, routes=routes, mix_weights=mix_weights, w_gate=w_gate, w_up=w_up, w_down=w_down, q_prev=q_prev)


def slot_tables(route_rows, mix_rows):
    token_count = route_rows.shape[0]
    flat_routes = route_rows.reshape(-1).astype(jnp.int32)
    one_hot = (flat_routes[:, None] == jnp.arange(EXPERTS, dtype=jnp.int32)[None, :]).astype(jnp.int32)
    rank_in_expert = lax.optimization_barrier(jnp.sum(jnp.cumsum(one_hot, axis=0) * one_hot, axis=1)) - 1
    slot_ids = flat_routes * CAP + rank_in_expert
    slot_hits = (slot_ids[:, None] == jnp.arange(EXPERTS * CAP, dtype=jnp.int32)[None, :]).astype(jnp.float32)
    slot_hits = slot_hits.reshape(token_count, TOP, EXPERTS * CAP)
    picker = lax.optimization_barrier(jnp.sum(slot_hits, axis=1)).T
    weigher = lax.optimization_barrier(jnp.sum(slot_hits * mix_rows[:, :, None].astype(jnp.float32), axis=1)).T
    return (picker, weigher)

def expert_grads(input_rows, grad_rows, gate_weight, up_weight, down_weight):
    pre_gate = jnp.dot(input_rows.astype(jnp.float32), gate_weight.astype(jnp.float32), preferred_element_type=jnp.float32)
    pre_up = jnp.dot(input_rows.astype(jnp.float32), up_weight.astype(jnp.float32), preferred_element_type=jnp.float32)
    sigmoid_gate = jax.nn.sigmoid(pre_gate)
    silu_gate = pre_gate * sigmoid_gate
    hidden = (silu_gate * pre_up).astype(jnp.bfloat16)
    grad_hidden = lax.dot_general(grad_rows.astype(jnp.float32), down_weight.astype(jnp.float32), (((1,), (1,)), ((), ())), preferred_element_type=jnp.float32)
    grad_gate = (grad_hidden * pre_up * sigmoid_gate * (1.0 + pre_gate * (1.0 - sigmoid_gate))).astype(jnp.bfloat16)
    grad_up = (grad_hidden * silu_gate).astype(jnp.bfloat16)
    input_rows_grad = lax.dot_general(grad_gate.astype(jnp.float32), gate_weight.astype(jnp.float32), (((1,), (1,)), ((), ())), preferred_element_type=jnp.float32)
    input_rows_grad = input_rows_grad + lax.dot_general(grad_up.astype(jnp.float32), up_weight.astype(jnp.float32), (((1,), (1,)), ((), ())), preferred_element_type=jnp.float32)
    gate_total = lax.dot_general(input_rows.astype(jnp.float32), grad_gate.astype(jnp.float32), (((0,), (0,)), ((), ())), preferred_element_type=jnp.float32)
    up_total = lax.dot_general(input_rows.astype(jnp.float32), grad_up.astype(jnp.float32), (((0,), (0,)), ((), ())), preferred_element_type=jnp.float32)
    down_total = lax.dot_general(grad_rows.astype(jnp.float32), hidden.astype(jnp.float32), (((0,), (0,)), ((), ())), preferred_element_type=jnp.float32)
    return (input_rows_grad, gate_total, up_total, down_total)

def orthonormal(lower_factor, factor):
    return jax.scipy.linalg.solve_triangular(lower_factor, factor.T, lower=True).T

def reference(saved_inputs, top_grad, routes, mix_weights, w_gate, w_up, w_down, q_prev):
    blocks = N_DP
    groups = N_EXPERT // COPY
    highest = lax.Precision.HIGHEST
    arriving_all = top_grad
    grads_list, basis_list, q_list = ([], [], [])
    for section_index in range(N_PIPE - 1, -1, -1):
        gate_section = w_gate[section_index].reshape(groups, COPY, EXP_DEV, D, FSLICE).transpose(0, 2, 3, 1, 4).reshape(EXPERTS, D, F)
        up_section = w_up[section_index].reshape(groups, COPY, EXP_DEV, D, FSLICE).transpose(0, 2, 3, 1, 4).reshape(EXPERTS, D, F)
        down_section = w_down[section_index].reshape(groups, COPY, EXP_DEV, FSLICE, D).transpose(0, 2, 1, 3, 4).reshape(EXPERTS, F, D)
        right_section = q_prev[section_index].reshape(groups, COPY, EXP_DEV, 3, FSLICE, R).transpose(0, 2, 3, 1, 4, 5).reshape(EXPERTS, 3, F, R)

        def regroup(slots):
            slots = slots.reshape(blocks, EXPERTS, CAP, D).transpose(1, 0, 2, 3)
            return slots.reshape(EXPERTS, blocks * CAP, D)

        def per_expert(inputs):
            return expert_grads(inputs[0], inputs[1], inputs[2], inputs[3], inputs[4])

        def one_micro(totals, inputs):
            tokens_in, arriving, route_micro, mix_micro = inputs
            input_blocks = tokens_in.reshape(blocks, TOK_DEV, D).astype(jnp.float32)
            arriving_blocks = arriving.reshape(blocks, TOK_DEV, D).astype(jnp.float32)
            pickers, weighers = jax.vmap(slot_tables)(route_micro.reshape(blocks, TOK_DEV, TOP), mix_micro.reshape(blocks, TOK_DEV, TOP))
            input_slots = jnp.einsum('bjt,btd->bjd', pickers, input_blocks, precision=highest).astype(jnp.bfloat16)
            grad_slots = jnp.einsum('bjt,btd->bjd', weighers, arriving_blocks, precision=highest).astype(jnp.bfloat16)
            slot_grads, gate_total, up_total, down_total = lax.map(per_expert, (regroup(input_slots), regroup(grad_slots), gate_section, up_section, down_section))
            slot_grads = slot_grads.reshape(EXPERTS, blocks, CAP, D).transpose(1, 0, 2, 3).reshape(blocks, EXPERTS * CAP, D)
            combined = arriving_blocks + jnp.einsum('bjt,bjd->btd', pickers, slot_grads, precision=highest)
            totals = (totals[0] + gate_total, totals[1] + up_total, totals[2] + down_total)
            return (totals, combined.astype(jnp.bfloat16).reshape(TOKENS, D))
        empty_grad = jnp.zeros((EXPERTS, D, F), jnp.float32)
        totals, section_grads = lax.scan(one_micro, (empty_grad, empty_grad, empty_grad), (saved_inputs[section_index], arriving_all, routes[section_index], mix_weights[section_index]))
        arriving_all = section_grads
        factor = jnp.einsum('edf,efr->edr', totals[0], right_section[:, 0], precision=highest)
        factor = factor + jnp.einsum('edf,efr->edr', totals[1], right_section[:, 1], precision=highest)
        factor = factor + jnp.einsum('edf,efr->edr', totals[2], right_section[:, 2], precision=highest)
        gram_matrix = jnp.einsum('edr,eds->ers', factor, factor, precision=highest)
        lower_factor = jnp.linalg.cholesky(gram_matrix)
        ortho = jax.vmap(orthonormal)(lower_factor, factor)
        scale_back = math.sqrt(float(MICRO * TOKENS))
        q_parts = [jnp.einsum('edf,edr->efr', totals[part], ortho, precision=highest) / scale_back for part in range(3)]
        q_new = jnp.stack(q_parts, axis=1)
        q_new = q_new.reshape(groups, EXP_DEV, 3, COPY, FSLICE, R).transpose(0, 3, 1, 2, 4, 5).reshape(N_EXPERT, EXP_DEV, 3, FSLICE, R)
        basis_now = (ortho * math.sqrt(float(D))).reshape(groups, 1, EXP_DEV, D, R)
        basis_now = jnp.broadcast_to(basis_now, (groups, COPY, EXP_DEV, D, R)).reshape(N_EXPERT, EXP_DEV, D, R)
        grads_list.insert(0, section_grads)
        basis_list.insert(0, basis_now)
        q_list.insert(0, q_new)
    return (jnp.stack(grads_list), jnp.stack(basis_list), jnp.stack(q_list))
```

```python
import math

import jax
import jax.numpy as jnp
from jax import lax
from jax.sharding import PartitionSpec as P

D = 3072
EXPERTS = 4
R = 64
MICRO = 4

BF = jnp.bfloat16
F32 = jnp.float32


def swap_cores(value):
    return lax.ppermute(value, "dp", [(0, 1), (1, 0)])


def exchange(pieces, groups=None):
    return lax.all_to_all(pieces, "expert", 0, 0, tiled=True, axis_index_groups=groups)


def times(a, b, ca=1, cb=0, precision=None):
    return lax.dot_general(
        a, b, (((ca,), (cb,)), ((), ())), preferred_element_type=F32, precision=precision
    )


def shards(saved_inputs, top_grad, routes, mix_weights, w_gate, w_up, w_down, q_prev):
    sections = lax.axis_size("pipe")
    section_index = lax.axis_index("pipe")
    peers = lax.axis_size("expert")
    expert_index = lax.axis_index("expert")
    replicas = lax.axis_size("dp")
    dp_index = lax.axis_index("dp")
    gate, up, down = (w_gate[0, 0, 0], w_up[0, 0, 0], w_down[0, 0, 0])
    right = q_prev[0, 0, 0]
    copies = peers // EXPERTS
    token_count = saved_inputs.shape[2]
    rows = MICRO * token_count
    rows_each = rows // peers
    plane = [[c * copies + i for i in range(copies)] for c in range(EXPERTS)]
    own_expert = expert_index // copies

    own_inputs = saved_inputs[0].reshape(rows, D)
    top_rows = top_grad.reshape(rows, D)
    hits = routes[0].reshape(rows, 2) == own_expert
    own_weight = jnp.sum(jnp.where(hits, mix_weights[0].reshape(rows, 2), 0.0), axis=1)
    weight = jnp.concatenate([own_weight, swap_cores(own_weight)])[:, None]
    inputs = jnp.concatenate([own_inputs, swap_cores(own_inputs)])

    pre_gate = times(inputs, gate)
    pre_up = times(inputs, up)
    sigmoid_gate = jax.nn.sigmoid(pre_gate)
    silu_gate = pre_gate * sigmoid_gate
    hidden = (silu_gate * pre_up).astype(BF)
    slope = pre_up * sigmoid_gate * (1.0 + pre_gate * (1.0 - sigmoid_gate))

    def phase(arriving):
        both = jnp.concatenate([arriving, swap_cores(arriving)])
        grad_rows = (weight * both.astype(F32)).astype(BF)
        grad_hidden = times(grad_rows, down, 1, 1)
        grad_gate = (grad_hidden * slope).astype(BF)
        grad_up = (grad_hidden * silu_gate).astype(BF)
        partial = times(grad_gate, gate, 1, 1) + times(grad_up, up, 1, 1)
        mine = partial[:rows] + swap_cores(partial[rows:].astype(BF)).astype(F32)
        pieces = exchange(mine.astype(BF).reshape(peers, rows_each, D))
        share = jnp.sum(pieces.astype(F32), axis=0)
        base = lax.dynamic_slice_in_dim(arriving, expert_index * rows_each, rows_each, 0)
        return (base.astype(F32) + share).astype(BF), grad_rows, grad_gate, grad_up

    def gathered(part):
        return exchange(jnp.broadcast_to(part, (peers, rows_each, D))).reshape(rows, D)

    part, _, _, _ = phase(top_rows)
    incoming = gathered(lax.ppermute(part, "pipe", [(i, i - 1) for i in range(1, sections)]))
    arriving = jnp.where(section_index == sections - 1, top_rows, incoming)
    part, grad_rows, grad_gate, grad_up = phase(arriving)
    produced = gathered(part)

    right16 = right.astype(BF)
    sums = jnp.concatenate(
        [times(grad_gate, right16[0]) + times(grad_up, right16[1]), times(hidden, right16[2])],
        axis=1,
    )
    other = swap_cores(sums)
    sums = sums + jnp.concatenate([other[rows:], other[:rows]])
    pieces = exchange(sums.reshape(copies, replicas * rows // copies, 2 * R), plane)
    piece = jnp.sum(pieces, axis=0)
    sums = exchange(jnp.broadcast_to(piece, (copies, *piece.shape)), plane)
    sums = sums.reshape(replicas * rows, 2 * R).astype(BF)
    factor = times(inputs, sums[:, :R], 0, 0) + times(grad_rows, sums[:, R:], 0, 0)
    gram_matrix = times(factor, factor, 0, 0, lax.Precision.HIGHEST)
    lower_factor = jnp.linalg.cholesky(gram_matrix)
    ortho = jax.scipy.linalg.solve_triangular(lower_factor, factor.T, lower=True).T
    ortho16 = ortho.astype(BF)
    along_inputs = times(inputs, ortho16).astype(BF)
    along_grads = times(grad_rows, ortho16).astype(BF)
    scale = 1.0 / math.sqrt(float(replicas * rows))
    q_next = jnp.stack(
        [
            times(grad_gate, along_inputs, 0, 0),
            times(grad_up, along_inputs, 0, 0),
            times(hidden, along_grads, 0, 0),
        ]
    )
    row_count = D // replicas
    basis = lax.dynamic_slice_in_dim(ortho, dp_index * row_count, row_count, 0)
    return (
        produced.reshape(1, MICRO, token_count, D),
        (basis * math.sqrt(float(D)))[None, None, None],
        (q_next * scale)[None, None, None],
    )


def solution(mesh):
    placed = (
        P("pipe", None, "dp", None),
        P(None, "dp", None),
        P("pipe", None, "dp", None),
        P("pipe", None, "dp", None),
        P("pipe", "expert", None, None, "dp"),
        P("pipe", "expert", None, None, "dp"),
        P("pipe", "expert", None, "dp", None),
        P("pipe", "expert", None, None, "dp", None),
    )
    return jax.shard_map(
        shards,
        mesh=mesh,
        in_specs=placed,
        out_specs=(
            P("pipe", None, "dp", None),
            P("pipe", "expert", None, "dp", None),
            P("pipe", "expert", None, None, "dp", None),
        ),
        check_vma=False,
    )
```

```python
import math

import jax
import jax.numpy as jnp
from jax import lax
from jax.sharding import PartitionSpec as P

D = 3072
EXPERTS = 4
R = 64
MICRO = 4
CAP = 48

BF = jnp.bfloat16
F32 = jnp.float32


def swap_cores(value):
    return lax.ppermute(value, "dp", [(0, 1), (1, 0)])


def exchange(pieces):
    return lax.all_to_all(pieces, "expert", 0, 0, tiled=True)


def times(a, b, ca=1, cb=0, precision=None):
    return lax.dot_general(
        a, b, (((ca,), (cb,)), ((), ())), preferred_element_type=F32, precision=precision
    )


def slots_of(route_rows):
    flat = route_rows.reshape(MICRO, -1)
    count = flat.shape[1]
    earlier = lax.broadcasted_iota(jnp.int32, (count, count), 1) < lax.broadcasted_iota(
        jnp.int32, (count, count), 0
    )
    same = (flat[:, :, None] == flat[:, None, :]) & earlier[None]
    return jnp.sum(same.astype(jnp.int32), axis=2).reshape(route_rows.shape)


def hit_table(ids, count):
    rows = lax.broadcasted_iota(jnp.int32, (count, ids.shape[0]), 0)
    return rows == ids[None, :, 0], rows == ids[None, :, 1]


def add_copies(values, copies):
    def x_pair(i):
        return i ^ 1

    def y_pair(i):
        return i ^ 2

    def y_cross(i):
        y = i // 2 % 4
        return i + (((3 - y) % 4) - y) * 2

    for partner in (x_pair, y_pair, y_cross):
        route = [(i, partner(i)) for i in range(copies * EXPERTS)]
        values = values + lax.ppermute(values, "expert", route)
    return values


def shards(saved_inputs, top_grad, routes, mix_weights, w_gate, w_up, w_down, q_prev):
    sections = lax.axis_size("pipe")
    last = lax.axis_index("pipe") == sections - 1
    peers = lax.axis_size("expert")
    expert_index = lax.axis_index("expert")
    replicas = lax.axis_size("dp")
    dp_index = lax.axis_index("dp")
    gate, up, down = (w_gate[0, 0, 0], w_up[0, 0, 0], w_down[0, 0, 0])
    right = q_prev[0, 0, 0].astype(BF)
    copies = peers // EXPERTS
    tokens = saved_inputs.shape[2]
    rows = MICRO * tokens
    slots = MICRO * CAP
    columns = D // copies
    major, minor = (expert_index // copies, expert_index % copies)

    own_inputs = saved_inputs[0].reshape(rows, D)
    top_rows = top_grad.reshape(rows, D)
    rank = slots_of(routes[0])
    mix = mix_weights[0].reshape(rows, 2)
    micro_start = (jnp.arange(MICRO, dtype=jnp.int32) * CAP)[:, None, None]
    own_ids = jnp.where(routes[0] == major, micro_start + rank, -1).reshape(rows, 2)
    first, second = hit_table(own_ids, slots)
    own_pick = (first | second).astype(BF)
    weight = jnp.sum(
        jnp.where(first, mix[None, :, 0], 0.0) + jnp.where(second, mix[None, :, 1], 0.0),
        axis=1,
        keepdims=True,
    )
    part_ids = lax.dynamic_index_in_dim(routes[0] * CAP + rank, major, 0, keepdims=False)
    first, second = hit_table(part_ids, EXPERTS * CAP)
    part_pick = (first | second).astype(BF)

    def both_cores(own):
        return jnp.concatenate([own, swap_cores(own)])

    inputs = both_cores(times(own_pick, own_inputs).astype(BF))
    pre_gate = times(inputs, gate)
    pre_up = times(inputs, up)
    sigmoid_gate = jax.nn.sigmoid(pre_gate)
    silu_gate = pre_gate * sigmoid_gate
    hidden = (silu_gate * pre_up).astype(BF)
    slope = pre_up * sigmoid_gate * (1.0 + pre_gate * (1.0 - sigmoid_gate))

    def phase(own_rows, base):
        grad_rows = both_cores((weight * own_rows).astype(BF))
        grad_hidden = times(grad_rows, down, 1, 1)
        grad_gate = (grad_hidden * slope).astype(BF)
        grad_up = (grad_hidden * silu_gate).astype(BF)
        partial = times(grad_gate, gate, 1, 1) + times(grad_up, up, 1, 1)
        mine = partial[:slots] + swap_cores(partial[slots:].astype(BF)).astype(F32)
        mine = mine.astype(BF).reshape(MICRO, CAP, copies, columns).transpose(0, 2, 1, 3)
        pieces = exchange(mine.reshape(peers, CAP, columns))
        summed = jnp.sum(pieces.astype(F32).reshape(EXPERTS, copies, CAP, columns), axis=1)
        share = times(
            part_pick.astype(F32),
            summed.reshape(EXPERTS * CAP, columns),
            0,
            0,
            lax.Precision.HIGHEST,
        )
        return (base.astype(F32) + share).astype(BF), grad_rows, grad_gate, grad_up

    top_part = lax.dynamic_slice(
        top_grad, (major, 0, minor * columns), (1, tokens, columns)
    ).reshape(tokens, columns)
    part, _, _, _ = phase(times(own_pick, top_rows), top_part)
    incoming = lax.ppermute(part, "pipe", [(i, i - 1) for i in range(1, sections)])
    base = jnp.where(last, top_part, incoming)
    listed = times(part_pick, base).astype(BF).reshape(EXPERTS, 1, CAP, columns)
    pieces = jnp.broadcast_to(listed, (EXPERTS, copies, CAP, columns))
    own_rows = exchange(pieces.reshape(peers, CAP, columns))
    own_rows = own_rows.reshape(MICRO, copies, CAP, columns).transpose(0, 2, 1, 3)
    part, grad_rows, grad_gate, grad_up = phase(own_rows.reshape(slots, D).astype(F32), base)
    produced = exchange(jnp.broadcast_to(part, (peers, tokens, columns)))
    produced = produced.reshape(MICRO, copies, tokens, columns).transpose(0, 2, 1, 3)

    sums = jnp.concatenate(
        [times(grad_gate, right[0]) + times(grad_up, right[1]), times(hidden, right[2])], axis=1
    )
    other = swap_cores(sums)
    sums = sums + jnp.concatenate([other[slots:], other[:slots]])
    sums = add_copies(sums, copies).astype(BF)
    factor = times(inputs, sums[:, :R], 0, 0) + times(grad_rows, sums[:, R:], 0, 0)
    gram_matrix = times(factor, factor, 0, 0, lax.Precision.HIGHEST)
    lower_factor = jnp.linalg.cholesky(gram_matrix)
    ortho = jax.scipy.linalg.solve_triangular(lower_factor, factor.T, lower=True).T
    ortho16 = ortho.astype(BF)
    along_inputs = times(inputs, ortho16).astype(BF)
    along_grads = times(grad_rows, ortho16).astype(BF)
    scale = 1.0 / math.sqrt(float(replicas * rows))
    q_next = jnp.stack(
        [
            times(grad_gate, along_inputs, 0, 0),
            times(grad_up, along_inputs, 0, 0),
            times(hidden, along_grads, 0, 0),
        ]
    )
    row_count = D // replicas
    basis = lax.dynamic_slice_in_dim(ortho, dp_index * row_count, row_count, 0)
    return (
        produced.reshape(1, MICRO, tokens, D),
        (basis * math.sqrt(float(D)))[None, None, None],
        (q_next * scale)[None, None, None],
    )


def solution(mesh):
    placed = (
        P("pipe", None, "dp", None),
        P(None, "dp", None),
        P("pipe", None, "dp", None),
        P("pipe", None, "dp", None),
        P("pipe", "expert", None, None, "dp"),
        P("pipe", "expert", None, None, "dp"),
        P("pipe", "expert", None, "dp", None),
        P("pipe", "expert", None, None, "dp", None),
    )
    return jax.shard_map(
        shards,
        mesh=mesh,
        in_specs=placed,
        out_specs=(
            P("pipe", None, "dp", None),
            P("pipe", "expert", None, "dp", None),
            P("pipe", "expert", None, None, "dp", None),
        ),
        check_vma=False,
    )
```

```python
import math

import jax
import jax.numpy as jnp
from jax import lax
from jax.experimental import pallas as pl
from jax.experimental.pallas import tpu as pltpu
from jax.sharding import PartitionSpec as P

D = 3072
EXPERTS = 4
R = 64
MICRO = 4
CAP = 48

BF = jnp.bfloat16
F32 = jnp.float32


def swap_cores(value):
    return lax.ppermute(value, "dp", [(0, 1), (1, 0)])


def exchange(pieces):
    return lax.all_to_all(pieces, "expert", 0, 0, tiled=True)


def times(a, b, ca=1, cb=0, precision=None):
    return lax.dot_general(
        a, b, (((ca,), (cb,)), ((), ())), preferred_element_type=F32, precision=precision
    )


def slots_of(route_rows):
    flat = route_rows.reshape(MICRO, -1)
    count = flat.shape[1]
    earlier = lax.broadcasted_iota(jnp.int32, (count, count), 1) < lax.broadcasted_iota(
        jnp.int32, (count, count), 0
    )
    same = (flat[:, :, None] == flat[:, None, :]) & earlier[None]
    return jnp.sum(same.astype(jnp.int32), axis=2).reshape(route_rows.shape)


def hit_table(ids, count):
    rows = lax.broadcasted_iota(jnp.int32, (count, ids.shape[0]), 0)
    return rows == ids[None, :, 0], rows == ids[None, :, 1]


def add_copies(values, copies):
    def x_pair(i):
        return i ^ 1

    def y_pair(i):
        return i ^ 2

    def y_cross(i):
        y = i // 2 % 4
        return i + (((3 - y) % 4) - y) * 2

    for partner in (x_pair, y_pair, y_cross):
        route = [(i, partner(i)) for i in range(copies * EXPERTS)]
        values = values + lax.ppermute(values, "expert", route)
    return values


def eliminate(gram_ref, inverse_ref):
    height = 8
    lanes = lax.broadcasted_iota(jnp.int32, (height, 2 * R), 1)
    depth = lax.broadcasted_iota(jnp.int32, (height, 2 * R), 0)
    blocks = []
    for b in range(R // height):
        held = jnp.concatenate([jnp.zeros((height, R), F32), gram_ref[pl.ds(b * height, height), :]], 1)
        blocks.append(jnp.where(lanes == depth + b * height, 1.0, held))
    for k in range(R):
        at, row = divmod(k, height)
        pivot_row = blocks[at][row : row + 1, :]
        pivot_row = pivot_row * (1.0 / pivot_row[:, R + k : R + k + 1])
        for b in range((k + 1) // height, R // height):
            below = blocks[b] - blocks[b][:, R + k : R + k + 1] * pivot_row
            blocks[b] = jnp.where(depth + b * height > k, below, blocks[b]) if b == at else below
    for b in range(R // height):
        diagonal = jnp.where(lanes == depth + R + b * height, blocks[b], 0.0)
        pivots = jnp.sum(diagonal, axis=1, keepdims=True)
        inverse_ref[pl.ds(b * height, height), :] = (blocks[b] * lax.rsqrt(pivots))[:, :R]


def inverse_lower(gram_matrix):
    return pl.pallas_call(
        eliminate, out_shape=jax.ShapeDtypeStruct((R, R), F32), name="inverse_lower"
    )(gram_matrix)


def side_by_side(pieces):
    micro, copies, tokens, columns = pieces.shape

    def kernel(pieces_ref, out_ref, done):
        moves = [
            pltpu.make_async_copy(
                pieces_ref.at[:, c], out_ref.at[:, :, pl.ds(c * columns, columns)], done.at[c]
            )
            for c in range(copies)
        ]
        for move in moves:
            move.start()
        for move in moves:
            move.wait()

    return pl.pallas_call(
        kernel,
        out_shape=jax.ShapeDtypeStruct((micro, tokens, copies * columns), pieces.dtype),
        in_specs=[pl.BlockSpec(memory_space=pl.ANY)],
        out_specs=pl.BlockSpec(memory_space=pl.ANY),
        scratch_shapes=[pltpu.SemaphoreType.DMA((copies,))],
        name="side_by_side",
    )(pieces)


def shards(saved_inputs, top_grad, routes, mix_weights, w_gate, w_up, w_down, q_prev):
    sections = lax.axis_size("pipe")
    last = lax.axis_index("pipe") == sections - 1
    peers = lax.axis_size("expert")
    expert_index = lax.axis_index("expert")
    replicas = lax.axis_size("dp")
    dp_index = lax.axis_index("dp")
    gate, up, down = (w_gate[0, 0, 0], w_up[0, 0, 0], w_down[0, 0, 0])
    right = q_prev[0, 0, 0].astype(BF)
    copies = peers // EXPERTS
    tokens = saved_inputs.shape[2]
    rows = MICRO * tokens
    slots = MICRO * CAP
    columns = D // copies
    major, minor = (expert_index // copies, expert_index % copies)

    own_inputs = saved_inputs[0].reshape(rows, D)
    top_rows = top_grad.reshape(rows, D)
    rank = slots_of(routes[0])
    mix = mix_weights[0].reshape(rows, 2)
    micro_start = (jnp.arange(MICRO, dtype=jnp.int32) * CAP)[:, None, None]
    own_ids = jnp.where(routes[0] == major, micro_start + rank, -1).reshape(rows, 2)
    first, second = hit_table(own_ids, slots)
    own_pick = (first | second).astype(BF)
    weight = jnp.sum(
        jnp.where(first, mix[None, :, 0], 0.0) + jnp.where(second, mix[None, :, 1], 0.0),
        axis=1,
        keepdims=True,
    )
    part_ids = lax.dynamic_index_in_dim(routes[0] * CAP + rank, major, 0, keepdims=False)
    first, second = hit_table(part_ids, EXPERTS * CAP)
    part_pick = (first | second).astype(BF)

    def both_cores(own):
        return jnp.concatenate([own, swap_cores(own)])

    inputs = both_cores(times(own_pick, own_inputs).astype(BF))
    pre_gate = times(inputs, gate)
    pre_up = times(inputs, up)
    sigmoid_gate = jax.nn.sigmoid(pre_gate)
    silu_gate = pre_gate * sigmoid_gate
    hidden = (silu_gate * pre_up).astype(BF)
    slope = pre_up * sigmoid_gate * (1.0 + pre_gate * (1.0 - sigmoid_gate))

    def phase(own_rows, base):
        grad_rows = both_cores((weight * own_rows).astype(BF))
        grad_hidden = times(grad_rows, down, 1, 1)
        grad_gate = (grad_hidden * slope).astype(BF)
        grad_up = (grad_hidden * silu_gate).astype(BF)
        partial = times(grad_gate, gate, 1, 1) + times(grad_up, up, 1, 1)
        other = swap_cores(partial[slots:].astype(BF))
        mine = partial[:slots] + other.astype(F32)
        mine = mine.astype(BF).reshape(MICRO, CAP, copies, columns).transpose(0, 2, 1, 3)
        pieces = exchange(mine.reshape(peers, CAP, columns))
        summed = jnp.sum(pieces.astype(F32).reshape(EXPERTS, copies, CAP, columns), axis=1)
        share = times(
            part_pick.astype(F32),
            summed.reshape(EXPERTS * CAP, columns),
            0,
            0,
            lax.Precision.HIGHEST,
        )
        part = (base.astype(F32) + share).astype(BF)
        return part, grad_rows, grad_gate, grad_up

    top_part = lax.dynamic_slice(
        top_grad, (major, 0, minor * columns), (1, tokens, columns)
    ).reshape(tokens, columns)
    part, _, _, _ = phase(times(own_pick, top_rows), top_part)
    incoming = lax.ppermute(part, "pipe", [(i, i - 1) for i in range(1, sections)])
    base = jnp.where(last, top_part, incoming)
    listed = times(part_pick, base).astype(BF).reshape(EXPERTS, 1, CAP, columns)
    pieces = jnp.broadcast_to(listed, (EXPERTS, copies, CAP, columns))
    own_rows = exchange(pieces.reshape(peers, CAP, columns))
    own_rows = own_rows.reshape(MICRO, copies, CAP, columns).transpose(0, 2, 1, 3)
    part, grad_rows, grad_gate, grad_up = phase(own_rows.reshape(slots, D).astype(F32), base)
    produced = exchange(jnp.broadcast_to(part, (peers, tokens, columns)))
    produced = side_by_side(produced.reshape(MICRO, copies, tokens, columns))

    sums = jnp.concatenate(
        [times(grad_gate, right[0]) + times(grad_up, right[1]), times(hidden, right[2])], axis=1
    )
    other = swap_cores(sums)
    sums = sums + jnp.concatenate([other[slots:], other[:slots]])
    sums = add_copies(sums, copies).astype(BF)
    factor = times(inputs, sums[:, :R], 0, 0) + times(grad_rows, sums[:, R:], 0, 0)
    gram_matrix = times(factor, factor, 0, 0, lax.Precision.HIGHEST)
    inverse = inverse_lower(gram_matrix)
    ortho = times(factor, inverse, 1, 1, lax.Precision.HIGHEST)
    ortho16 = ortho.astype(BF)
    along_inputs = times(inputs, ortho16).astype(BF)
    along_grads = times(grad_rows, ortho16).astype(BF)
    scale = 1.0 / math.sqrt(float(replicas * rows))
    q_next = jnp.stack(
        [
            times(grad_gate, along_inputs, 0, 0),
            times(grad_up, along_inputs, 0, 0),
            times(hidden, along_grads, 0, 0),
        ]
    )
    row_count = D // replicas
    basis = lax.dynamic_slice_in_dim(ortho, dp_index * row_count, row_count, 0)
    return (
        produced.reshape(1, MICRO, tokens, D),
        (basis * math.sqrt(float(D)))[None, None, None],
        (q_next * scale)[None, None, None],
    )


def solution(mesh):
    placed = (
        P("pipe", None, "dp", None),
        P(None, "dp", None),
        P("pipe", None, "dp", None),
        P("pipe", None, "dp", None),
        P("pipe", "expert", None, None, "dp"),
        P("pipe", "expert", None, None, "dp"),
        P("pipe", "expert", None, "dp", None),
        P("pipe", "expert", None, None, "dp", None),
    )
    return jax.shard_map(
        shards,
        mesh=mesh,
        in_specs=placed,
        out_specs=(
            P("pipe", None, "dp", None),
            P("pipe", "expert", None, "dp", None),
            P("pipe", "expert", None, None, "dp", None),
        ),
        check_vma=False,
    )
```

```python
import math

import jax
import jax.numpy as jnp
from jax import lax
from jax.experimental import pallas as pl
from jax.experimental.pallas import tpu as pltpu
from jax.sharding import PartitionSpec as P

D = 3072
EXPERTS = 4
R = 64
MICRO = 4
CAP = 48

BF = jnp.bfloat16
F32 = jnp.float32


def swap_cores(value):
    return lax.ppermute(value, "dp", [(0, 1), (1, 0)])


def exchange(pieces):
    return lax.all_to_all(pieces, "expert", 0, 0, tiled=True)


def times(a, b, ca=1, cb=0, precision=None):
    return lax.dot_general(
        a, b, (((ca,), (cb,)), ((), ())), preferred_element_type=F32, precision=precision
    )


def slots_of(route_rows):
    flat = route_rows.reshape(MICRO, -1)
    count = flat.shape[1]
    earlier = lax.broadcasted_iota(jnp.int32, (count, count), 1) < lax.broadcasted_iota(
        jnp.int32, (count, count), 0
    )
    same = (flat[:, :, None] == flat[:, None, :]) & earlier[None]
    return jnp.sum(same.astype(jnp.int32), axis=2).reshape(route_rows.shape)


def hit_table(ids, count):
    rows = lax.broadcasted_iota(jnp.int32, (count, ids.shape[0]), 0)
    return rows == ids[None, :, 0], rows == ids[None, :, 1]


def add_copies(values, copies):
    def x_pair(i):
        return i ^ 1

    def y_pair(i):
        return i ^ 2

    def y_cross(i):
        y = i // 2 % 4
        return i + (((3 - y) % 4) - y) * 2

    for partner in (x_pair, y_pair, y_cross):
        route = [(i, partner(i)) for i in range(copies * EXPERTS)]
        rounded = values.astype(BF)
        other = lax.ppermute(rounded, "expert", route)
        values = rounded.astype(F32) + other.astype(F32)
    return values


def inverse_lower(gram):
    height = 8
    lanes = lax.broadcasted_iota(jnp.int32, (height, 2 * R), 1)
    depth = lax.broadcasted_iota(jnp.int32, (height, 2 * R), 0)
    blocks = []
    for b in range(R // height):
        rows = gram[b * height : (b + 1) * height, :]
        held = jnp.concatenate([jnp.zeros((height, R), F32), rows], 1)
        blocks.append(jnp.where(lanes == depth + b * height, 1.0, held))
    for k in range(R):
        at, row = divmod(k, height)
        pivot_row = blocks[at][row : row + 1, :]
        pivot_row = pivot_row * (1.0 / pivot_row[:, R + k : R + k + 1])
        for b in range((k + 1) // height, R // height):
            below = blocks[b] - blocks[b][:, R + k : R + k + 1] * pivot_row
            blocks[b] = jnp.where(depth + b * height > k, below, blocks[b]) if b == at else below
    for b in range(R // height):
        diagonal = jnp.where(lanes == depth + R + b * height, blocks[b], 0.0)
        pivots = jnp.sum(diagonal, axis=1, keepdims=True)
        blocks[b] = (blocks[b] * lax.rsqrt(pivots))[:, :R]
    return jnp.concatenate(blocks, axis=0)


def halves(value):
    high = value.astype(BF)
    return high, (value - high.astype(F32)).astype(BF)


def finish(dp_index, sums, squares, rows16, grads, token_total):
    wide = rows16[0].shape[1]
    half = wide // 2
    count = sums.shape[0]
    units = grads[0].shape[1]
    height = rows16[0].shape[0]

    def kernel(dp_ref, sums_ref, *refs):
        squares_hbm, rows_hbm, grads_hbm = (refs[:3], refs[3:7], refs[7:10])
        q_ref, basis_ref = refs[10:12]
        squares_ref, rows_ref, grads_ref, done = refs[12:]
        moves = [
            pltpu.make_async_copy(squares_hbm[i], squares_ref.at[i], done.at[i]) for i in range(3)
        ]
        moves += [
            pltpu.make_async_copy(grads_hbm[i], grads_ref.at[i], done.at[3 + i]) for i in range(3)
        ]
        start = pl.multiple_of(dp_ref[0] * half, half)
        moves += [
            pltpu.make_async_copy(
                rows_hbm[i].at[:, pl.ds(start, half)],
                rows_ref.at[pl.ds(i * height, height)],
                done.at[6 + i],
            )
            for i in range(4)
        ]
        for move in moves:
            move.start()
        turned = sums_ref[...].T
        of_inputs, of_grads = (turned[:R].astype(BF), turned[R:].astype(BF))
        for move in moves[:3]:
            move.wait()

        def twice(left, right, cb):
            high, low = halves(right)
            return times(left, high, 1, cb) + times(left, low, 1, cb)

        inputs_inputs, grads_inputs, grads_grads = (squares_ref[i] for i in range(3))
        along_inputs = twice(of_inputs, inputs_inputs, 0) + twice(of_grads, grads_inputs, 0)
        along_grads = twice(of_inputs, grads_inputs, 1) + twice(of_grads, grads_grads, 0)
        gram = twice(of_inputs, along_inputs, 1) + twice(of_grads, along_grads, 1)
        inverse = inverse_lower(0.5 * (gram + gram.T))
        exact = lax.Precision.HIGHEST
        weights = jnp.concatenate(
            [
                times(inverse, of_inputs.astype(F32), 1, 0, exact),
                times(inverse, of_grads.astype(F32), 1, 0, exact),
            ],
            axis=1,
        ).astype(BF)
        scale = 1.0 / math.sqrt(float(token_total))
        along_inputs = times(inverse, along_inputs, 1, 0, exact).astype(BF)
        along_grads = times(inverse, along_grads, 1, 0, exact).astype(BF)
        for move in moves[3:]:
            move.wait()
        q_ref[0] = times(along_inputs, grads_ref[0]) * scale
        q_ref[1] = times(along_inputs, grads_ref[1]) * scale
        q_ref[2] = times(along_grads, grads_ref[2]) * scale
        basis_ref[...] = times(weights, rows_ref[...]) * math.sqrt(float(wide))

    anywhere = pl.BlockSpec(memory_space=pl.ANY)
    return pl.pallas_call(
        kernel,
        out_shape=(
            jax.ShapeDtypeStruct((3, R, units), F32),
            jax.ShapeDtypeStruct((R, half), F32),
        ),
        in_specs=[
            pl.BlockSpec(memory_space=pltpu.SMEM),
            pl.BlockSpec(memory_space=pltpu.VMEM),
            *[anywhere] * 10,
        ],
        scratch_shapes=[
            pltpu.VMEM((3, count, count), F32),
            pltpu.VMEM((4 * height, half), BF),
            pltpu.VMEM((3, count, units), BF),
            pltpu.SemaphoreType.DMA((10,)),
        ],
        compiler_params=pltpu.CompilerParams(vmem_limit_bytes=32 << 20),
        name="finish",
    )(dp_index.reshape(1), sums, *squares, *rows16, *grads)


def side_by_side(pieces):
    micro, copies, tokens, columns = pieces.shape

    def kernel(pieces_ref, out_ref):
        for c in range(copies):
            out_ref[0, :, c * columns : (c + 1) * columns] = pieces_ref[0, c]

    return pl.pallas_call(
        kernel,
        grid=(micro,),
        out_shape=jax.ShapeDtypeStruct((micro, tokens, copies * columns), pieces.dtype),
        in_specs=[pl.BlockSpec((1, copies, tokens, columns), lambda m: (m, 0, 0, 0))],
        out_specs=pl.BlockSpec((1, tokens, copies * columns), lambda m: (m, 0, 0)),
        name="side_by_side",
    )(pieces)


def shards(saved_inputs, top_grad, routes, mix_weights, w_gate, w_up, w_down, q_prev):
    sections = lax.axis_size("pipe")
    last = lax.axis_index("pipe") == sections - 1
    peers = lax.axis_size("expert")
    expert_index = lax.axis_index("expert")
    replicas = lax.axis_size("dp")
    dp_index = lax.axis_index("dp")
    gate, up, down = (w_gate[0, 0, 0], w_up[0, 0, 0], w_down[0, 0, 0])
    right = q_prev[0, 0, 0].astype(BF)
    copies = peers // EXPERTS
    tokens = saved_inputs.shape[2]
    rows = MICRO * tokens
    slots = MICRO * CAP
    columns = D // copies
    major, minor = (expert_index // copies, expert_index % copies)

    own_inputs = saved_inputs[0].reshape(rows, D)
    top_rows = top_grad.reshape(rows, D)
    rank = slots_of(routes[0])
    mix = mix_weights[0].reshape(rows, 2)
    micro_start = (jnp.arange(MICRO, dtype=jnp.int32) * CAP)[:, None, None]
    own_ids = jnp.where(routes[0] == major, micro_start + rank, -1).reshape(rows, 2)
    first, second = hit_table(own_ids, slots)
    own_pick = (first | second).astype(BF)
    weight = jnp.sum(
        jnp.where(first, mix[None, :, 0], 0.0) + jnp.where(second, mix[None, :, 1], 0.0),
        axis=1,
        keepdims=True,
    )
    part_ids = lax.dynamic_index_in_dim(routes[0] * CAP + rank, major, 0, keepdims=False)
    first, second = hit_table(part_ids, EXPERTS * CAP)
    part_pick = (first | second).astype(BF)

    own_slots = times(own_pick, own_inputs).astype(BF)
    inputs_both = (own_slots, swap_cores(own_slots))
    inputs = jnp.concatenate(inputs_both)
    pre_gate = times(inputs, gate)
    pre_up = times(inputs, up)
    sigmoid_gate = jax.nn.sigmoid(pre_gate)
    silu_gate = pre_gate * sigmoid_gate
    hidden = (silu_gate * pre_up).astype(BF)
    slope = pre_up * sigmoid_gate * (1.0 + pre_gate * (1.0 - sigmoid_gate))

    def phase(own_rows, base):
        own_grads = (weight * own_rows).astype(BF)
        grads_both = (own_grads, swap_cores(own_grads))
        grad_rows = jnp.concatenate(grads_both)
        grad_hidden = times(grad_rows, down, 1, 1)
        grad_gate = (grad_hidden * slope).astype(BF)
        grad_up = (grad_hidden * silu_gate).astype(BF)
        partial = times(grad_gate, gate, 1, 1) + times(grad_up, up, 1, 1)
        other = swap_cores(partial[slots:].astype(BF))
        mine = partial[:slots] + other.astype(F32)
        mine = mine.astype(BF).reshape(MICRO, CAP, copies, columns).transpose(0, 2, 1, 3)
        pieces = exchange(mine.reshape(peers, CAP, columns))
        summed = jnp.sum(pieces.astype(F32).reshape(EXPERTS, copies, CAP, columns), axis=1)
        share = times(
            part_pick.astype(F32),
            summed.reshape(EXPERTS * CAP, columns),
            0,
            0,
            lax.Precision.HIGHEST,
        )
        part = (base.astype(F32) + share).astype(BF)
        return part, grads_both, grad_gate, grad_up

    top_part = lax.dynamic_slice(
        top_grad, (major, 0, minor * columns), (1, tokens, columns)
    ).reshape(tokens, columns)
    part, _, _, _ = phase(times(own_pick, top_rows), top_part)
    incoming = lax.ppermute(part, "pipe", [(i, i - 1) for i in range(1, sections)])
    base = jnp.where(last, top_part, incoming)
    listed = times(part_pick, base).astype(BF).reshape(EXPERTS, 1, CAP, columns)
    pieces = jnp.broadcast_to(listed, (EXPERTS, copies, CAP, columns))
    own_rows = exchange(pieces.reshape(peers, CAP, columns))
    own_rows = own_rows.reshape(MICRO, copies, CAP, columns).transpose(0, 2, 1, 3)
    part, grads_both, grad_gate, grad_up = phase(own_rows.reshape(slots, D).astype(F32), base)
    produced = exchange(jnp.broadcast_to(part, (peers, tokens, columns)))
    produced = side_by_side(produced.reshape(MICRO, copies, tokens, columns))

    sums = jnp.concatenate(
        [times(grad_gate, right[0]) + times(grad_up, right[1]), times(hidden, right[2])], axis=1
    )
    rounded = sums.astype(BF)
    other = swap_cores(rounded)
    sums = rounded.astype(F32) + jnp.concatenate([other[slots:], other[:slots]]).astype(F32)
    sums = add_copies(sums, copies)
    grad_rows = jnp.concatenate(grads_both)
    squares = (
        times(inputs, inputs, 1, 1),
        times(grad_rows, inputs, 1, 1),
        times(grad_rows, grad_rows, 1, 1),
    )
    q_next, basis = finish(
        dp_index,
        sums,
        squares,
        (*inputs_both, *grads_both),
        (grad_gate, grad_up, hidden),
        replicas * rows,
    )
    return (
        produced.reshape(1, MICRO, tokens, D),
        basis.T[None, None, None],
        q_next.transpose(0, 2, 1)[None, None, None],
    )


def solution(mesh):
    placed = (
        P("pipe", None, "dp", None),
        P(None, "dp", None),
        P("pipe", None, "dp", None),
        P("pipe", None, "dp", None),
        P("pipe", "expert", None, None, "dp"),
        P("pipe", "expert", None, None, "dp"),
        P("pipe", "expert", None, "dp", None),
        P("pipe", "expert", None, None, "dp", None),
    )
    return jax.shard_map(
        shards,
        mesh=mesh,
        in_specs=placed,
        out_specs=(
            P("pipe", None, "dp", None),
            P("pipe", "expert", None, "dp", None),
            P("pipe", "expert", None, None, "dp", None),
        ),
        check_vma=False,
    )
```

```python
import math

import jax
import jax.numpy as jnp
from jax import lax
from jax.experimental import pallas as pl
from jax.experimental.pallas import tpu as pltpu
from jax.sharding import PartitionSpec as P

D = 3072
EXPERTS = 4
R = 64
MICRO = 4
CAP = 48

BF = jnp.bfloat16
F32 = jnp.float32


def swap_cores(value):
    return lax.ppermute(value, "dp", [(0, 1), (1, 0)])


def exchange(pieces):
    return lax.all_to_all(pieces, "expert", 0, 0, tiled=True)


def times(a, b, ca=1, cb=0, precision=None):
    return lax.dot_general(
        a, b, (((ca,), (cb,)), ((), ())), preferred_element_type=F32, precision=precision
    )


def slots_of(route_rows):
    flat = route_rows.reshape(MICRO, -1)
    count = flat.shape[1]
    earlier = lax.broadcasted_iota(jnp.int32, (count, count), 1) < lax.broadcasted_iota(
        jnp.int32, (count, count), 0
    )
    same = (flat[:, :, None] == flat[:, None, :]) & earlier[None]
    return jnp.sum(same.astype(jnp.int32), axis=2).reshape(route_rows.shape)


def hit_table(ids, count):
    rows = lax.broadcasted_iota(jnp.int32, (count, ids.shape[0]), 0)
    return rows == ids[None, :, 0], rows == ids[None, :, 1]


def add_copies(values, copies):
    def x_pair(i):
        return i ^ 1

    def y_pair(i):
        return i ^ 2

    def y_cross(i):
        y = i // 2 % 4
        return i + (((3 - y) % 4) - y) * 2

    for partner in (x_pair, y_pair, y_cross):
        route = [(i, partner(i)) for i in range(copies * EXPERTS)]
        rounded = values.astype(BF)
        other = lax.ppermute(rounded, "expert", route)
        values = rounded.astype(F32) + other.astype(F32)
    return values


def inverse_lower(gram):
    height = 8
    lanes = lax.broadcasted_iota(jnp.int32, (height, 2 * R), 1)
    depth = lax.broadcasted_iota(jnp.int32, (height, 2 * R), 0)
    blocks = []
    for b in range(R // height):
        rows = gram[b * height : (b + 1) * height, :]
        held = jnp.concatenate([jnp.zeros((height, R), F32), rows], 1)
        blocks.append(jnp.where(lanes == depth + b * height, 1.0, held))
    for k in range(R):
        at, row = divmod(k, height)
        pivot_row = blocks[at][row : row + 1, :]
        pivot_row = pivot_row * (1.0 / pivot_row[:, R + k : R + k + 1])
        for b in range((k + 1) // height, R // height):
            below = blocks[b] - blocks[b][:, R + k : R + k + 1] * pivot_row
            blocks[b] = jnp.where(depth + b * height > k, below, blocks[b]) if b == at else below
    for b in range(R // height):
        diagonal = jnp.where(lanes == depth + R + b * height, blocks[b], 0.0)
        pivots = jnp.sum(diagonal, axis=1, keepdims=True)
        blocks[b] = (blocks[b] * lax.rsqrt(pivots))[:, :R]
    return jnp.concatenate(blocks, axis=0)


def halves(value):
    high = value.astype(BF)
    return high, (value - high.astype(F32)).astype(BF)


def finish(dp_index, sums, squares, rows16, grads, token_total):
    wide = rows16[0].shape[1]
    half = wide // 2
    count = sums.shape[0]
    units = grads[0].shape[1]
    height = rows16[0].shape[0]

    def kernel(dp_ref, sums_ref, *refs):
        squares_hbm, rows_hbm, grads_hbm = (refs[:3], refs[3:7], refs[7:10])
        q_ref, basis_ref = refs[10:12]
        squares_ref, rows_ref, grads_ref, done = refs[12:]
        moves = [
            pltpu.make_async_copy(squares_hbm[i], squares_ref.at[i], done.at[i]) for i in range(3)
        ]
        moves += [
            pltpu.make_async_copy(grads_hbm[i], grads_ref.at[i], done.at[3 + i]) for i in range(3)
        ]
        start = pl.multiple_of(dp_ref[0] * half, half)
        moves += [
            pltpu.make_async_copy(
                rows_hbm[i].at[:, pl.ds(start, half)],
                rows_ref.at[pl.ds(i * height, height)],
                done.at[6 + i],
            )
            for i in range(4)
        ]
        for move in moves:
            move.start()
        turned = sums_ref[...].T
        of_inputs, of_grads = (turned[:R].astype(BF), turned[R:].astype(BF))
        for move in moves[:3]:
            move.wait()

        def twice(left, right, cb):
            high, low = halves(right)
            return times(left, high, 1, cb) + times(left, low, 1, cb)

        inputs_inputs, grads_inputs, grads_grads = (squares_ref[i] for i in range(3))
        along_inputs = twice(of_inputs, inputs_inputs, 0) + twice(of_grads, grads_inputs, 0)
        along_grads = twice(of_inputs, grads_inputs, 1) + twice(of_grads, grads_grads, 0)
        gram = twice(of_inputs, along_inputs, 1) + twice(of_grads, along_grads, 1)
        inverse = inverse_lower(0.5 * (gram + gram.T))
        exact = lax.Precision.HIGHEST
        weights = jnp.concatenate(
            [
                times(inverse, of_inputs.astype(F32), 1, 0, exact),
                times(inverse, of_grads.astype(F32), 1, 0, exact),
            ],
            axis=1,
        ).astype(BF)
        scale = 1.0 / math.sqrt(float(token_total))
        along_inputs = times(inverse, along_inputs, 1, 0, exact).astype(BF)
        along_grads = times(inverse, along_grads, 1, 0, exact).astype(BF)
        for move in moves[3:]:
            move.wait()
        q_ref[0] = times(along_inputs, grads_ref[0]) * scale
        q_ref[1] = times(along_inputs, grads_ref[1]) * scale
        q_ref[2] = times(along_grads, grads_ref[2]) * scale
        basis_ref[...] = times(weights, rows_ref[...]) * math.sqrt(float(wide))

    anywhere = pl.BlockSpec(memory_space=pl.ANY)
    return pl.pallas_call(
        kernel,
        out_shape=(
            jax.ShapeDtypeStruct((3, R, units), F32),
            jax.ShapeDtypeStruct((R, half), F32),
        ),
        in_specs=[
            pl.BlockSpec(memory_space=pltpu.SMEM),
            pl.BlockSpec(memory_space=pltpu.VMEM),
            *[anywhere] * 10,
        ],
        scratch_shapes=[
            pltpu.VMEM((3, count, count), F32),
            pltpu.VMEM((4 * height, half), BF),
            pltpu.VMEM((3, count, units), BF),
            pltpu.SemaphoreType.DMA((10,)),
        ],
        compiler_params=pltpu.CompilerParams(vmem_limit_bytes=20 << 20),
        name="finish",
    )(dp_index.reshape(1), sums, *squares, *rows16, *grads)


ANYWHERE = pl.BlockSpec(memory_space=pl.ANY)
IN_SMEM = pl.BlockSpec(memory_space=pltpu.SMEM)


def pick_slots(own_expert, routes, mix, inputs, grads):
    micro, _, tokens = routes.shape
    width = inputs.shape[1]
    block = width // 4

    def kernel(expert_ref, routes_ref, mix_ref, inputs_ref, grads_ref, picked_ref, scaled_ref, w_ref):
        expert = expert_ref[0]
        filler = jnp.zeros((8 - micro, tokens), F32)
        first = routes_ref[:, 0, :] == expert
        second = routes_ref[:, 1, :] == expert
        hit = jnp.where(first | second, 1.0, 0.0)
        weight = jnp.where(first, mix_ref[:, 0, :], 0.0) + jnp.where(second, mix_ref[:, 1, :], 0.0)
        earlier = lax.broadcasted_iota(jnp.int32, (tokens, tokens), 0) < lax.broadcasted_iota(
            jnp.int32, (tokens, tokens), 1
        )
        counted = jnp.concatenate([hit, filler]).astype(BF)
        rank = times(counted, jnp.where(earlier, 1.0, 0.0).astype(BF))[:micro]
        place = jnp.where(hit > 0.0, rank, -1.0)
        slot = lax.broadcasted_iota(jnp.int32, (CAP, tokens), 0).astype(F32)
        for m in range(micro):
            chosen = slot == place[m : m + 1]
            pick = jnp.where(chosen, 1.0, 0.0).astype(BF)
            by_slot = jnp.sum(jnp.where(chosen, weight[m : m + 1], 0.0), axis=1, keepdims=True)
            source = pl.ds(m * tokens, tokens)
            target = pl.ds(m * CAP, CAP)
            picked_ref[target, :] = times(pick, inputs_ref[source, :]).astype(BF)
            scaled_ref[target, :] = (by_slot * times(pick, grads_ref[source, :])).astype(BF)
            w_ref[target, :] = jnp.broadcast_to(by_slot, (CAP, 128))

    def whole(shape):
        return pl.BlockSpec(shape, lambda d: (0,) * len(shape))

    return pl.pallas_call(
        kernel,
        grid=(width // block,),
        out_shape=(
            jax.ShapeDtypeStruct((micro * CAP, width), BF),
            jax.ShapeDtypeStruct((micro * CAP, width), BF),
            jax.ShapeDtypeStruct((micro * CAP, 128), F32),
        ),
        in_specs=[
            IN_SMEM,
            whole(routes.shape),
            whole(mix.shape),
            pl.BlockSpec((micro * tokens, block), lambda d: (0, d)),
            pl.BlockSpec((micro * tokens, block), lambda d: (0, d)),
        ],
        out_specs=(
            pl.BlockSpec((micro * CAP, block), lambda d: (0, d)),
            pl.BlockSpec((micro * CAP, block), lambda d: (0, d)),
            whole((micro * CAP, 128)),
        ),
        name="pick_slots",
    )(own_expert.reshape(1), routes, mix, inputs, grads)


def experts(gate, up, down, grads_both, copies, inputs_both=None, forward=None, right=None):
    fresh = forward is None
    slots, width = grads_both[0].shape
    count = 2 * slots
    units = gate.shape[1]
    columns = width // copies
    cuts = 3
    part = width // cuts
    operands = [*grads_both, down, gate, up] + ([*inputs_both] if fresh else [*forward, right])
    halves_shape = (MICRO, copies, CAP, columns)
    square = (count, units)
    if fresh:
        results = [(square, F32), (square, F32), (square, BF)]
    else:
        results = [(square, BF), (square, BF), ((count, 2 * R), BF)]
    results += [(halves_shape, F32), (halves_shape, BF)]

    def kernel(*refs):
        ins, outs = (refs[: len(operands)], refs[len(operands) : len(operands) + len(results)])
        rest = list(refs[len(operands) + len(results) :])
        grads_v, down_v, gate_v, up_v, gg_v, gu_v, own_v, par_v = rest[:8]
        in_done, out_done = rest[8:10]
        more = rest[10:]
        moves = {}
        used = [0]

        def load(key, source, target):
            moves[key] = pltpu.make_async_copy(source, target, in_done.at[used[0]])
            moves[key].start()
            used[0] += 1

        def load_rows(name, pair, target, d):
            for i in range(2):
                load(
                    (name, i, d),
                    pair[i].at[:, pl.ds(d * part, part)],
                    target.at[d, pl.ds(i * slots, slots)],
                )

        def load_grads(d):
            load_rows("grads", ins[:2], grads_v, d)
            load(("down", 0, d), ins[2].at[:, pl.ds(d * part, part)], down_v.at[d])

        def load_weight(name, source, target, d):
            load((name, 0, d), source.at[pl.ds(d * part, part)], target.at[pl.ds(d * part, part)])

        if fresh:
            rows_v, slope_v, silu_v, hidden_v = more
            for d in range(cuts):
                load_rows("rows", ins[5:7], rows_v, d)
                load_weight("gate", ins[3], gate_v, d)
                load_weight("up", ins[4], up_v, d)
            for d in range(cuts):
                load_grads(d)
        else:
            slope_v, silu_v, hidden_v, right_v, sums_v = more
            for d in range(cuts):
                load_grads(d)
            for i, target in enumerate((slope_v, silu_v, hidden_v, right_v)):
                load(("forward", i, 0), ins[5 + i], target)
            for d in range(cuts):
                load_weight("gate", ins[3], gate_v, d)
                load_weight("up", ins[4], up_v, d)

        def arrive(*keys):
            for key in keys:
                moves[key].wait()

        stores = []

        def store(source, target):
            move = pltpu.make_async_copy(source, target, out_done.at[len(stores)])
            move.start()
            stores.append(move)

        if fresh:
            for d in range(cuts):
                arrive(("rows", 0, d), ("rows", 1, d), ("gate", 0, d))
                held = pl.ds(d * part, part)
                term = times(rows_v[d], gate_v[held, :])
                slope_v[...] = term if d == 0 else slope_v[...] + term
                arrive(("up", 0, d))
                term = times(rows_v[d], up_v[held, :])
                silu_v[...] = term if d == 0 else silu_v[...] + term
            pre_gate, pre_up = (slope_v[...], silu_v[...])
            sigmoid = 1.0 / (1.0 + jnp.exp(-pre_gate))
            silu = pre_gate * sigmoid
            hidden_v[...] = (silu * pre_up).astype(BF)
            slope_v[...] = pre_up * sigmoid * (1.0 + pre_gate * (1.0 - sigmoid))
            silu_v[...] = silu
            store(slope_v, outs[0])
            store(silu_v, outs[1])
            store(hidden_v, outs[2])
        grad_hidden = None
        for d in range(cuts):
            arrive(("grads", 0, d), ("grads", 1, d), ("down", 0, d))
            term = times(grads_v[d], down_v[d], 1, 1)
            grad_hidden = term if d == 0 else grad_hidden + term
        if not fresh:
            arrive(*[("forward", i, 0) for i in range(4)])
        gg_v[...] = (grad_hidden * slope_v[...]).astype(BF)
        gu_v[...] = (grad_hidden * silu_v[...]).astype(BF)
        if not fresh:
            store(gg_v, outs[0])
            store(gu_v, outs[1])
            right16 = right_v[...].astype(BF)
            of_inputs = times(gg_v[...], right16[0], 1, 1) + times(gu_v[...], right16[1], 1, 1)
            of_grads = times(hidden_v[...], right16[2], 1, 1)
            sums_v[...] = jnp.concatenate([of_inputs, of_grads], axis=1).astype(BF)
            store(sums_v, outs[2])
            for d in range(cuts):
                arrive(("gate", 0, d), ("up", 0, d))

        def column(c, carry):
            held = pl.ds(pl.multiple_of(c * columns, columns), columns)
            total = times(gg_v[...], gate_v[held, :], 1, 1) + times(gu_v[...], up_v[held, :], 1, 1)
            for m in range(MICRO):
                own_v[m, c] = total[m * CAP : (m + 1) * CAP]
                par_v[m, c] = total[slots + m * CAP : slots + (m + 1) * CAP].astype(BF)
            return carry

        lax.fori_loop(0, copies, column, 0)
        store(own_v, outs[3])
        store(par_v, outs[4])
        for move in stores:
            move.wait()

    scratch = [
        pltpu.VMEM((cuts, count, part), BF),
        pltpu.VMEM((cuts, units, part), BF),
        pltpu.VMEM((width, units), BF),
        pltpu.VMEM((width, units), BF),
        pltpu.VMEM(square, BF),
        pltpu.VMEM(square, BF),
        pltpu.VMEM(halves_shape, F32),
        pltpu.VMEM(halves_shape, BF),
        pltpu.SemaphoreType.DMA((10 * cuts,)),
        pltpu.SemaphoreType.DMA((5,)),
    ]
    if fresh:
        scratch += [pltpu.VMEM((cuts, count, part), BF)]
    scratch += [pltpu.VMEM(square, F32), pltpu.VMEM(square, F32), pltpu.VMEM(square, BF)]
    if not fresh:
        scratch += [pltpu.VMEM(right.shape, F32), pltpu.VMEM((count, 2 * R), BF)]
    return pl.pallas_call(
        kernel,
        out_shape=tuple(jax.ShapeDtypeStruct(*result) for result in results),
        in_specs=[ANYWHERE] * len(operands),
        out_specs=(ANYWHERE,) * len(results),
        scratch_shapes=scratch,
        compiler_params=pltpu.CompilerParams(vmem_limit_bytes=44 << 20),
        name="experts_first" if fresh else "experts_last",
    )(*operands)


def side_by_side(pieces):
    micro, copies, tokens, columns = pieces.shape

    def kernel(pieces_ref, out_ref):
        for c in range(copies):
            out_ref[0, :, c * columns : (c + 1) * columns] = pieces_ref[0, c]

    return pl.pallas_call(
        kernel,
        grid=(micro, 2),
        out_shape=jax.ShapeDtypeStruct((micro, tokens, copies * columns), pieces.dtype),
        in_specs=[pl.BlockSpec((1, copies, tokens // 2, columns), lambda m, h: (m, 0, h, 0))],
        out_specs=pl.BlockSpec((1, tokens // 2, copies * columns), lambda m, h: (m, h, 0)),
        name="side_by_side",
    )(pieces)


def shards(saved_inputs, top_grad, routes, mix_weights, w_gate, w_up, w_down, q_prev):
    sections = lax.axis_size("pipe")
    last = lax.axis_index("pipe") == sections - 1
    peers = lax.axis_size("expert")
    expert_index = lax.axis_index("expert")
    replicas = lax.axis_size("dp")
    dp_index = lax.axis_index("dp")
    gate, up, down = (w_gate[0, 0, 0], w_up[0, 0, 0], w_down[0, 0, 0])
    right = q_prev[0, 0, 0].transpose(0, 2, 1)
    copies = peers // EXPERTS
    tokens = saved_inputs.shape[2]
    rows = MICRO * tokens
    slots = MICRO * CAP
    columns = D // copies
    major, minor = (expert_index // copies, expert_index % copies)

    own_inputs = saved_inputs[0].reshape(rows, D)
    top_rows = top_grad.reshape(rows, D)
    rank = slots_of(routes[0])
    part_ids = lax.dynamic_index_in_dim(routes[0] * CAP + rank, major, 0, keepdims=False)
    first, second = hit_table(part_ids, EXPERTS * CAP)
    part_pick = (first | second).astype(BF)

    own_slots, own_grads, slot_weights = pick_slots(
        major,
        routes[0].transpose(0, 2, 1),
        mix_weights[0].transpose(0, 2, 1),
        own_inputs,
        top_rows,
    )
    inputs_both = (own_slots, swap_cores(own_slots))
    *forward, own_half, other_half = experts(
        gate, up, down, (own_grads, swap_cores(own_grads)), copies, inputs_both=inputs_both
    )

    def reduced(own_half, other_half, base):
        other = swap_cores(other_half)
        mine = (own_half + other.astype(F32)).astype(BF)
        pieces = exchange(mine.reshape(peers, CAP, columns))
        summed = jnp.sum(pieces.astype(F32).reshape(EXPERTS, copies, CAP, columns), axis=1)
        share = times(
            part_pick.astype(F32),
            summed.reshape(EXPERTS * CAP, columns),
            0,
            0,
            lax.Precision.HIGHEST,
        )
        part = (base.astype(F32) + share).astype(BF)
        return part

    top_part = lax.dynamic_slice(
        top_grad, (major, 0, minor * columns), (1, tokens, columns)
    ).reshape(tokens, columns)
    part = reduced(own_half, other_half, top_part)
    incoming = lax.ppermute(part, "pipe", [(i, i - 1) for i in range(1, sections)])
    base = jnp.where(last, top_part, incoming)
    listed = times(part_pick, base).astype(BF).reshape(EXPERTS, 1, CAP, columns)
    pieces = jnp.broadcast_to(listed, (EXPERTS, copies, CAP, columns))
    own_rows = exchange(pieces.reshape(peers, CAP, columns))
    own_rows = own_rows.reshape(MICRO, copies, CAP, columns).transpose(0, 2, 1, 3)
    own_grads = (slot_weights[:, :1] * own_rows.reshape(slots, D).astype(F32)).astype(BF)
    grads_both = (own_grads, swap_cores(own_grads))
    grad_gate, grad_up, sums, own_half, other_half = experts(
        gate, up, down, grads_both, copies, forward=forward, right=right
    )
    part = reduced(own_half, other_half, base)
    produced = exchange(jnp.broadcast_to(part, (peers, tokens, columns)))
    produced = side_by_side(produced.reshape(MICRO, copies, tokens, columns))

    other = swap_cores(sums)
    sums = sums.astype(F32) + jnp.concatenate([other[slots:], other[:slots]]).astype(F32)
    sums = add_copies(sums, copies)
    inputs = jnp.concatenate(inputs_both)
    grad_rows = jnp.concatenate(grads_both)
    squares = (
        times(inputs, inputs, 1, 1),
        times(grad_rows, inputs, 1, 1),
        times(grad_rows, grad_rows, 1, 1),
    )
    q_next, basis = finish(
        dp_index,
        sums,
        squares,
        (*inputs_both, *grads_both),
        (grad_gate, grad_up, forward[2]),
        replicas * rows,
    )
    return (
        produced.reshape(1, MICRO, tokens, D),
        basis.T[None, None, None],
        q_next.transpose(0, 2, 1)[None, None, None],
    )


def solution(mesh):
    placed = (
        P("pipe", None, "dp", None),
        P(None, "dp", None),
        P("pipe", None, "dp", None),
        P("pipe", None, "dp", None),
        P("pipe", "expert", None, None, "dp"),
        P("pipe", "expert", None, None, "dp"),
        P("pipe", "expert", None, "dp", None),
        P("pipe", "expert", None, None, "dp", None),
    )
    return jax.shard_map(
        shards,
        mesh=mesh,
        in_specs=placed,
        out_specs=(
            P("pipe", None, "dp", None),
            P("pipe", "expert", None, "dp", None),
            P("pipe", "expert", None, None, "dp", None),
        ),
        check_vma=False,
    )
```

```python
import math

import jax
import jax.numpy as jnp
from jax import lax
from jax.experimental import pallas as pl
from jax.experimental.pallas import tpu as pltpu
from jax.sharding import PartitionSpec as P

D = 3072
EXPERTS = 4
R = 64
MICRO = 4
CAP = 48

BF = jnp.bfloat16
F32 = jnp.float32
IN_SMEM = pl.BlockSpec(memory_space=pltpu.SMEM)


def swap_cores(value):
    return lax.ppermute(value, "dp", [(0, 1), (1, 0)])


def exchange(pieces):
    return lax.all_to_all(pieces, "expert", 0, 0, tiled=True)


def times(a, b, ca=1, cb=0, precision=None):
    return lax.dot_general(
        a, b, (((ca,), (cb,)), ((), ())), preferred_element_type=F32, precision=precision
    )


def slots_of(route_rows):
    flat = route_rows.reshape(MICRO, -1)
    count = flat.shape[1]
    earlier = lax.broadcasted_iota(jnp.int32, (count, count), 1) < lax.broadcasted_iota(
        jnp.int32, (count, count), 0
    )
    same = (flat[:, :, None] == flat[:, None, :]) & earlier[None]
    return jnp.sum(same.astype(jnp.int32), axis=2).reshape(route_rows.shape)


def hit_table(ids, count):
    rows = lax.broadcasted_iota(jnp.int32, (count, ids.shape[0]), 0)
    return rows == ids[None, :, 0], rows == ids[None, :, 1]


def add_copies(values, copies):
    def x_pair(i):
        return i ^ 1

    def y_pair(i):
        return i ^ 2

    def y_cross(i):
        y = i // 2 % 4
        return i + (((3 - y) % 4) - y) * 2

    for partner in (x_pair, y_pair, y_cross):
        route = [(i, partner(i)) for i in range(copies * EXPERTS)]
        rounded = values.astype(BF)
        other = lax.ppermute(rounded, "expert", route)
        values = rounded.astype(F32) + other.astype(F32)
    return values


def inverse_lower(gram):
    height = 8
    lanes = lax.broadcasted_iota(jnp.int32, (height, 2 * R), 1)
    depth = lax.broadcasted_iota(jnp.int32, (height, 2 * R), 0)
    blocks = []
    for b in range(R // height):
        rows = gram[b * height : (b + 1) * height, :]
        held = jnp.concatenate([jnp.zeros((height, R), F32), rows], 1)
        blocks.append(jnp.where(lanes == depth + b * height, 1.0, held))
    for k in range(R):
        at, row = divmod(k, height)
        pivot_row = blocks[at][row : row + 1, :]
        pivot_row = pivot_row * (1.0 / pivot_row[:, R + k : R + k + 1])
        for b in range((k + 1) // height, R // height):
            below = blocks[b] - blocks[b][:, R + k : R + k + 1] * pivot_row
            blocks[b] = jnp.where(depth + b * height > k, below, blocks[b]) if b == at else below
    for b in range(R // height):
        diagonal = jnp.where(lanes == depth + R + b * height, blocks[b], 0.0)
        pivots = jnp.sum(diagonal, axis=1, keepdims=True)
        blocks[b] = (blocks[b] * lax.rsqrt(pivots))[:, :R]
    return jnp.concatenate(blocks, axis=0)


def halves(value):
    high = value.astype(BF)
    return high, (value - high.astype(F32)).astype(BF)


def finish(dp_index, sums, squares, rows16, grads, token_total):
    wide = rows16[0].shape[1]
    half = wide // 2
    units = grads[0].shape[1]

    def kernel(dp_ref, sums_ref, *refs):
        squares_ref, rows_ref, grads_ref = (refs[:3], refs[3:7], refs[7:10])
        q_ref, basis_ref = refs[10:12]
        start = pl.multiple_of(dp_ref[0] * half, half)
        turned = sums_ref[...].T
        of_inputs, of_grads = (turned[:R].astype(BF), turned[R:].astype(BF))

        def twice(left, right, cb):
            high, low = halves(right)
            return times(left, high, 1, cb) + times(left, low, 1, cb)

        inputs_inputs, grads_inputs, grads_grads = (ref[...] for ref in squares_ref)
        along_inputs = twice(of_inputs, inputs_inputs, 0) + twice(of_grads, grads_inputs, 0)
        along_grads = twice(of_inputs, grads_inputs, 1) + twice(of_grads, grads_grads, 0)
        gram = twice(of_inputs, along_inputs, 1) + twice(of_grads, along_grads, 1)
        inverse = inverse_lower(0.5 * (gram + gram.T))
        exact = lax.Precision.HIGHEST
        weights = jnp.concatenate(
            [
                times(inverse, of_inputs.astype(F32), 1, 0, exact),
                times(inverse, of_grads.astype(F32), 1, 0, exact),
            ],
            axis=1,
        ).astype(BF)
        scale = 1.0 / math.sqrt(float(token_total))
        along_inputs = times(inverse, along_inputs, 1, 0, exact).astype(BF)
        along_grads = times(inverse, along_grads, 1, 0, exact).astype(BF)
        q_ref[0] = times(along_inputs, grads_ref[0][...]) * scale
        q_ref[1] = times(along_inputs, grads_ref[1][...]) * scale
        q_ref[2] = times(along_grads, grads_ref[2][...]) * scale
        rows = jnp.concatenate([ref[:, pl.ds(start, half)] for ref in rows_ref])
        basis_ref[...] = times(weights, rows) * math.sqrt(float(wide))

    return pl.pallas_call(
        kernel,
        out_shape=(
            jax.ShapeDtypeStruct((3, R, units), F32),
            jax.ShapeDtypeStruct((R, half), F32),
        ),
        in_specs=[IN_SMEM] + [pl.BlockSpec(memory_space=pltpu.VMEM)] * 11,
        compiler_params=pltpu.CompilerParams(vmem_limit_bytes=20 << 20),
        name="finish",
    )(dp_index.reshape(1), sums, *squares, *rows16, *grads)


def pick_slots(own_expert, routes, mix, inputs, grads):
    micro, _, tokens = routes.shape
    width = inputs.shape[1]
    block = width // 4

    def kernel(expert_ref, routes_ref, mix_ref, inputs_ref, grads_ref, picked_ref, scaled_ref, w_ref):
        expert = expert_ref[0]
        filler = jnp.zeros((8 - micro, tokens), F32)
        first = routes_ref[:, 0, :] == expert
        second = routes_ref[:, 1, :] == expert
        hit = jnp.where(first | second, 1.0, 0.0)
        weight = jnp.where(first, mix_ref[:, 0, :], 0.0) + jnp.where(second, mix_ref[:, 1, :], 0.0)
        earlier = lax.broadcasted_iota(jnp.int32, (tokens, tokens), 0) < lax.broadcasted_iota(
            jnp.int32, (tokens, tokens), 1
        )
        counted = jnp.concatenate([hit, filler]).astype(BF)
        rank = times(counted, jnp.where(earlier, 1.0, 0.0).astype(BF))[:micro]
        base = lax.broadcasted_iota(jnp.int32, (micro, tokens), 0).astype(F32) * CAP
        place = jnp.where(hit > 0.0, rank + base, -1.0)
        place = jnp.concatenate([place[m : m + 1] for m in range(micro)], axis=1)
        weight = jnp.concatenate([weight[m : m + 1] for m in range(micro)], axis=1)
        slot = lax.broadcasted_iota(jnp.int32, (micro * CAP, micro * tokens), 0).astype(F32)
        chosen = slot == place
        pick = jnp.where(chosen, 1.0, 0.0).astype(BF)
        by_slot = jnp.sum(jnp.where(chosen, weight, 0.0), axis=1, keepdims=True)
        picked_ref[...] = times(pick, inputs_ref[...]).astype(BF)
        scaled_ref[...] = (by_slot * times(pick, grads_ref[...])).astype(BF)
        w_ref[...] = jnp.broadcast_to(by_slot, (micro * CAP, 128))

    def whole(shape):
        return pl.BlockSpec(shape, lambda d: (0,) * len(shape))

    return pl.pallas_call(
        kernel,
        grid=(width // block,),
        out_shape=(
            jax.ShapeDtypeStruct((micro * CAP, width), BF),
            jax.ShapeDtypeStruct((micro * CAP, width), BF),
            jax.ShapeDtypeStruct((micro * CAP, 128), F32),
        ),
        in_specs=[
            IN_SMEM,
            whole(routes.shape),
            whole(mix.shape),
            pl.BlockSpec((micro * tokens, block), lambda d: (0, d)),
            pl.BlockSpec((micro * tokens, block), lambda d: (0, d)),
        ],
        out_specs=(
            pl.BlockSpec((micro * CAP, block), lambda d: (0, d)),
            pl.BlockSpec((micro * CAP, block), lambda d: (0, d)),
            whole((micro * CAP, 128)),
        ),
        name="pick_slots",
    )(own_expert.reshape(1), routes, mix, inputs, grads)


def experts(gate, up, down, grads_both, copies, inputs_both=None, forward=None, right=None):
    fresh = forward is None
    slots, width = grads_both[0].shape
    count = 2 * slots
    units = gate.shape[1]
    columns = width // copies
    halves_shape = (MICRO, copies, CAP, columns)
    square = (count, units)
    operands = [*grads_both, down, gate, up] + ([*inputs_both] if fresh else [*forward, right])
    if fresh:
        results = [(square, F32), (square, F32), (square, BF)]
    else:
        results = [(square, BF), (square, BF), ((count, 2 * R), BF)]
    results += [(halves_shape, F32), (halves_shape, BF)]

    def kernel(*refs):
        ins, outs = (refs[: len(operands)], refs[len(operands) : len(operands) + len(results)])
        down_ref, gate_ref, up_ref = ins[2:5]
        own_ref, par_ref = outs[3:]

        def both(pair):
            return jnp.concatenate([pair[0][...], pair[1][...]])

        if fresh:
            gg_ref, gu_ref = refs[len(operands) + len(results) :]
            inputs = both(ins[5:7])
            pre_gate = times(inputs, gate_ref[...])
            pre_up = times(inputs, up_ref[...])
            sigmoid = 1.0 / (1.0 + jnp.exp(-pre_gate))
            silu = pre_gate * sigmoid
            outs[0][...] = pre_up * sigmoid * (1.0 + pre_gate * (1.0 - sigmoid))
            outs[1][...] = silu
            outs[2][...] = (silu * pre_up).astype(BF)
            slope_ref, silu_ref = outs[:2]
        else:
            gg_ref, gu_ref, sums_ref = outs[:3]
            slope_ref, silu_ref, hidden_ref, right_ref = ins[5:9]
        grad_hidden = times(both(ins[:2]), down_ref[...], 1, 1)
        gg_ref[...] = (grad_hidden * slope_ref[...]).astype(BF)
        gu_ref[...] = (grad_hidden * silu_ref[...]).astype(BF)
        if not fresh:
            right16 = right_ref[...].astype(BF)
            of_inputs = times(gg_ref[...], right16[0], 1, 1) + times(gu_ref[...], right16[1], 1, 1)
            of_grads = times(hidden_ref[...], right16[2], 1, 1)
            sums_ref[...] = jnp.concatenate([of_inputs, of_grads], axis=1).astype(BF)

        def column(c, carry):
            held = pl.ds(pl.multiple_of(c * columns, columns), columns)
            total = times(gg_ref[...], gate_ref[held, :], 1, 1)
            total = total + times(gu_ref[...], up_ref[held, :], 1, 1)
            for m in range(MICRO):
                own_ref[m, c] = total[m * CAP : (m + 1) * CAP]
                par_ref[m, c] = total[slots + m * CAP : slots + (m + 1) * CAP].astype(BF)
            return carry

        lax.fori_loop(0, copies, column, 0)

    return pl.pallas_call(
        kernel,
        out_shape=tuple(jax.ShapeDtypeStruct(*result) for result in results),
        scratch_shapes=[pltpu.VMEM(square, BF), pltpu.VMEM(square, BF)] if fresh else [],
        compiler_params=pltpu.CompilerParams(vmem_limit_bytes=32 << 20),
        name="experts_first" if fresh else "experts_last",
    )(*operands)


def side_by_side(pieces):
    micro, copies, tokens, columns = pieces.shape

    def kernel(pieces_ref, out_ref):
        for c in range(copies):
            out_ref[:, :, c * columns : (c + 1) * columns] = pieces_ref[:, c]

    return pl.pallas_call(
        kernel,
        out_shape=jax.ShapeDtypeStruct((micro, tokens, copies * columns), pieces.dtype),
        compiler_params=pltpu.CompilerParams(vmem_limit_bytes=8 << 20),
        name="side_by_side",
    )(pieces)


def shards(saved_inputs, top_grad, routes, mix_weights, w_gate, w_up, w_down, q_prev):
    sections = lax.axis_size("pipe")
    last = lax.axis_index("pipe") == sections - 1
    peers = lax.axis_size("expert")
    expert_index = lax.axis_index("expert")
    replicas = lax.axis_size("dp")
    dp_index = lax.axis_index("dp")
    gate, up, down = (w_gate[0, 0, 0], w_up[0, 0, 0], w_down[0, 0, 0])
    right = q_prev[0, 0, 0].transpose(0, 2, 1)
    copies = peers // EXPERTS
    tokens = saved_inputs.shape[2]
    rows = MICRO * tokens
    slots = MICRO * CAP
    columns = D // copies
    major, minor = (expert_index // copies, expert_index % copies)

    own_inputs = saved_inputs[0].reshape(rows, D)
    top_rows = top_grad.reshape(rows, D)
    rank = slots_of(routes[0])
    part_ids = lax.dynamic_index_in_dim(routes[0] * CAP + rank, major, 0, keepdims=False)
    first, second = hit_table(part_ids, EXPERTS * CAP)
    part_pick = (first | second).astype(BF)

    own_slots, own_grads, slot_weights = pick_slots(
        major,
        routes[0].transpose(0, 2, 1),
        mix_weights[0].transpose(0, 2, 1),
        own_inputs,
        top_rows,
    )
    inputs_both = (own_slots, swap_cores(own_slots))
    *forward, own_half, other_half = experts(
        gate, up, down, (own_grads, swap_cores(own_grads)), copies, inputs_both=inputs_both
    )

    def reduced(own_half, other_half, base):
        other = swap_cores(other_half)
        mine = (own_half + other.astype(F32)).astype(BF)
        pieces = exchange(mine.reshape(peers, CAP, columns))
        summed = jnp.sum(pieces.astype(F32).reshape(EXPERTS, copies, CAP, columns), axis=1)
        share = times(
            part_pick.astype(F32),
            summed.reshape(EXPERTS * CAP, columns),
            0,
            0,
            lax.Precision.HIGHEST,
        )
        part = (base.astype(F32) + share).astype(BF)
        return part

    top_part = lax.dynamic_slice(
        top_grad, (major, 0, minor * columns), (1, tokens, columns)
    ).reshape(tokens, columns)
    part = reduced(own_half, other_half, top_part)
    incoming = lax.ppermute(part, "pipe", [(i, i - 1) for i in range(1, sections)])
    base = jnp.where(last, top_part, incoming)
    listed = times(part_pick, base).astype(BF).reshape(EXPERTS, 1, CAP, columns)
    pieces = jnp.broadcast_to(listed, (EXPERTS, copies, CAP, columns))
    own_rows = exchange(pieces.reshape(peers, CAP, columns))
    own_rows = own_rows.reshape(MICRO, copies, CAP, columns).transpose(0, 2, 1, 3)
    own_grads = (slot_weights[:, :1] * own_rows.reshape(slots, D).astype(F32)).astype(BF)
    grads_both = (own_grads, swap_cores(own_grads))
    grad_gate, grad_up, sums, own_half, other_half = experts(
        gate, up, down, grads_both, copies, forward=forward, right=right
    )
    part = reduced(own_half, other_half, base)
    produced = exchange(jnp.broadcast_to(part, (peers, tokens, columns)))
    produced = side_by_side(produced.reshape(MICRO, copies, tokens, columns))

    other = swap_cores(sums)
    sums = sums.astype(F32) + jnp.concatenate([other[slots:], other[:slots]]).astype(F32)
    sums = add_copies(sums, copies)
    inputs = jnp.concatenate(inputs_both)
    grad_rows = jnp.concatenate(grads_both)
    squares = (
        times(inputs, inputs, 1, 1),
        times(grad_rows, inputs, 1, 1),
        times(grad_rows, grad_rows, 1, 1),
    )
    q_next, basis = finish(
        dp_index,
        sums,
        squares,
        (*inputs_both, *grads_both),
        (grad_gate, grad_up, forward[2]),
        replicas * rows,
    )
    return (
        produced.reshape(1, MICRO, tokens, D),
        basis.T[None, None, None],
        q_next.transpose(0, 2, 1)[None, None, None],
    )


def solution(mesh):
    placed = (
        P("pipe", None, "dp", None),
        P(None, "dp", None),
        P("pipe", None, "dp", None),
        P("pipe", None, "dp", None),
        P("pipe", "expert", None, None, "dp"),
        P("pipe", "expert", None, None, "dp"),
        P("pipe", "expert", None, "dp", None),
        P("pipe", "expert", None, None, "dp", None),
    )
    return jax.shard_map(
        shards,
        mesh=mesh,
        in_specs=placed,
        out_specs=(
            P("pipe", None, "dp", None),
            P("pipe", "expert", None, "dp", None),
            P("pipe", "expert", None, None, "dp", None),
        ),
        check_vma=False,
    )
```

```python
import math

import jax
import jax.numpy as jnp
from jax import lax
from jax.experimental import pallas as pl
from jax.experimental.pallas import tpu as pltpu
from jax.sharding import PartitionSpec as P

D = 3072
EXPERTS = 4
R = 64
MICRO = 4
CAP = 48

BF = jnp.bfloat16
F32 = jnp.float32
IN_SMEM = pl.BlockSpec(memory_space=pltpu.SMEM)
IN_VMEM = pl.BlockSpec(memory_space=pltpu.VMEM)
IN_HBM = pl.BlockSpec(memory_space=pltpu.HBM)


def cost(flops, moved):
    return pl.CostEstimate(flops=int(flops), bytes_accessed=int(moved), transcendentals=0)


def swap_cores(value):
    return lax.ppermute(value, "dp", [(0, 1), (1, 0)])


def exchange(pieces):
    return lax.all_to_all(pieces, "expert", 0, 0, tiled=True)


def times(a, b, ca=1, cb=0, precision=None):
    return lax.dot_general(
        a, b, (((ca,), (cb,)), ((), ())), preferred_element_type=F32, precision=precision
    )


def slots_of(route_rows):
    flat = route_rows.reshape(MICRO, -1)
    count = flat.shape[1]
    earlier = lax.broadcasted_iota(jnp.int32, (count, count), 1) < lax.broadcasted_iota(
        jnp.int32, (count, count), 0
    )
    same = (flat[:, :, None] == flat[:, None, :]) & earlier[None]
    return jnp.sum(same.astype(jnp.int32), axis=2).reshape(route_rows.shape)


def hit_table(ids, count):
    rows = lax.broadcasted_iota(jnp.int32, (count, ids.shape[0]), 0)
    return rows == ids[None, :, 0], rows == ids[None, :, 1]


def add_copies(values, copies):
    def x_pair(i):
        return i ^ 1

    def y_pair(i):
        return i ^ 2

    def y_cross(i):
        y = i // 2 % 4
        return i + (((3 - y) % 4) - y) * 2

    for partner in (x_pair, y_pair, y_cross):
        route = [(i, partner(i)) for i in range(copies * EXPERTS)]
        rounded = values.astype(BF)
        other = lax.ppermute(rounded, "expert", route)
        values = rounded.astype(F32) + other.astype(F32)
    return values


def inverse_lower(gram):
    height = 8
    lanes = lax.broadcasted_iota(jnp.int32, (height, 2 * R), 1)
    depth = lax.broadcasted_iota(jnp.int32, (height, 2 * R), 0)
    blocks = []
    for b in range(R // height):
        rows = gram[b * height : (b + 1) * height, :]
        held = jnp.concatenate([jnp.zeros((height, R), F32), rows], 1)
        blocks.append(jnp.where(lanes == depth + b * height, 1.0, held))
    for k in range(R):
        at, row = divmod(k, height)
        pivot_row = blocks[at][row : row + 1, :]
        pivot_row = pivot_row * (1.0 / pivot_row[:, R + k : R + k + 1])
        for b in range((k + 1) // height, R // height):
            below = blocks[b] - blocks[b][:, R + k : R + k + 1] * pivot_row
            blocks[b] = jnp.where(depth + b * height > k, below, blocks[b]) if b == at else below
    for b in range(R // height):
        diagonal = jnp.where(lanes == depth + R + b * height, blocks[b], 0.0)
        pivots = jnp.sum(diagonal, axis=1, keepdims=True)
        blocks[b] = (blocks[b] * lax.rsqrt(pivots))[:, :R]
    return jnp.concatenate(blocks, axis=0)


def halves(value):
    high = value.astype(BF)
    return high, (value - high.astype(F32)).astype(BF)


def finish(dp_index, sums, squares, rows16, grads, token_total):
    count, wide = rows16[0].shape
    half = wide // 2
    units = grads.shape[2]

    def kernel(dp_ref, sums_ref, *refs):
        squares_hbm, rows_hbm, grads_hbm = (refs[:3], refs[3:5], refs[5])
        q_ref, basis_ref, squares_ref, rows_ref, grads_ref, done = refs[6:]
        start = pl.multiple_of(dp_ref[0] * half, half)
        moves = [
            pltpu.make_async_copy(squares_hbm[i], squares_ref.at[i], done.at[i]) for i in range(3)
        ]
        moves.append(pltpu.make_async_copy(grads_hbm, grads_ref, done.at[3]))
        moves += [
            pltpu.make_async_copy(
                rows_hbm[i].at[:, pl.ds(start, half)],
                rows_ref.at[pl.ds(i * count, count)],
                done.at[4 + i],
            )
            for i in range(2)
        ]
        for move in moves:
            move.start()
        turned = sums_ref[...].T
        of_inputs, of_grads = (turned[:R].astype(BF), turned[R:].astype(BF))
        for move in moves[:3]:
            move.wait()

        def twice(left, right, cb):
            high, low = halves(right)
            return times(left, high, 1, cb) + times(left, low, 1, cb)

        inputs_inputs, grads_inputs, grads_grads = (squares_ref[i] for i in range(3))
        along_inputs = twice(of_inputs, inputs_inputs, 0) + twice(of_grads, grads_inputs, 0)
        along_grads = twice(of_inputs, grads_inputs, 1) + twice(of_grads, grads_grads, 0)
        gram = twice(of_inputs, along_inputs, 1) + twice(of_grads, along_grads, 1)
        inverse = inverse_lower(0.5 * (gram + gram.T))
        exact = lax.Precision.HIGHEST
        weights = jnp.concatenate(
            [
                times(inverse, of_inputs.astype(F32), 1, 0, exact),
                times(inverse, of_grads.astype(F32), 1, 0, exact),
            ],
            axis=1,
        ).astype(BF)
        scale = 1.0 / math.sqrt(float(token_total))
        along_inputs = times(inverse, along_inputs, 1, 0, exact).astype(BF)
        along_grads = times(inverse, along_grads, 1, 0, exact).astype(BF)
        for move in moves[3:]:
            move.wait()
        q_ref[0] = times(along_inputs, grads_ref[0]) * scale
        q_ref[1] = times(along_inputs, grads_ref[1]) * scale
        q_ref[2] = times(along_grads, grads_ref[2]) * scale
        basis_ref[...] = times(weights, rows_ref[...]) * math.sqrt(float(wide))

    return pl.pallas_call(
        kernel,
        out_shape=(
            jax.ShapeDtypeStruct((3, R, units), F32),
            jax.ShapeDtypeStruct((R, half), F32),
        ),
        in_specs=[IN_SMEM, IN_VMEM] + [IN_HBM] * 6,
        scratch_shapes=[
            pltpu.VMEM((3, count, count), F32),
            pltpu.VMEM((2 * count, half), BF),
            pltpu.VMEM((3, count, units), BF),
            pltpu.SemaphoreType.DMA((6,)),
        ],
        compiler_params=pltpu.CompilerParams(vmem_limit_bytes=61 << 20),
        cost_estimate=cost(4 * R * count * wide, 2 * count * (wide + 3 * units) + 12 * count**2),
        name="finish",
    )(dp_index.reshape(1), sums, *squares, *rows16, grads)


def pick_slots(own_expert, routes, mix, inputs, grads):
    micro, _, tokens = routes.shape
    width = inputs.shape[1]
    block = width // 4
    count = micro * CAP

    def kernel(expert_ref, routes_ref, mix_ref, inputs_ref, grads_ref, picked_ref, scaled_ref, w_ref):
        expert = expert_ref[0]
        filler = jnp.zeros((8 - micro, tokens), F32)
        first = routes_ref[:, 0, :] == expert
        second = routes_ref[:, 1, :] == expert
        hit = jnp.where(first | second, 1.0, 0.0)
        weight = jnp.where(first, mix_ref[:, 0, :], 0.0) + jnp.where(second, mix_ref[:, 1, :], 0.0)
        earlier = lax.broadcasted_iota(jnp.int32, (tokens, tokens), 0) < lax.broadcasted_iota(
            jnp.int32, (tokens, tokens), 1
        )
        counted = jnp.concatenate([hit, filler]).astype(BF)
        rank = times(counted, jnp.where(earlier, 1.0, 0.0).astype(BF))[:micro]
        base = lax.broadcasted_iota(jnp.int32, (micro, tokens), 0).astype(F32) * CAP
        place = jnp.where(hit > 0.0, rank + base, -1.0)
        place = jnp.concatenate([place[m : m + 1] for m in range(micro)], axis=1)
        weight = jnp.concatenate([weight[m : m + 1] for m in range(micro)], axis=1)
        slot = lax.broadcasted_iota(jnp.int32, (micro * CAP, micro * tokens), 0).astype(F32)
        chosen = slot == place
        pick = jnp.where(chosen, 1.0, 0.0).astype(BF)
        by_slot = jnp.sum(jnp.where(chosen, weight, 0.0), axis=1, keepdims=True)
        w_ref[...] = jnp.broadcast_to(by_slot, (count, 128))
        for at in range(0, width, block):
            held = pl.ds(at, block)
            picked_ref[:, held] = times(pick, inputs_ref[:, held]).astype(BF)
            scaled_ref[:, held] = (by_slot * times(pick, grads_ref[:, held])).astype(BF)

    return pl.pallas_call(
        kernel,
        out_shape=(
            jax.ShapeDtypeStruct((count, width), BF),
            jax.ShapeDtypeStruct((count, width), BF),
            jax.ShapeDtypeStruct((count, 128), F32),
        ),
        in_specs=[IN_SMEM] + [IN_VMEM] * 4,
        compiler_params=pltpu.CompilerParams(vmem_limit_bytes=14 << 20),
        cost_estimate=cost(4 * count * micro * tokens * width, 60 << 20),
        name="pick_slots",
    )(own_expert.reshape(1), routes, mix, inputs, grads)


def scale_rows(pieces, slot_weights):
    micro, copies, cap, columns = pieces.shape

    def kernel(pieces_ref, w_ref, out_ref):
        for m in range(micro):
            held = pl.ds(m * cap, cap)
            weight = w_ref[held, :1]
            for c in range(copies):
                scaled = weight * pieces_ref[m, c].astype(F32)
                out_ref[held, c * columns : (c + 1) * columns] = scaled.astype(BF)

    return pl.pallas_call(
        kernel,
        out_shape=jax.ShapeDtypeStruct((micro * cap, copies * columns), BF),
        compiler_params=pltpu.CompilerParams(vmem_limit_bytes=8 << 20),
        name="scale_rows",
    )(pieces, slot_weights)


def combine(pieces, pick, base, peers):
    experts_count, copies, _, columns = pieces.shape
    tokens = base.shape[0]

    def kernel(pieces_ref, pick_ref, base_ref, out_ref):
        share = base_ref[...].astype(F32)
        for e in range(experts_count):
            total = pieces_ref[e, 0].astype(F32)
            for c in range(1, copies):
                total = total + pieces_ref[e, c].astype(F32)
            for term in halves(total):
                share = share + times(pick_ref[e], term)
        part = share.astype(BF)
        for peer in range(peers):
            out_ref[peer] = part

    return pl.pallas_call(
        kernel,
        out_shape=jax.ShapeDtypeStruct((peers, tokens, columns), BF),
        compiler_params=pltpu.CompilerParams(vmem_limit_bytes=8 << 20),
        name="combine",
    )(pieces, pick, base)


def deal(last, top_part, incoming, pick, copies):
    tokens, columns = incoming.shape
    slots = pick.shape[0]
    cap = slots // EXPERTS

    def kernel(last_ref, top_ref, incoming_ref, pick_ref, base_ref, out_ref):
        base = jnp.where(last_ref[0] == 1, top_ref[...].astype(F32), incoming_ref[...].astype(F32))
        base = base.astype(BF)
        base_ref[...] = base
        listed = times(pick_ref[...], base).astype(BF)
        for e in range(EXPERTS):
            for c in range(copies):
                out_ref[e, c] = listed[e * cap : (e + 1) * cap]

    return pl.pallas_call(
        kernel,
        out_shape=(
            jax.ShapeDtypeStruct((tokens, columns), BF),
            jax.ShapeDtypeStruct((EXPERTS, copies, cap, columns), BF),
        ),
        in_specs=[IN_SMEM] + [IN_VMEM] * 3,
        compiler_params=pltpu.CompilerParams(vmem_limit_bytes=8 << 20),
        cost_estimate=cost(2 * slots * tokens * columns, 60 << 20),
        name="deal",
    )(last.astype(jnp.int32).reshape(1), top_part, incoming, pick)


def experts(gate, up, down, grads_both, copies, inputs_both=None, forward=None, right=None):
    fresh = forward is None
    slots, width = grads_both[0].shape
    count = 2 * slots
    units = gate.shape[1]
    columns = width // copies
    halves_shape = (MICRO, copies, CAP, columns)
    square = (count, units)
    operands = [*grads_both, down, gate, up] + ([*inputs_both] if fresh else [*forward, right])
    made = [(halves_shape, F32), (halves_shape, BF)]
    if fresh:
        made = [(square, F32), (square, F32), (square, BF)] + made
        kept = []
    else:
        made = [((count, 2 * R), BF)] + made
        kept = [((3, *square), BF)]
    kept += [((count, width), BF)]

    def kernel(*refs):
        ins, refs = (refs[: len(operands)], refs[len(operands) :])
        outs, refs = (refs[: len(made)], refs[len(made) :])
        keeps, (gg_ref, gu_ref, done) = (refs[: len(kept)], refs[len(kept) :])
        down_ref, gate_ref, up_ref = ins[2:5]
        own_ref, par_ref = outs[-2:]
        moves = []

        def keep(source, target):
            move = pltpu.make_async_copy(source, target, done.at[len(moves)])
            move.start()
            moves.append(move)

        rows_refs = ins[5:7] if fresh else ins[:2]
        for i in range(2):
            keep(rows_refs[i], keeps[-1].at[pl.ds(i * slots, slots)])

        def both(pair):
            return jnp.concatenate([pair[0][...], pair[1][...]])

        if fresh:
            inputs = both(ins[5:7])
            pre_gate = times(inputs, gate_ref[...])
            pre_up = times(inputs, up_ref[...])
            sigmoid = 1.0 / (1.0 + jnp.exp(-pre_gate))
            silu = pre_gate * sigmoid
            outs[0][...] = pre_up * sigmoid * (1.0 + pre_gate * (1.0 - sigmoid))
            outs[1][...] = silu
            outs[2][...] = (silu * pre_up).astype(BF)
            slope_ref, silu_ref = outs[:2]
        else:
            slope_ref, silu_ref, hidden_ref, right_ref = ins[5:9]
            keep(hidden_ref, keeps[0].at[2])
        grad_hidden = times(both(ins[:2]), down_ref[...], 1, 1)
        gg_ref[...] = (grad_hidden * slope_ref[...]).astype(BF)
        gu_ref[...] = (grad_hidden * silu_ref[...]).astype(BF)
        if not fresh:
            keep(gg_ref, keeps[0].at[0])
            keep(gu_ref, keeps[0].at[1])
            right16 = right_ref[...].astype(BF)
            of_inputs = times(gg_ref[...], right16[0], 1, 1) + times(gu_ref[...], right16[1], 1, 1)
            of_grads = times(hidden_ref[...], right16[2], 1, 1)
            outs[0][...] = jnp.concatenate([of_inputs, of_grads], axis=1).astype(BF)

        def column(c, carry):
            held = pl.ds(pl.multiple_of(c * columns, columns), columns)
            total = times(gg_ref[...], gate_ref[held, :], 1, 1)
            total = total + times(gu_ref[...], up_ref[held, :], 1, 1)
            for m in range(MICRO):
                own_ref[m, c] = total[m * CAP : (m + 1) * CAP]
                par_ref[m, c] = total[slots + m * CAP : slots + (m + 1) * CAP].astype(BF)
            return carry

        lax.fori_loop(0, copies, column, 0)
        for move in moves:
            move.wait()

    return pl.pallas_call(
        kernel,
        out_shape=tuple(jax.ShapeDtypeStruct(*result) for result in made + kept),
        in_specs=[IN_VMEM] * len(operands),
        out_specs=(*[IN_VMEM] * len(made), *[IN_HBM] * len(kept)),
        scratch_shapes=[
            pltpu.VMEM(square, BF),
            pltpu.VMEM(square, BF),
            pltpu.SemaphoreType.DMA((5,)),
        ],
        compiler_params=pltpu.CompilerParams(vmem_limit_bytes=30 << 20),
        cost_estimate=cost(
            2 * count * width * units * (5 if fresh else 3), 2 * width * (3 * units + 4 * count)
        ),
        name="experts_first" if fresh else "experts_last",
    )(*operands)


def side_by_side(pieces):
    micro, copies, tokens, columns = pieces.shape

    def kernel(pieces_ref, out_ref):
        for c in range(copies):
            out_ref[:, :, c * columns : (c + 1) * columns] = pieces_ref[:, c]

    return pl.pallas_call(
        kernel,
        out_shape=jax.ShapeDtypeStruct((micro, tokens, copies * columns), pieces.dtype),
        compiler_params=pltpu.CompilerParams(vmem_limit_bytes=8 << 20),
        name="side_by_side",
    )(pieces)


def shards(saved_inputs, top_grad, routes, mix_weights, w_gate, w_up, w_down, q_prev):
    sections = lax.axis_size("pipe")
    last = lax.axis_index("pipe") == sections - 1
    peers = lax.axis_size("expert")
    expert_index = lax.axis_index("expert")
    replicas = lax.axis_size("dp")
    dp_index = lax.axis_index("dp")
    gate, up, down = (w_gate[0, 0, 0], w_up[0, 0, 0], w_down[0, 0, 0])
    right = q_prev[0, 0, 0].transpose(0, 2, 1)
    copies = peers // EXPERTS
    tokens = saved_inputs.shape[2]
    rows = MICRO * tokens
    slots = MICRO * CAP
    columns = D // copies
    major, minor = (expert_index // copies, expert_index % copies)

    own_inputs = saved_inputs[0].reshape(rows, D)
    top_rows = top_grad.reshape(rows, D)
    rank = slots_of(routes[0])
    part_ids = lax.dynamic_index_in_dim(routes[0] * CAP + rank, major, 0, keepdims=False)
    first, second = hit_table(part_ids, EXPERTS * CAP)
    deal_pick = (first | second).astype(BF)
    part_pick = deal_pick.reshape(EXPERTS, CAP, tokens).transpose(0, 2, 1)

    own_slots, own_grads, slot_weights = pick_slots(
        major,
        routes[0].transpose(0, 2, 1),
        mix_weights[0].transpose(0, 2, 1),
        own_inputs,
        top_rows,
    )
    inputs_both = (own_slots, swap_cores(own_slots))
    *forward, own_half, other_half, inputs = experts(
        gate, up, down, (own_grads, swap_cores(own_grads)), copies, inputs_both=inputs_both
    )

    def reduced(own_half, other_half, base, targets):
        other = swap_cores(other_half)
        mine = (own_half + other.astype(F32)).astype(BF)
        pieces = exchange(mine.reshape(peers, CAP, columns))
        return combine(
            pieces.reshape(EXPERTS, copies, CAP, columns), part_pick, base, targets
        )

    top_part = lax.dynamic_slice(
        top_grad, (major, 0, minor * columns), (1, tokens, columns)
    ).reshape(tokens, columns)
    part = reduced(own_half, other_half, top_part, 1)[0]
    incoming = lax.ppermute(part, "pipe", [(i, i - 1) for i in range(1, sections)])
    base, pieces = deal(last, top_part, incoming, deal_pick, copies)
    own_rows = exchange(pieces.reshape(peers, CAP, columns))
    own_grads = scale_rows(own_rows.reshape(MICRO, copies, CAP, columns), slot_weights)
    sums, own_half, other_half, grads, grad_rows = experts(
        gate,
        up,
        down,
        (own_grads, swap_cores(own_grads)),
        copies,
        forward=forward,
        right=right,
    )
    parts = reduced(own_half, other_half, base, peers)
    produced = exchange(parts)
    produced = side_by_side(produced.reshape(MICRO, copies, tokens, columns))

    other = swap_cores(sums)
    sums = sums.astype(F32) + jnp.concatenate([other[slots:], other[:slots]]).astype(F32)
    sums = add_copies(sums, copies)
    squares = (
        times(inputs, inputs, 1, 1),
        times(grad_rows, inputs, 1, 1),
        times(grad_rows, grad_rows, 1, 1),
    )
    q_next, basis = finish(
        dp_index,
        sums,
        squares,
        (inputs, grad_rows),
        grads,
        replicas * rows,
    )
    return (
        produced.reshape(1, MICRO, tokens, D),
        basis.T[None, None, None],
        q_next.transpose(0, 2, 1)[None, None, None],
    )


def solution(mesh):
    placed = (
        P("pipe", None, "dp", None),
        P(None, "dp", None),
        P("pipe", None, "dp", None),
        P("pipe", None, "dp", None),
        P("pipe", "expert", None, None, "dp"),
        P("pipe", "expert", None, None, "dp"),
        P("pipe", "expert", None, "dp", None),
        P("pipe", "expert", None, None, "dp", None),
    )
    return jax.shard_map(
        shards,
        mesh=mesh,
        in_specs=placed,
        out_specs=(
            P("pipe", None, "dp", None),
            P("pipe", "expert", None, "dp", None),
            P("pipe", "expert", None, None, "dp", None),
        ),
        check_vma=False,
    )
```

```python
import math

import jax
import jax.numpy as jnp
from jax import lax
from jax.experimental import pallas as pl
from jax.experimental.pallas import tpu as pltpu
from jax.sharding import PartitionSpec as P

D = 3072
EXPERTS = 4
R = 64
MICRO = 4
CAP = 48

BF = jnp.bfloat16
F32 = jnp.float32
IN_SMEM = pl.BlockSpec(memory_space=pltpu.SMEM)
IN_VMEM = pl.BlockSpec(memory_space=pltpu.VMEM)
IN_HBM = pl.BlockSpec(memory_space=pltpu.HBM)


def cost(flops, moved):
    return pl.CostEstimate(flops=int(flops), bytes_accessed=int(moved), transcendentals=0)


def swap_cores(value):
    return lax.ppermute(value, "dp", [(0, 1), (1, 0)])


def exchange(pieces):
    return lax.all_to_all(pieces, "expert", 0, 0, tiled=True)


def times(a, b, ca=1, cb=0, precision=None):
    return lax.dot_general(
        a, b, (((ca,), (cb,)), ((), ())), preferred_element_type=F32, precision=precision
    )


def slots_of(route_rows):
    flat = route_rows.reshape(MICRO, -1)
    count = flat.shape[1]
    earlier = lax.broadcasted_iota(jnp.int32, (count, count), 1) < lax.broadcasted_iota(
        jnp.int32, (count, count), 0
    )
    same = (flat[:, :, None] == flat[:, None, :]) & earlier[None]
    return jnp.sum(same.astype(jnp.int32), axis=2).reshape(route_rows.shape)


def hit_table(ids, count):
    rows = lax.broadcasted_iota(jnp.int32, (count, ids.shape[0]), 0)
    return rows == ids[None, :, 0], rows == ids[None, :, 1]


def add_copies(values, copies):
    def x_pair(i):
        return i ^ 1

    def y_pair(i):
        return i ^ 2

    def y_cross(i):
        y = i // 2 % 4
        return i + (((3 - y) % 4) - y) * 2

    for partner in (x_pair, y_pair, y_cross):
        route = [(i, partner(i)) for i in range(copies * EXPERTS)]
        rounded = values.astype(BF)
        other = lax.ppermute(rounded, "expert", route)
        values = rounded.astype(F32) + other.astype(F32)
    return values


def inverse_lower(gram):
    height = 8
    lanes = lax.broadcasted_iota(jnp.int32, (height, 2 * R), 1)
    depth = lax.broadcasted_iota(jnp.int32, (height, 2 * R), 0)
    blocks = []
    for b in range(R // height):
        rows = gram[b * height : (b + 1) * height, :]
        held = jnp.concatenate([jnp.zeros((height, R), F32), rows], 1)
        blocks.append(jnp.where(lanes == depth + b * height, 1.0, held))
    for k in range(R):
        at, row = divmod(k, height)
        pivot_row = blocks[at][row : row + 1, :]
        pivot_row = pivot_row * (1.0 / pivot_row[:, R + k : R + k + 1])
        for b in range((k + 1) // height, R // height):
            below = blocks[b] - blocks[b][:, R + k : R + k + 1] * pivot_row
            blocks[b] = jnp.where(depth + b * height > k, below, blocks[b]) if b == at else below
    for b in range(R // height):
        diagonal = jnp.where(lanes == depth + R + b * height, blocks[b], 0.0)
        pivots = jnp.sum(diagonal, axis=1, keepdims=True)
        blocks[b] = (blocks[b] * lax.rsqrt(pivots))[:, :R]
    return jnp.concatenate(blocks, axis=0)


def halves(value):
    high = value.astype(BF)
    return high, (value - high.astype(F32)).astype(BF)


def finish(dp_index, sums, squares, rows16, grads, token_total):
    count, wide = rows16[0].shape
    half = wide // 2
    units = grads.shape[2]

    def kernel(dp_ref, sums_ref, *refs):
        squares_hbm, rows_hbm, grads_hbm = (refs[:3], refs[3:5], refs[5])
        q_ref, basis_ref, squares_ref, rows_ref, grads_ref, done = refs[6:]
        start = pl.multiple_of(dp_ref[0] * half, half)
        moves = [
            pltpu.make_async_copy(squares_hbm[i], squares_ref.at[i], done.at[i]) for i in range(3)
        ]
        moves.append(pltpu.make_async_copy(grads_hbm, grads_ref, done.at[3]))
        moves += [
            pltpu.make_async_copy(
                rows_hbm[i].at[:, pl.ds(start, half)],
                rows_ref.at[pl.ds(i * count, count)],
                done.at[4 + i],
            )
            for i in range(2)
        ]
        for move in moves:
            move.start()
        turned = sums_ref[...].T
        of_inputs, of_grads = (turned[:R].astype(BF), turned[R:].astype(BF))
        for move in moves[:3]:
            move.wait()

        def twice(left, right, cb):
            high, low = halves(right)
            return times(left, high, 1, cb) + times(left, low, 1, cb)

        inputs_inputs, grads_inputs, grads_grads = (squares_ref[i] for i in range(3))
        along_inputs = twice(of_inputs, inputs_inputs, 0) + twice(of_grads, grads_inputs, 0)
        along_grads = twice(of_inputs, grads_inputs, 1) + twice(of_grads, grads_grads, 0)
        gram = twice(of_inputs, along_inputs, 1) + twice(of_grads, along_grads, 1)
        inverse = inverse_lower(0.5 * (gram + gram.T))
        exact = lax.Precision.HIGHEST
        weights = jnp.concatenate(
            [
                times(inverse, of_inputs.astype(F32), 1, 0, exact),
                times(inverse, of_grads.astype(F32), 1, 0, exact),
            ],
            axis=1,
        ).astype(BF)
        scale = 1.0 / math.sqrt(float(token_total))
        along_inputs = times(inverse, along_inputs, 1, 0, exact).astype(BF)
        along_grads = times(inverse, along_grads, 1, 0, exact).astype(BF)
        for move in moves[3:]:
            move.wait()
        q_ref[0] = times(along_inputs, grads_ref[0]) * scale
        q_ref[1] = times(along_inputs, grads_ref[1]) * scale
        q_ref[2] = times(along_grads, grads_ref[2]) * scale
        basis_ref[...] = times(weights, rows_ref[...]) * math.sqrt(float(wide))

    return pl.pallas_call(
        kernel,
        out_shape=(
            jax.ShapeDtypeStruct((3, R, units), F32),
            jax.ShapeDtypeStruct((R, half), F32),
        ),
        in_specs=[IN_SMEM, IN_VMEM] + [IN_HBM] * 6,
        scratch_shapes=[
            pltpu.VMEM((3, count, count), F32),
            pltpu.VMEM((2 * count, half), BF),
            pltpu.VMEM((3, count, units), BF),
            pltpu.SemaphoreType.DMA((6,)),
        ],
        compiler_params=pltpu.CompilerParams(vmem_limit_bytes=61 << 20),
        cost_estimate=cost(4 * R * count * wide, 2 * count * (wide + 3 * units) + 12 * count**2),
        name="finish",
    )(dp_index.reshape(1), sums, *squares, *rows16, grads)


def pick_slots(own_expert, routes, values, mix=None):
    micro, _, tokens = routes.shape
    width = values.shape[1]
    block = width // 4
    count = micro * CAP
    weighted = mix is not None

    def kernel(expert_ref, routes_ref, *refs):
        values_ref, slots_ref = (refs[weighted], refs[weighted + 1])
        expert = expert_ref[0]
        filler = jnp.zeros((8 - micro, tokens), F32)
        first = routes_ref[:, 0, :] == expert
        second = routes_ref[:, 1, :] == expert
        hit = jnp.where(first | second, 1.0, 0.0)
        earlier = lax.broadcasted_iota(jnp.int32, (tokens, tokens), 0) < lax.broadcasted_iota(
            jnp.int32, (tokens, tokens), 1
        )
        counted = jnp.concatenate([hit, filler]).astype(BF)
        rank = times(counted, jnp.where(earlier, 1.0, 0.0).astype(BF))[:micro]
        base = lax.broadcasted_iota(jnp.int32, (micro, tokens), 0).astype(F32) * CAP
        place = jnp.where(hit > 0.0, rank + base, -1.0)
        place = jnp.concatenate([place[m : m + 1] for m in range(micro)], axis=1)
        slot = lax.broadcasted_iota(jnp.int32, (count, micro * tokens), 0).astype(F32)
        chosen = slot == place
        pick = jnp.where(chosen, 1.0, 0.0).astype(BF)
        by_slot = 1.0
        if weighted:
            mix_ref, w_ref = (refs[0], refs[3])
            weight = jnp.where(first, mix_ref[:, 0, :], 0.0)
            weight = weight + jnp.where(second, mix_ref[:, 1, :], 0.0)
            weight = jnp.concatenate([weight[m : m + 1] for m in range(micro)], axis=1)
            by_slot = jnp.sum(jnp.where(chosen, weight, 0.0), axis=1, keepdims=True)
            w_ref[...] = jnp.broadcast_to(by_slot, (count, 128))
        for at in range(0, width, block):
            held = pl.ds(at, block)
            slots_ref[:, held] = (by_slot * times(pick, values_ref[:, held])).astype(BF)

    slots_shape = jax.ShapeDtypeStruct((count, width), BF)
    operands = (own_expert.reshape(1), routes, *([mix] if weighted else []), values)
    return pl.pallas_call(
        kernel,
        out_shape=(slots_shape, jax.ShapeDtypeStruct((count, 128), F32))
        if weighted
        else slots_shape,
        in_specs=[IN_SMEM] + [IN_VMEM] * (len(operands) - 1),
        compiler_params=pltpu.CompilerParams(vmem_limit_bytes=12 << 20),
        cost_estimate=cost(2 * count * micro * tokens * width, 2 * (count + micro * tokens) * width),
        name="pick_weighted" if weighted else "pick_slots",
    )(*operands)


def scale_rows(pieces, slot_weights):
    micro, copies, cap, columns = pieces.shape

    def kernel(pieces_ref, w_ref, out_ref):
        for m in range(micro):
            held = pl.ds(m * cap, cap)
            weight = w_ref[held, :1]
            for c in range(copies):
                scaled = weight * pieces_ref[m, c].astype(F32)
                out_ref[held, c * columns : (c + 1) * columns] = scaled.astype(BF)

    return pl.pallas_call(
        kernel,
        out_shape=jax.ShapeDtypeStruct((micro * cap, copies * columns), BF),
        compiler_params=pltpu.CompilerParams(vmem_limit_bytes=8 << 20),
        name="scale_rows",
    )(pieces, slot_weights)


def combine(pieces, pick, base, peers):
    experts_count, copies, _, columns = pieces.shape
    tokens = base.shape[0]

    def kernel(pieces_ref, pick_ref, base_ref, out_ref):
        share = base_ref[...].astype(F32)
        for e in range(experts_count):
            total = pieces_ref[e, 0].astype(F32)
            for c in range(1, copies):
                total = total + pieces_ref[e, c].astype(F32)
            for term in halves(total):
                share = share + times(pick_ref[e], term)
        part = share.astype(BF)
        for peer in range(peers):
            out_ref[peer] = part

    return pl.pallas_call(
        kernel,
        out_shape=jax.ShapeDtypeStruct((peers, tokens, columns), BF),
        compiler_params=pltpu.CompilerParams(vmem_limit_bytes=8 << 20),
        name="combine",
    )(pieces, pick, base)


def deal(last, top_part, incoming, pick, copies):
    tokens, columns = incoming.shape
    slots = pick.shape[0]
    cap = slots // EXPERTS

    def kernel(last_ref, top_ref, incoming_ref, pick_ref, base_ref, out_ref):
        base = jnp.where(last_ref[0] == 1, top_ref[...].astype(F32), incoming_ref[...].astype(F32))
        base = base.astype(BF)
        base_ref[...] = base
        listed = times(pick_ref[...], base).astype(BF)
        for e in range(EXPERTS):
            for c in range(copies):
                out_ref[e, c] = listed[e * cap : (e + 1) * cap]

    return pl.pallas_call(
        kernel,
        out_shape=(
            jax.ShapeDtypeStruct((tokens, columns), BF),
            jax.ShapeDtypeStruct((EXPERTS, copies, cap, columns), BF),
        ),
        in_specs=[IN_SMEM] + [IN_VMEM] * 3,
        compiler_params=pltpu.CompilerParams(vmem_limit_bytes=8 << 20),
        cost_estimate=cost(2 * slots * tokens * columns, 60 << 20),
        name="deal",
    )(last.astype(jnp.int32).reshape(1), top_part, incoming, pick)


def fetch(arrays):
    count = len(arrays)

    def kernel(*refs):
        done = refs[-1]
        moves = [
            pltpu.make_async_copy(refs[i], refs[count + i], done.at[i]) for i in range(count)
        ]
        for move in moves:
            move.start()
        for move in moves:
            move.wait()

    return pl.pallas_call(
        kernel,
        out_shape=tuple(jax.ShapeDtypeStruct(a.shape, a.dtype) for a in arrays),
        in_specs=[IN_HBM] * count,
        out_specs=(IN_VMEM,) * count,
        scratch_shapes=[pltpu.SemaphoreType.DMA((count,))],
        compiler_params=pltpu.CompilerParams(vmem_limit_bytes=12 << 20),
    )(*arrays)


def expert_slopes(down, grads_both, forward, right):
    slots, width = grads_both[0].shape
    count = 2 * slots
    units = right.shape[2]
    square = (count, units)

    def kernel(*refs):
        own_ref, partner_ref, down_ref, slope_ref, silu_ref, hidden_ref, right_ref = refs[:7]
        sums_ref, gg_ref, gu_ref, grads_hbm, rows_hbm, done = refs[7:]
        moves = []

        def keep(source, target):
            move = pltpu.make_async_copy(source, target, done.at[len(moves)])
            move.start()
            moves.append(move)

        keep(own_ref, rows_hbm.at[pl.ds(0, slots)])
        keep(partner_ref, rows_hbm.at[pl.ds(slots, slots)])
        keep(hidden_ref, grads_hbm.at[2])
        rows = jnp.concatenate([own_ref[...], partner_ref[...]])
        grad_hidden = times(rows, down_ref[...], 1, 1)
        gg_ref[...] = (grad_hidden * slope_ref[...]).astype(BF)
        gu_ref[...] = (grad_hidden * silu_ref[...]).astype(BF)
        keep(gg_ref, grads_hbm.at[0])
        keep(gu_ref, grads_hbm.at[1])
        right16 = right_ref[...].astype(BF)
        of_inputs = times(gg_ref[...], right16[0], 1, 1) + times(gu_ref[...], right16[1], 1, 1)
        of_grads = times(hidden_ref[...], right16[2], 1, 1)
        sums_ref[...] = jnp.concatenate([of_inputs, of_grads], axis=1).astype(BF)
        for move in moves:
            move.wait()

    return pl.pallas_call(
        kernel,
        out_shape=(
            jax.ShapeDtypeStruct((count, 2 * R), BF),
            jax.ShapeDtypeStruct(square, BF),
            jax.ShapeDtypeStruct(square, BF),
            jax.ShapeDtypeStruct((3, *square), BF),
            jax.ShapeDtypeStruct((count, width), BF),
        ),
        in_specs=[IN_VMEM] * 7,
        out_specs=(*[IN_VMEM] * 3, *[IN_HBM] * 2),
        scratch_shapes=[pltpu.SemaphoreType.DMA((5,))],
        compiler_params=pltpu.CompilerParams(vmem_limit_bytes=20 << 20),
        cost_estimate=cost(
            2 * count * width * units, 2 * width * (units + 2 * count) + 12 * count * units
        ),
        name="expert_slopes",
    )(*grads_both, down, *forward, right)


def expert_rows(gate, up, grad_gate, grad_up, copies):
    width, units = gate.shape
    count = grad_gate.shape[0]
    slots = count // 2
    columns = width // copies
    shape = (MICRO, copies, CAP, columns)

    def kernel(gg_ref, gu_ref, gate_hbm, up_hbm, own_ref, par_ref, gate_ref, up_ref, done):
        def arrival(c, which):
            source, target = ((gate_hbm, gate_ref), (up_hbm, up_ref))[which]
            held = pl.ds(c * columns, columns)
            return pltpu.make_async_copy(source.at[held], target.at[c], done.at[which, c])

        for c in range(copies):
            arrival(c, 0).start()
            arrival(c, 1).start()
        for c in range(copies):
            arrival(c, 0).wait()
            total = times(gg_ref[...], gate_ref[c], 1, 1)
            arrival(c, 1).wait()
            total = total + times(gu_ref[...], up_ref[c], 1, 1)
            for m in range(MICRO):
                own_ref[m, c] = total[m * CAP : (m + 1) * CAP]
                par_ref[m, c] = total[slots + m * CAP : slots + (m + 1) * CAP].astype(BF)

    return pl.pallas_call(
        kernel,
        out_shape=(jax.ShapeDtypeStruct(shape, F32), jax.ShapeDtypeStruct(shape, BF)),
        in_specs=[IN_VMEM] * 2 + [IN_HBM] * 2,
        scratch_shapes=[
            pltpu.VMEM((copies, columns, units), BF),
            pltpu.VMEM((copies, columns, units), BF),
            pltpu.SemaphoreType.DMA((2, copies)),
        ],
        compiler_params=pltpu.CompilerParams(vmem_limit_bytes=24 << 20),
        cost_estimate=cost(
            4 * count * width * units, 4 * width * units + 6 * count * width
        ),
        name="expert_rows",
    )(grad_gate, grad_up, gate, up)


def experts(gate, up, down, grads_both, copies, inputs_both):
    slots, width = grads_both[0].shape
    count = 2 * slots
    units = gate.shape[1]
    columns = width // copies
    halves_shape = (MICRO, copies, CAP, columns)
    square = (count, units)
    made = [(square, F32), (square, F32), (square, BF), (halves_shape, F32), (halves_shape, BF)]

    def kernel(*refs):
        grads_refs, (down_ref, gate_ref, up_ref), rows_refs = (refs[:2], refs[2:5], refs[5:7])
        slope_ref, silu_ref, hidden_ref, own_ref, par_ref, rows_hbm = refs[7:13]
        gg_ref, gu_ref, done = refs[13:]
        moves = [
            pltpu.make_async_copy(rows_refs[i], rows_hbm.at[pl.ds(i * slots, slots)], done.at[i])
            for i in range(2)
        ]
        for move in moves:
            move.start()

        def both(pair):
            return jnp.concatenate([pair[0][...], pair[1][...]])

        inputs = both(rows_refs)
        pre_gate = times(inputs, gate_ref[...])
        pre_up = times(inputs, up_ref[...])
        sigmoid = 1.0 / (1.0 + jnp.exp(-pre_gate))
        silu = pre_gate * sigmoid
        slope_ref[...] = pre_up * sigmoid * (1.0 + pre_gate * (1.0 - sigmoid))
        silu_ref[...] = silu
        hidden_ref[...] = (silu * pre_up).astype(BF)
        grad_hidden = times(both(grads_refs), down_ref[...], 1, 1)
        gg_ref[...] = (grad_hidden * slope_ref[...]).astype(BF)
        gu_ref[...] = (grad_hidden * silu_ref[...]).astype(BF)

        def column(c, carry):
            held = pl.ds(pl.multiple_of(c * columns, columns), columns)
            total = times(gg_ref[...], gate_ref[held, :], 1, 1)
            total = total + times(gu_ref[...], up_ref[held, :], 1, 1)
            for m in range(MICRO):
                own_ref[m, c] = total[m * CAP : (m + 1) * CAP]
                par_ref[m, c] = total[slots + m * CAP : slots + (m + 1) * CAP].astype(BF)
            return carry

        lax.fori_loop(0, copies, column, 0)
        for move in moves:
            move.wait()

    return pl.pallas_call(
        kernel,
        out_shape=(
            *[jax.ShapeDtypeStruct(*result) for result in made],
            jax.ShapeDtypeStruct((count, width), BF),
        ),
        in_specs=[IN_VMEM] * 7,
        out_specs=(*[IN_VMEM] * 5, IN_HBM),
        scratch_shapes=[
            pltpu.VMEM(square, BF),
            pltpu.VMEM(square, BF),
            pltpu.SemaphoreType.DMA((2,)),
        ],
        compiler_params=pltpu.CompilerParams(vmem_limit_bytes=30 << 20),
        cost_estimate=cost(10 * count * width * units, 2 * width * (3 * units + 4 * count)),
        name="experts_first",
    )(*grads_both, down, gate, up, *inputs_both)


def side_by_side(pieces):
    micro, copies, tokens, columns = pieces.shape

    def kernel(pieces_ref, out_ref):
        for c in range(copies):
            out_ref[:, :, c * columns : (c + 1) * columns] = pieces_ref[:, c]

    return pl.pallas_call(
        kernel,
        out_shape=jax.ShapeDtypeStruct((micro, tokens, copies * columns), pieces.dtype),
        compiler_params=pltpu.CompilerParams(vmem_limit_bytes=8 << 20),
        name="side_by_side",
    )(pieces)


def shards(saved_inputs, top_grad, routes, mix_weights, w_gate, w_up, w_down, q_prev):
    sections = lax.axis_size("pipe")
    last = lax.axis_index("pipe") == sections - 1
    peers = lax.axis_size("expert")
    expert_index = lax.axis_index("expert")
    replicas = lax.axis_size("dp")
    dp_index = lax.axis_index("dp")
    gate, up, down = (w_gate[0, 0, 0], w_up[0, 0, 0], w_down[0, 0, 0])
    right = q_prev[0, 0, 0].transpose(0, 2, 1)
    copies = peers // EXPERTS
    tokens = saved_inputs.shape[2]
    rows = MICRO * tokens
    slots = MICRO * CAP
    columns = D // copies
    major, minor = (expert_index // copies, expert_index % copies)

    own_inputs = saved_inputs[0].reshape(rows, D)
    top_rows = top_grad.reshape(rows, D)
    rank = slots_of(routes[0])
    part_ids = lax.dynamic_index_in_dim(routes[0] * CAP + rank, major, 0, keepdims=False)
    first, second = hit_table(part_ids, EXPERTS * CAP)
    deal_pick = (first | second).astype(BF)
    part_pick = deal_pick.reshape(EXPERTS, CAP, tokens).transpose(0, 2, 1)

    routes_by_choice = routes[0].transpose(0, 2, 1)
    own_slots = pick_slots(major, routes_by_choice, own_inputs)
    inputs_both = (own_slots, swap_cores(own_slots))
    own_grads, slot_weights = pick_slots(
        major, routes_by_choice, top_rows, mix_weights[0].transpose(0, 2, 1)
    )
    gate_first, up_first = fetch((gate, up))
    *forward, own_half, other_half, inputs = experts(
        gate_first, up_first, down, (own_grads, swap_cores(own_grads)), copies, inputs_both=inputs_both
    )

    def reduced(own_half, other_half, base, targets):
        other = swap_cores(other_half)
        mine = (own_half + other.astype(F32)).astype(BF)
        pieces = exchange(mine.reshape(peers, CAP, columns))
        return combine(
            pieces.reshape(EXPERTS, copies, CAP, columns), part_pick, base, targets
        )

    top_part = lax.dynamic_slice(
        top_grad, (major, 0, minor * columns), (1, tokens, columns)
    ).reshape(tokens, columns)
    part = reduced(own_half, other_half, top_part, 1)[0]
    incoming = lax.ppermute(part, "pipe", [(i, i - 1) for i in range(1, sections)])
    base, pieces = deal(last, top_part, incoming, deal_pick, copies)
    own_rows = exchange(pieces.reshape(peers, CAP, columns))
    own_grads = scale_rows(own_rows.reshape(MICRO, copies, CAP, columns), slot_weights)
    sums, grad_gate, grad_up, grads, grad_rows = expert_slopes(
        down, (own_grads, swap_cores(own_grads)), forward, right
    )
    other_sums = swap_cores(sums)
    own_half, other_half = expert_rows(gate, up, grad_gate, grad_up, copies)
    parts = reduced(own_half, other_half, base, peers)
    produced = exchange(parts)
    produced = side_by_side(produced.reshape(MICRO, copies, tokens, columns))

    sums = sums.astype(F32) + jnp.concatenate([other_sums[slots:], other_sums[:slots]]).astype(F32)
    sums = add_copies(sums, copies)
    squares = (
        times(inputs, inputs, 1, 1),
        times(grad_rows, inputs, 1, 1),
        times(grad_rows, grad_rows, 1, 1),
    )
    q_next, basis = finish(
        dp_index,
        sums,
        squares,
        (inputs, grad_rows),
        grads,
        replicas * rows,
    )
    return (
        produced.reshape(1, MICRO, tokens, D),
        basis.T[None, None, None],
        q_next.transpose(0, 2, 1)[None, None, None],
    )


def solution(mesh):
    placed = (
        P("pipe", None, "dp", None),
        P(None, "dp", None),
        P("pipe", None, "dp", None),
        P("pipe", None, "dp", None),
        P("pipe", "expert", None, None, "dp"),
        P("pipe", "expert", None, None, "dp"),
        P("pipe", "expert", None, "dp", None),
        P("pipe", "expert", None, None, "dp", None),
    )
    return jax.shard_map(
        shards,
        mesh=mesh,
        in_specs=placed,
        out_specs=(
            P("pipe", None, "dp", None),
            P("pipe", "expert", None, "dp", None),
            P("pipe", "expert", None, None, "dp", None),
        ),
        check_vma=False,
    )
```

```python
import math

import jax
import jax.numpy as jnp
from jax import lax
from jax.experimental import pallas as pl
from jax.experimental.pallas import tpu as pltpu
from jax.sharding import PartitionSpec as P

D = 3072
EXPERTS = 4
R = 64
MICRO = 4
CAP = 48

BF = jnp.bfloat16
F32 = jnp.float32
IN_SMEM = pl.BlockSpec(memory_space=pltpu.SMEM)
IN_VMEM = pl.BlockSpec(memory_space=pltpu.VMEM)
IN_HBM = pl.BlockSpec(memory_space=pltpu.HBM)


def cost(flops, moved):
    return pl.CostEstimate(flops=int(flops), bytes_accessed=int(moved), transcendentals=0)


def swap_cores(value):
    return lax.ppermute(value, "dp", [(0, 1), (1, 0)])


def exchange(pieces):
    return lax.all_to_all(pieces, "expert", 0, 0, tiled=True)


def times(a, b, ca=1, cb=0, precision=None):
    return lax.dot_general(
        a, b, (((ca,), (cb,)), ((), ())), preferred_element_type=F32, precision=precision
    )


def slots_of(route_rows):
    flat = route_rows.reshape(MICRO, -1)
    count = flat.shape[1]
    earlier = lax.broadcasted_iota(jnp.int32, (count, count), 1) < lax.broadcasted_iota(
        jnp.int32, (count, count), 0
    )
    same = (flat[:, :, None] == flat[:, None, :]) & earlier[None]
    return jnp.sum(same.astype(jnp.int32), axis=2).reshape(route_rows.shape)


def hit_table(ids, count):
    rows = lax.broadcasted_iota(jnp.int32, (count, ids.shape[0]), 0)
    return rows == ids[None, :, 0], rows == ids[None, :, 1]


def add_copies(values, copies):
    def x_pair(i):
        return i ^ 1

    def y_pair(i):
        return i ^ 2

    def y_cross(i):
        y = i // 2 % 4
        return i + (((3 - y) % 4) - y) * 2

    for partner in (x_pair, y_pair, y_cross):
        route = [(i, partner(i)) for i in range(copies * EXPERTS)]
        rounded = values.astype(BF)
        other = lax.ppermute(rounded, "expert", route)
        values = rounded.astype(F32) + other.astype(F32)
    return values


def inverse_lower(gram):
    height = 8
    lanes = lax.broadcasted_iota(jnp.int32, (height, 2 * R), 1)
    depth = lax.broadcasted_iota(jnp.int32, (height, 2 * R), 0)
    blocks = []
    for b in range(R // height):
        rows = gram[b * height : (b + 1) * height, :]
        held = jnp.concatenate([jnp.zeros((height, R), F32), rows], 1)
        blocks.append(jnp.where(lanes == depth + b * height, 1.0, held))
    for k in range(R):
        at, row = divmod(k, height)
        pivot_row = blocks[at][row : row + 1, :]
        pivot_row = pivot_row * (1.0 / pivot_row[:, R + k : R + k + 1])
        for b in range((k + 1) // height, R // height):
            below = blocks[b] - blocks[b][:, R + k : R + k + 1] * pivot_row
            blocks[b] = jnp.where(depth + b * height > k, below, blocks[b]) if b == at else below
    for b in range(R // height):
        diagonal = jnp.where(lanes == depth + R + b * height, blocks[b], 0.0)
        pivots = jnp.sum(diagonal, axis=1, keepdims=True)
        blocks[b] = (blocks[b] * lax.rsqrt(pivots))[:, :R]
    return jnp.concatenate(blocks, axis=0)


def halves(value):
    high = value.astype(BF)
    return high, (value - high.astype(F32)).astype(BF)


def finish(dp_index, sums, squares, rows16, grads, token_total):
    count, wide = rows16[0].shape
    half = wide // 2
    units = grads.shape[2]

    def kernel(dp_ref, sums_ref, *refs):
        squares_hbm, rows_hbm, grads_hbm = (refs[:3], refs[3:5], refs[5])
        q_ref, basis_ref, squares_ref, rows_ref, grads_ref, done = refs[6:]
        start = pl.multiple_of(dp_ref[0] * half, half)
        moves = [
            pltpu.make_async_copy(squares_hbm[i], squares_ref.at[i], done.at[i]) for i in range(3)
        ]
        moves.append(pltpu.make_async_copy(grads_hbm, grads_ref, done.at[3]))
        moves += [
            pltpu.make_async_copy(
                rows_hbm[i].at[:, pl.ds(start, half)],
                rows_ref.at[pl.ds(i * count, count)],
                done.at[4 + i],
            )
            for i in range(2)
        ]
        for move in moves:
            move.start()
        turned = sums_ref[...].T
        of_inputs, of_grads = (turned[:R].astype(BF), turned[R:].astype(BF))
        for move in moves[:3]:
            move.wait()

        def twice(left, right, cb):
            high, low = halves(right)
            return times(left, high, 1, cb) + times(left, low, 1, cb)

        inputs_inputs, grads_inputs, grads_grads = (squares_ref[i] for i in range(3))
        along_inputs = twice(of_inputs, inputs_inputs, 0) + twice(of_grads, grads_inputs, 0)
        along_grads = twice(of_inputs, grads_inputs, 1) + twice(of_grads, grads_grads, 0)
        gram = twice(of_inputs, along_inputs, 1) + twice(of_grads, along_grads, 1)
        inverse = inverse_lower(0.5 * (gram + gram.T))
        exact = lax.Precision.HIGHEST
        weights = jnp.concatenate(
            [
                times(inverse, of_inputs.astype(F32), 1, 0, exact),
                times(inverse, of_grads.astype(F32), 1, 0, exact),
            ],
            axis=1,
        ).astype(BF)
        scale = 1.0 / math.sqrt(float(token_total))
        along_inputs = times(inverse, along_inputs, 1, 0, exact).astype(BF)
        along_grads = times(inverse, along_grads, 1, 0, exact).astype(BF)
        for move in moves[3:]:
            move.wait()
        q_ref[0] = times(along_inputs, grads_ref[0]) * scale
        q_ref[1] = times(along_inputs, grads_ref[1]) * scale
        q_ref[2] = times(along_grads, grads_ref[2]) * scale
        basis_ref[...] = times(weights, rows_ref[...]) * math.sqrt(float(wide))

    return pl.pallas_call(
        kernel,
        out_shape=(
            jax.ShapeDtypeStruct((3, R, units), F32),
            jax.ShapeDtypeStruct((R, half), F32),
        ),
        in_specs=[IN_SMEM, IN_VMEM] + [IN_HBM] * 6,
        scratch_shapes=[
            pltpu.VMEM((3, count, count), F32),
            pltpu.VMEM((2 * count, half), BF),
            pltpu.VMEM((3, count, units), BF),
            pltpu.SemaphoreType.DMA((6,)),
        ],
        compiler_params=pltpu.CompilerParams(vmem_limit_bytes=61 << 20),
        cost_estimate=cost(4 * R * count * wide, 2 * count * (wide + 3 * units) + 12 * count**2),
        name="finish",
    )(dp_index.reshape(1), sums, *squares, *rows16, grads)


def pick_slots(own_expert, routes, values, mix=None):
    micro, _, tokens = routes.shape
    width = values.shape[1]
    block = width // 4
    count = micro * CAP
    weighted = mix is not None

    def kernel(expert_ref, routes_ref, *refs):
        values_ref, slots_ref = (refs[weighted], refs[weighted + 1])
        expert = expert_ref[0]
        filler = jnp.zeros((8 - micro, tokens), F32)
        first = routes_ref[:, 0, :] == expert
        second = routes_ref[:, 1, :] == expert
        hit = jnp.where(first | second, 1.0, 0.0)
        earlier = lax.broadcasted_iota(jnp.int32, (tokens, tokens), 0) < lax.broadcasted_iota(
            jnp.int32, (tokens, tokens), 1
        )
        counted = jnp.concatenate([hit, filler]).astype(BF)
        rank = times(counted, jnp.where(earlier, 1.0, 0.0).astype(BF))[:micro]
        base = lax.broadcasted_iota(jnp.int32, (micro, tokens), 0).astype(F32) * CAP
        place = jnp.where(hit > 0.0, rank + base, -1.0)
        place = jnp.concatenate([place[m : m + 1] for m in range(micro)], axis=1)
        slot = lax.broadcasted_iota(jnp.int32, (count, micro * tokens), 0).astype(F32)
        chosen = slot == place
        pick = jnp.where(chosen, 1.0, 0.0).astype(BF)
        by_slot = 1.0
        if weighted:
            mix_ref, w_ref = (refs[0], refs[3])
            weight = jnp.where(first, mix_ref[:, 0, :], 0.0)
            weight = weight + jnp.where(second, mix_ref[:, 1, :], 0.0)
            weight = jnp.concatenate([weight[m : m + 1] for m in range(micro)], axis=1)
            by_slot = jnp.sum(jnp.where(chosen, weight, 0.0), axis=1, keepdims=True)
            w_ref[...] = jnp.broadcast_to(by_slot, (count, 128))
        for at in range(0, width, block):
            held = pl.ds(at, block)
            slots_ref[:, held] = (by_slot * times(pick, values_ref[:, held])).astype(BF)

    slots_shape = jax.ShapeDtypeStruct((count, width), BF)
    operands = (own_expert.reshape(1), routes, *([mix] if weighted else []), values)
    return pl.pallas_call(
        kernel,
        out_shape=(slots_shape, jax.ShapeDtypeStruct((count, 128), F32))
        if weighted
        else slots_shape,
        in_specs=[IN_SMEM] + [IN_VMEM] * (len(operands) - 1),
        compiler_params=pltpu.CompilerParams(vmem_limit_bytes=12 << 20),
        cost_estimate=cost(2 * count * micro * tokens * width, 2 * (count + micro * tokens) * width),
        name="pick_weighted" if weighted else "pick_slots",
    )(*operands)


def scale_rows(pieces, slot_weights):
    micro, copies, cap, columns = pieces.shape

    def kernel(pieces_ref, w_ref, out_ref):
        for m in range(micro):
            held = pl.ds(m * cap, cap)
            weight = w_ref[held, :1]
            for c in range(copies):
                scaled = weight * pieces_ref[m, c].astype(F32)
                out_ref[held, c * columns : (c + 1) * columns] = scaled.astype(BF)

    return pl.pallas_call(
        kernel,
        out_shape=jax.ShapeDtypeStruct((micro * cap, copies * columns), BF),
        compiler_params=pltpu.CompilerParams(vmem_limit_bytes=8 << 20),
        name="scale_rows",
    )(pieces, slot_weights)


def combine(pieces, pick, base, peers):
    experts_count, copies, _, columns = pieces.shape
    tokens = base.shape[0]

    def kernel(pieces_ref, pick_ref, base_ref, out_ref):
        share = base_ref[...].astype(F32)
        for e in range(experts_count):
            total = pieces_ref[e, 0].astype(F32)
            for c in range(1, copies):
                total = total + pieces_ref[e, c].astype(F32)
            for term in halves(total):
                share = share + times(pick_ref[e], term)
        part = share.astype(BF)
        for peer in range(peers):
            out_ref[peer] = part

    return pl.pallas_call(
        kernel,
        out_shape=jax.ShapeDtypeStruct((peers, tokens, columns), BF),
        compiler_params=pltpu.CompilerParams(vmem_limit_bytes=8 << 20),
        name="combine",
    )(pieces, pick, base)


def deal(last, top_part, incoming, pick, copies):
    tokens, columns = incoming.shape
    slots = pick.shape[0]
    cap = slots // EXPERTS

    def kernel(last_ref, top_ref, incoming_ref, pick_ref, base_ref, out_ref):
        base = jnp.where(last_ref[0] == 1, top_ref[...].astype(F32), incoming_ref[...].astype(F32))
        base = base.astype(BF)
        base_ref[...] = base
        listed = times(pick_ref[...], base).astype(BF)
        for e in range(EXPERTS):
            for c in range(copies):
                out_ref[e, c] = listed[e * cap : (e + 1) * cap]

    return pl.pallas_call(
        kernel,
        out_shape=(
            jax.ShapeDtypeStruct((tokens, columns), BF),
            jax.ShapeDtypeStruct((EXPERTS, copies, cap, columns), BF),
        ),
        in_specs=[IN_SMEM] + [IN_VMEM] * 3,
        compiler_params=pltpu.CompilerParams(vmem_limit_bytes=8 << 20),
        cost_estimate=cost(2 * slots * tokens * columns, 60 << 20),
        name="deal",
    )(last.astype(jnp.int32).reshape(1), top_part, incoming, pick)


def fetch(arrays):
    count = len(arrays)

    def kernel(*refs):
        done = refs[-1]
        moves = [
            pltpu.make_async_copy(refs[i], refs[count + i], done.at[i]) for i in range(count)
        ]
        for move in moves:
            move.start()
        for move in moves:
            move.wait()

    return pl.pallas_call(
        kernel,
        out_shape=tuple(jax.ShapeDtypeStruct(a.shape, a.dtype) for a in arrays),
        in_specs=[IN_HBM] * count,
        out_specs=(IN_VMEM,) * count,
        scratch_shapes=[pltpu.SemaphoreType.DMA((count,))],
        compiler_params=pltpu.CompilerParams(vmem_limit_bytes=12 << 20),
    )(*arrays)


def expert_slopes(down, grads_both, forward, right):
    slots, width = grads_both[0].shape
    count = 2 * slots
    units = right.shape[2]
    square = (count, units)

    def kernel(*refs):
        own_ref, partner_ref, down_ref, slope_ref, silu_ref, hidden_ref, right_ref = refs[:7]
        sums_ref, gg_ref, gu_ref, rows_hbm, done = refs[7:]
        moves = []

        def keep(source, target):
            move = pltpu.make_async_copy(source, target, done.at[len(moves)])
            move.start()
            moves.append(move)

        keep(own_ref, rows_hbm.at[pl.ds(0, slots)])
        keep(partner_ref, rows_hbm.at[pl.ds(slots, slots)])
        rows = jnp.concatenate([own_ref[...], partner_ref[...]])
        grad_hidden = times(rows, down_ref[...], 1, 1)
        gg_ref[...] = (grad_hidden * slope_ref[...]).astype(BF)
        gu_ref[...] = (grad_hidden * silu_ref[...]).astype(BF)
        right16 = right_ref[...].astype(BF)
        of_inputs = times(gg_ref[...], right16[0], 1, 1) + times(gu_ref[...], right16[1], 1, 1)
        of_grads = times(hidden_ref[...], right16[2], 1, 1)
        sums_ref[...] = jnp.concatenate([of_inputs, of_grads], axis=1).astype(BF)
        for move in moves:
            move.wait()

    return pl.pallas_call(
        kernel,
        out_shape=(
            jax.ShapeDtypeStruct((count, 2 * R), BF),
            jax.ShapeDtypeStruct(square, BF),
            jax.ShapeDtypeStruct(square, BF),
            jax.ShapeDtypeStruct((count, width), BF),
        ),
        in_specs=[IN_VMEM] * 7,
        out_specs=(*[IN_VMEM] * 3, IN_HBM),
        scratch_shapes=[pltpu.SemaphoreType.DMA((2,))],
        compiler_params=pltpu.CompilerParams(vmem_limit_bytes=20 << 20),
        cost_estimate=cost(
            2 * count * width * units, 2 * width * (units + 2 * count) + 12 * count * units
        ),
        name="expert_slopes",
    )(*grads_both, down, *forward, right)


def expert_rows(gate, up, grad_gate, grad_up, hidden, copies):
    width, units = gate.shape
    count = grad_gate.shape[0]
    slots = count // 2
    columns = width // copies
    shape = (MICRO, copies, CAP, columns)

    def kernel(gg_ref, gu_ref, hidden_ref, gate_ref, up_ref, own_ref, par_ref, grads_hbm, done):
        moves = [
            pltpu.make_async_copy(source, grads_hbm.at[i], done.at[i])
            for i, source in enumerate((gg_ref, gu_ref, hidden_ref))
        ]
        for move in moves:
            move.start()

        def column(c, carry):
            held = pl.ds(pl.multiple_of(c * columns, columns), columns)
            total = times(gg_ref[...], gate_ref[held, :], 1, 1)
            total = total + times(gu_ref[...], up_ref[held, :], 1, 1)
            for m in range(MICRO):
                own_ref[m, c] = total[m * CAP : (m + 1) * CAP]
                par_ref[m, c] = total[slots + m * CAP : slots + (m + 1) * CAP].astype(BF)
            return carry

        lax.fori_loop(0, copies, column, 0)
        for move in moves:
            move.wait()

    return pl.pallas_call(
        kernel,
        out_shape=(
            jax.ShapeDtypeStruct(shape, F32),
            jax.ShapeDtypeStruct(shape, BF),
            jax.ShapeDtypeStruct((3, count, units), BF),
        ),
        in_specs=[IN_VMEM] * 5,
        out_specs=(IN_VMEM, IN_VMEM, IN_HBM),
        scratch_shapes=[pltpu.SemaphoreType.DMA((3,))],
        compiler_params=pltpu.CompilerParams(vmem_limit_bytes=24 << 20),
        cost_estimate=cost(4 * count * width * units, 4 * width * units + 6 * count * width),
        name="expert_rows",
    )(grad_gate, grad_up, hidden, gate, up)


def experts(gate, up, down, grads_both, copies, inputs_both):
    slots, width = grads_both[0].shape
    count = 2 * slots
    units = gate.shape[1]
    columns = width // copies
    halves_shape = (MICRO, copies, CAP, columns)
    square = (count, units)
    made = [(square, F32), (square, F32), (square, BF), (halves_shape, F32), (halves_shape, BF)]

    def kernel(*refs):
        grads_refs, (down_ref, gate_ref, up_ref), rows_refs = (refs[:2], refs[2:5], refs[5:7])
        slope_ref, silu_ref, hidden_ref, own_ref, par_ref, rows_hbm = refs[7:13]
        gg_ref, gu_ref, done = refs[13:]
        moves = [
            pltpu.make_async_copy(rows_refs[i], rows_hbm.at[pl.ds(i * slots, slots)], done.at[i])
            for i in range(2)
        ]
        for move in moves:
            move.start()

        def both(pair):
            return jnp.concatenate([pair[0][...], pair[1][...]])

        inputs = both(rows_refs)
        pre_gate = times(inputs, gate_ref[...])
        pre_up = times(inputs, up_ref[...])
        sigmoid = 1.0 / (1.0 + jnp.exp(-pre_gate))
        silu = pre_gate * sigmoid
        slope_ref[...] = pre_up * sigmoid * (1.0 + pre_gate * (1.0 - sigmoid))
        silu_ref[...] = silu
        hidden_ref[...] = (silu * pre_up).astype(BF)
        grad_hidden = times(both(grads_refs), down_ref[...], 1, 1)
        gg_ref[...] = (grad_hidden * slope_ref[...]).astype(BF)
        gu_ref[...] = (grad_hidden * silu_ref[...]).astype(BF)

        def column(c, carry):
            held = pl.ds(pl.multiple_of(c * columns, columns), columns)
            total = times(gg_ref[...], gate_ref[held, :], 1, 1)
            total = total + times(gu_ref[...], up_ref[held, :], 1, 1)
            for m in range(MICRO):
                own_ref[m, c] = total[m * CAP : (m + 1) * CAP]
                par_ref[m, c] = total[slots + m * CAP : slots + (m + 1) * CAP].astype(BF)
            return carry

        lax.fori_loop(0, copies, column, 0)
        for move in moves:
            move.wait()

    return pl.pallas_call(
        kernel,
        out_shape=(
            *[jax.ShapeDtypeStruct(*result) for result in made],
            jax.ShapeDtypeStruct((count, width), BF),
        ),
        in_specs=[IN_VMEM] * 7,
        out_specs=(*[IN_VMEM] * 5, IN_HBM),
        scratch_shapes=[
            pltpu.VMEM(square, BF),
            pltpu.VMEM(square, BF),
            pltpu.SemaphoreType.DMA((2,)),
        ],
        compiler_params=pltpu.CompilerParams(vmem_limit_bytes=30 << 20),
        cost_estimate=cost(10 * count * width * units, 2 * width * (3 * units + 4 * count)),
        name="experts_first",
    )(*grads_both, down, gate, up, *inputs_both)


def side_by_side(pieces):
    micro, copies, tokens, columns = pieces.shape

    def kernel(pieces_ref, out_ref):
        for c in range(copies):
            out_ref[:, :, c * columns : (c + 1) * columns] = pieces_ref[:, c]

    return pl.pallas_call(
        kernel,
        out_shape=jax.ShapeDtypeStruct((micro, tokens, copies * columns), pieces.dtype),
        compiler_params=pltpu.CompilerParams(vmem_limit_bytes=8 << 20),
        name="side_by_side",
    )(pieces)


def shards(saved_inputs, top_grad, routes, mix_weights, w_gate, w_up, w_down, q_prev):
    sections = lax.axis_size("pipe")
    last = lax.axis_index("pipe") == sections - 1
    peers = lax.axis_size("expert")
    expert_index = lax.axis_index("expert")
    replicas = lax.axis_size("dp")
    dp_index = lax.axis_index("dp")
    gate, up, down = (w_gate[0, 0, 0], w_up[0, 0, 0], w_down[0, 0, 0])
    right = q_prev[0, 0, 0].transpose(0, 2, 1)
    copies = peers // EXPERTS
    tokens = saved_inputs.shape[2]
    rows = MICRO * tokens
    slots = MICRO * CAP
    columns = D // copies
    major, minor = (expert_index // copies, expert_index % copies)

    own_inputs = saved_inputs[0].reshape(rows, D)
    top_rows = top_grad.reshape(rows, D)
    rank = slots_of(routes[0])
    part_ids = lax.dynamic_index_in_dim(routes[0] * CAP + rank, major, 0, keepdims=False)
    first, second = hit_table(part_ids, EXPERTS * CAP)
    deal_pick = (first | second).astype(BF)
    part_pick = deal_pick.reshape(EXPERTS, CAP, tokens).transpose(0, 2, 1)

    routes_by_choice = routes[0].transpose(0, 2, 1)
    own_slots = pick_slots(major, routes_by_choice, own_inputs)
    inputs_both = (own_slots, swap_cores(own_slots))
    own_grads, slot_weights = pick_slots(
        major, routes_by_choice, top_rows, mix_weights[0].transpose(0, 2, 1)
    )
    gate_first, up_first = fetch((gate, up))
    *forward, own_half, other_half, inputs = experts(
        gate_first, up_first, down, (own_grads, swap_cores(own_grads)), copies, inputs_both=inputs_both
    )

    def reduced(own_half, other_half, base, targets):
        other = swap_cores(other_half)
        mine = (own_half + other.astype(F32)).astype(BF)
        pieces = exchange(mine.reshape(peers, CAP, columns))
        return combine(
            pieces.reshape(EXPERTS, copies, CAP, columns), part_pick, base, targets
        )

    top_part = lax.dynamic_slice(
        top_grad, (major, 0, minor * columns), (1, tokens, columns)
    ).reshape(tokens, columns)
    part = reduced(own_half, other_half, top_part, 1)[0]
    incoming = lax.ppermute(part, "pipe", [(i, i - 1) for i in range(1, sections)])
    base, pieces = deal(last, top_part, incoming, deal_pick, copies)
    own_rows = exchange(pieces.reshape(peers, CAP, columns))
    own_grads = scale_rows(own_rows.reshape(MICRO, copies, CAP, columns), slot_weights)
    sums, grad_gate, grad_up, grad_rows = expert_slopes(
        down, (own_grads, swap_cores(own_grads)), forward, right
    )
    other_sums = swap_cores(sums)
    own_half, other_half, grads = expert_rows(
        gate, up, grad_gate, grad_up, forward[2], copies
    )
    parts = reduced(own_half, other_half, base, peers)
    produced = exchange(parts)
    produced = side_by_side(produced.reshape(MICRO, copies, tokens, columns))

    sums = sums.astype(F32) + jnp.concatenate([other_sums[slots:], other_sums[:slots]]).astype(F32)
    sums = add_copies(sums, copies)
    squares = (
        times(inputs, inputs, 1, 1),
        times(grad_rows, inputs, 1, 1),
        times(grad_rows, grad_rows, 1, 1),
    )
    q_next, basis = finish(
        dp_index,
        sums,
        squares,
        (inputs, grad_rows),
        grads,
        replicas * rows,
    )
    return (
        produced.reshape(1, MICRO, tokens, D),
        basis.T[None, None, None],
        q_next.transpose(0, 2, 1)[None, None, None],
    )


def solution(mesh):
    placed = (
        P("pipe", None, "dp", None),
        P(None, "dp", None),
        P("pipe", None, "dp", None),
        P("pipe", None, "dp", None),
        P("pipe", "expert", None, None, "dp"),
        P("pipe", "expert", None, None, "dp"),
        P("pipe", "expert", None, "dp", None),
        P("pipe", "expert", None, None, "dp", None),
    )
    return jax.shard_map(
        shards,
        mesh=mesh,
        in_specs=placed,
        out_specs=(
            P("pipe", None, "dp", None),
            P("pipe", "expert", None, "dp", None),
            P("pipe", "expert", None, None, "dp", None),
        ),
        check_vma=False,
    )
```

```python
import math

import jax
import jax.numpy as jnp
from jax import lax
from jax.experimental import pallas as pl
from jax.experimental.pallas import tpu as pltpu
from jax.sharding import PartitionSpec as P

D = 3072
EXPERTS = 4
R = 64
MICRO = 4
CAP = 48

BF = jnp.bfloat16
F32 = jnp.float32
IN_SMEM = pl.BlockSpec(memory_space=pltpu.SMEM)
IN_VMEM = pl.BlockSpec(memory_space=pltpu.VMEM)
IN_HBM = pl.BlockSpec(memory_space=pltpu.HBM)


def cost(flops, moved):
    return pl.CostEstimate(flops=int(flops), bytes_accessed=int(moved), transcendentals=0)


def swap_cores(value):
    return lax.ppermute(value, "dp", [(0, 1), (1, 0)])


def exchange(pieces):
    return lax.all_to_all(pieces, "expert", 0, 0, tiled=True)


def times(a, b, ca=1, cb=0, precision=None):
    return lax.dot_general(
        a, b, (((ca,), (cb,)), ((), ())), preferred_element_type=F32, precision=precision
    )


def slots_of(route_rows):
    flat = route_rows.reshape(MICRO, -1)
    count = flat.shape[1]
    earlier = lax.broadcasted_iota(jnp.int32, (count, count), 1) < lax.broadcasted_iota(
        jnp.int32, (count, count), 0
    )
    same = (flat[:, :, None] == flat[:, None, :]) & earlier[None]
    return jnp.sum(same.astype(jnp.int32), axis=2).reshape(route_rows.shape)


def hit_table(ids, count):
    rows = lax.broadcasted_iota(jnp.int32, (count, ids.shape[0]), 0)
    return rows == ids[None, :, 0], rows == ids[None, :, 1]


def add_copies(values, copies):
    def x_pair(i):
        return i ^ 1

    def y_pair(i):
        return i ^ 2

    def y_cross(i):
        y = i // 2 % 4
        return i + (((3 - y) % 4) - y) * 2

    for partner in (x_pair, y_pair, y_cross):
        route = [(i, partner(i)) for i in range(copies * EXPERTS)]
        rounded = values.astype(BF)
        other = lax.ppermute(rounded, "expert", route)
        values = rounded.astype(F32) + other.astype(F32)
    return rounded, other


def inverse_lower(gram):
    height = 8
    lanes = lax.broadcasted_iota(jnp.int32, (height, 2 * R), 1)
    depth = lax.broadcasted_iota(jnp.int32, (height, 2 * R), 0)
    blocks = []
    for b in range(R // height):
        rows = gram[b * height : (b + 1) * height, :]
        held = jnp.concatenate([jnp.zeros((height, R), F32), rows], 1)
        blocks.append(jnp.where(lanes == depth + b * height, 1.0, held))
    for k in range(R):
        at, row = divmod(k, height)
        pivot_row = blocks[at][row : row + 1, :]
        pivot_row = pivot_row * (1.0 / pivot_row[:, R + k : R + k + 1])
        for b in range((k + 1) // height, R // height):
            below = blocks[b] - blocks[b][:, R + k : R + k + 1] * pivot_row
            blocks[b] = jnp.where(depth + b * height > k, below, blocks[b]) if b == at else below
    for b in range(R // height):
        diagonal = jnp.where(lanes == depth + R + b * height, blocks[b], 0.0)
        pivots = jnp.sum(diagonal, axis=1, keepdims=True)
        blocks[b] = (blocks[b] * lax.rsqrt(pivots))[:, :R]
    return jnp.concatenate(blocks, axis=0)


def halves(value):
    high = value.astype(BF)
    return high, (value - high.astype(F32)).astype(BF)


def finish(dp_index, sums, squares, rows16, grads, token_total):
    count, wide = rows16[0].shape
    half = wide // 2
    units = grads.shape[2]

    def kernel(dp_ref, sums_ref, others_ref, *refs):
        squares_hbm, rows_hbm, grads_hbm = (refs[:3], refs[3:5], refs[5])
        q_ref, basis_ref, squares_ref, rows_ref, grads_ref, done = refs[6:]
        start = pl.multiple_of(dp_ref[0] * half, half)
        moves = [
            pltpu.make_async_copy(squares_hbm[i], squares_ref.at[i], done.at[i]) for i in range(3)
        ]
        moves.append(pltpu.make_async_copy(grads_hbm, grads_ref, done.at[3]))
        moves += [
            pltpu.make_async_copy(
                rows_hbm[i].at[:, pl.ds(start, half)],
                rows_ref.at[pl.ds(i * count, count)],
                done.at[4 + i],
            )
            for i in range(2)
        ]
        for move in moves:
            move.start()
        turned = (sums_ref[...].astype(F32) + others_ref[...].astype(F32)).T
        of_inputs, of_grads = (turned[:R].astype(BF), turned[R:].astype(BF))
        for move in moves[:3]:
            move.wait()

        def twice(left, right, cb):
            high, low = halves(right)
            return times(left, high, 1, cb) + times(left, low, 1, cb)

        inputs_inputs, grads_inputs, grads_grads = (squares_ref[i] for i in range(3))
        along_inputs = twice(of_inputs, inputs_inputs, 0) + twice(of_grads, grads_inputs, 0)
        along_grads = twice(of_inputs, grads_inputs, 1) + twice(of_grads, grads_grads, 0)
        gram = twice(of_inputs, along_inputs, 1) + twice(of_grads, along_grads, 1)
        inverse = inverse_lower(0.5 * (gram + gram.T))
        exact = lax.Precision.HIGHEST
        weights = jnp.concatenate(
            [
                times(inverse, of_inputs.astype(F32), 1, 0, exact),
                times(inverse, of_grads.astype(F32), 1, 0, exact),
            ],
            axis=1,
        ).astype(BF)
        scale = 1.0 / math.sqrt(float(token_total))
        along_inputs = times(inverse, along_inputs, 1, 0, exact).astype(BF)
        along_grads = times(inverse, along_grads, 1, 0, exact).astype(BF)
        for move in moves[3:]:
            move.wait()
        q_ref[0] = times(along_inputs, grads_ref[0]) * scale
        q_ref[1] = times(along_inputs, grads_ref[1]) * scale
        q_ref[2] = times(along_grads, grads_ref[2]) * scale
        basis_ref[...] = times(weights, rows_ref[...]) * math.sqrt(float(wide))

    return pl.pallas_call(
        kernel,
        out_shape=(
            jax.ShapeDtypeStruct((3, R, units), F32),
            jax.ShapeDtypeStruct((R, half), F32),
        ),
        in_specs=[IN_SMEM, IN_VMEM, IN_VMEM] + [IN_HBM] * 6,
        scratch_shapes=[
            pltpu.VMEM((3, count, count), F32),
            pltpu.VMEM((2 * count, half), BF),
            pltpu.VMEM((3, count, units), BF),
            pltpu.SemaphoreType.DMA((6,)),
        ],
        compiler_params=pltpu.CompilerParams(vmem_limit_bytes=61 << 20),
        cost_estimate=cost(4 * R * count * wide, 2 * count * (wide + 3 * units) + 12 * count**2),
        name="finish",
    )(dp_index.reshape(1), *sums, *squares, *rows16, grads)


def pick_slots(own_expert, routes, values, mix=None):
    micro, _, tokens = routes.shape
    width = values.shape[1]
    block = width // 4
    count = micro * CAP
    weighted = mix is not None

    def kernel(expert_ref, routes_ref, *refs):
        values_ref, slots_ref = (refs[weighted], refs[weighted + 1])
        expert = expert_ref[0]
        filler = jnp.zeros((8 - micro, tokens), F32)
        first = routes_ref[:, 0, :] == expert
        second = routes_ref[:, 1, :] == expert
        hit = jnp.where(first | second, 1.0, 0.0)
        earlier = lax.broadcasted_iota(jnp.int32, (tokens, tokens), 0) < lax.broadcasted_iota(
            jnp.int32, (tokens, tokens), 1
        )
        counted = jnp.concatenate([hit, filler]).astype(BF)
        rank = times(counted, jnp.where(earlier, 1.0, 0.0).astype(BF))[:micro]
        base = lax.broadcasted_iota(jnp.int32, (micro, tokens), 0).astype(F32) * CAP
        place = jnp.where(hit > 0.0, rank + base, -1.0)
        place = jnp.concatenate([place[m : m + 1] for m in range(micro)], axis=1)
        slot = lax.broadcasted_iota(jnp.int32, (count, micro * tokens), 0).astype(F32)
        chosen = slot == place
        pick = jnp.where(chosen, 1.0, 0.0).astype(BF)
        by_slot = 1.0
        if weighted:
            mix_ref, w_ref = (refs[0], refs[3])
            weight = jnp.where(first, mix_ref[:, 0, :], 0.0)
            weight = weight + jnp.where(second, mix_ref[:, 1, :], 0.0)
            weight = jnp.concatenate([weight[m : m + 1] for m in range(micro)], axis=1)
            by_slot = jnp.sum(jnp.where(chosen, weight, 0.0), axis=1, keepdims=True)
            w_ref[...] = jnp.broadcast_to(by_slot, (count, 128))
        for at in range(0, width, block):
            held = pl.ds(at, block)
            slots_ref[:, held] = (by_slot * times(pick, values_ref[:, held])).astype(BF)

    slots_shape = jax.ShapeDtypeStruct((count, width), BF)
    operands = (own_expert.reshape(1), routes, *([mix] if weighted else []), values)
    return pl.pallas_call(
        kernel,
        out_shape=(slots_shape, jax.ShapeDtypeStruct((count, 128), F32))
        if weighted
        else slots_shape,
        in_specs=[IN_SMEM] + [IN_VMEM] * (len(operands) - 1),
        compiler_params=pltpu.CompilerParams(vmem_limit_bytes=12 << 20),
        cost_estimate=cost(2 * count * micro * tokens * width, 2 * (count + micro * tokens) * width),
        name="pick_weighted" if weighted else "pick_slots",
    )(*operands)


def scale_rows(pieces, slot_weights):
    micro, copies, cap, columns = pieces.shape

    def kernel(pieces_ref, w_ref, out_ref):
        for m in range(micro):
            held = pl.ds(m * cap, cap)
            weight = w_ref[held, :1]
            for c in range(copies):
                scaled = weight * pieces_ref[m, c].astype(F32)
                out_ref[held, c * columns : (c + 1) * columns] = scaled.astype(BF)

    return pl.pallas_call(
        kernel,
        out_shape=jax.ShapeDtypeStruct((micro * cap, copies * columns), BF),
        compiler_params=pltpu.CompilerParams(vmem_limit_bytes=8 << 20),
        cost_estimate=cost(0, 8 * micro * cap * copies * columns),
        name="scale_rows",
    )(pieces, slot_weights)


def combine(pieces, pick, base, peers):
    experts_count, copies, _, columns = pieces.shape
    tokens = base.shape[0]

    def kernel(pieces_hbm, pick_ref, base_ref, out_hbm, pieces_ref, part_ref, arrived, sent):
        arrivals = [
            pltpu.make_async_copy(pieces_hbm.at[e], pieces_ref.at[e], arrived.at[e])
            for e in range(experts_count)
        ]
        for arrival in arrivals:
            arrival.start()
        share = base_ref[...].astype(F32)
        for e in range(experts_count):
            arrivals[e].wait()
            total = pieces_ref[e, 0].astype(F32)
            for c in range(1, copies):
                total = total + pieces_ref[e, c].astype(F32)
            for term in halves(total):
                share = share + times(pick_ref[e], term)
        part_ref[...] = share.astype(BF)
        sends = [
            pltpu.make_async_copy(part_ref, out_hbm.at[peer], sent.at[peer])
            for peer in range(peers)
        ]
        for send in sends:
            send.start()
        for send in sends:
            send.wait()

    return pl.pallas_call(
        kernel,
        out_shape=jax.ShapeDtypeStruct((peers, tokens, columns), BF),
        in_specs=[IN_HBM, IN_VMEM, IN_VMEM],
        out_specs=IN_HBM,
        scratch_shapes=[
            pltpu.VMEM(pieces.shape, BF),
            pltpu.VMEM((tokens, columns), BF),
            pltpu.SemaphoreType.DMA((experts_count,)),
            pltpu.SemaphoreType.DMA((peers,)),
        ],
        compiler_params=pltpu.CompilerParams(vmem_limit_bytes=61 << 20),
        name="combine",
    )(pieces, pick, base)


def deal(last, top_part, incoming, pick, copies):
    tokens, columns = incoming.shape
    slots = pick.shape[0]
    cap = slots // EXPERTS

    def kernel(last_ref, top_ref, incoming_ref, pick_ref, base_ref, out_ref):
        base = jnp.where(last_ref[0] == 1, top_ref[...].astype(F32), incoming_ref[...].astype(F32))
        base = base.astype(BF)
        base_ref[...] = base
        listed = times(pick_ref[...], base).astype(BF)
        for e in range(EXPERTS):
            for c in range(copies):
                out_ref[e, c] = listed[e * cap : (e + 1) * cap]

    return pl.pallas_call(
        kernel,
        out_shape=(
            jax.ShapeDtypeStruct((tokens, columns), BF),
            jax.ShapeDtypeStruct((EXPERTS, copies, cap, columns), BF),
        ),
        in_specs=[IN_SMEM] + [IN_VMEM] * 3,
        compiler_params=pltpu.CompilerParams(vmem_limit_bytes=8 << 20),
        cost_estimate=cost(2 * slots * tokens * columns, 60 << 20),
        name="deal",
    )(last.astype(jnp.int32).reshape(1), top_part, incoming, pick)


def fetch(arrays):
    count = len(arrays)

    def kernel(*refs):
        done = refs[-1]
        moves = [
            pltpu.make_async_copy(refs[i], refs[count + i], done.at[i]) for i in range(count)
        ]
        for move in moves:
            move.start()
        for move in moves:
            move.wait()

    return pl.pallas_call(
        kernel,
        out_shape=tuple(jax.ShapeDtypeStruct(a.shape, a.dtype) for a in arrays),
        in_specs=[IN_HBM] * count,
        out_specs=(IN_VMEM,) * count,
        scratch_shapes=[pltpu.SemaphoreType.DMA((count,))],
        compiler_params=pltpu.CompilerParams(vmem_limit_bytes=12 << 20),
    )(*arrays)


def expert_slopes(down, grads_both, forward, right):
    slots, width = grads_both[0].shape
    count = 2 * slots
    units = right.shape[2]
    square = (count, units)

    def kernel(*refs):
        own_ref, partner_ref, down_ref, slope_ref, silu_ref, hidden_ref, right_ref = refs[:7]
        sums_ref, gg_ref, gu_ref, rows_hbm, done = refs[7:]
        moves = []

        def keep(source, target):
            move = pltpu.make_async_copy(source, target, done.at[len(moves)])
            move.start()
            moves.append(move)

        keep(own_ref, rows_hbm.at[pl.ds(0, slots)])
        keep(partner_ref, rows_hbm.at[pl.ds(slots, slots)])
        rows = jnp.concatenate([own_ref[...], partner_ref[...]])
        grad_hidden = times(rows, down_ref[...], 1, 1)
        gg_ref[...] = (grad_hidden * slope_ref[...]).astype(BF)
        gu_ref[...] = (grad_hidden * silu_ref[...]).astype(BF)
        right16 = right_ref[...].astype(BF)
        of_inputs = times(gg_ref[...], right16[0], 1, 1) + times(gu_ref[...], right16[1], 1, 1)
        of_grads = times(hidden_ref[...], right16[2], 1, 1)
        sums_ref[...] = jnp.concatenate([of_inputs, of_grads], axis=1).astype(BF)
        for move in moves:
            move.wait()

    return pl.pallas_call(
        kernel,
        out_shape=(
            jax.ShapeDtypeStruct((count, 2 * R), BF),
            jax.ShapeDtypeStruct(square, BF),
            jax.ShapeDtypeStruct(square, BF),
            jax.ShapeDtypeStruct((count, width), BF),
        ),
        in_specs=[IN_VMEM] * 7,
        out_specs=(*[IN_VMEM] * 3, IN_HBM),
        scratch_shapes=[pltpu.SemaphoreType.DMA((2,))],
        compiler_params=pltpu.CompilerParams(vmem_limit_bytes=20 << 20),
        cost_estimate=cost(
            2 * count * width * units, 2 * width * (units + 2 * count) + 12 * count * units
        ),
        name="expert_slopes",
    )(*grads_both, down, *forward, right)


def expert_rows(gate, up, grad_gate, grad_up, hidden, copies):
    width, units = gate.shape
    count = grad_gate.shape[0]
    slots = count // 2
    columns = width // copies
    shape = (MICRO, copies, CAP, columns)

    def kernel(gg_ref, gu_ref, hidden_ref, gate_ref, up_ref, own_ref, par_ref, grads_hbm, done):
        moves = [
            pltpu.make_async_copy(source, grads_hbm.at[i], done.at[i])
            for i, source in enumerate((gg_ref, gu_ref, hidden_ref))
        ]
        for move in moves:
            move.start()

        def column(c, carry):
            held = pl.ds(pl.multiple_of(c * columns, columns), columns)
            total = times(gg_ref[...], gate_ref[held, :], 1, 1)
            total = total + times(gu_ref[...], up_ref[held, :], 1, 1)
            for m in range(MICRO):
                own_ref[m, c] = total[m * CAP : (m + 1) * CAP]
                par_ref[m, c] = total[slots + m * CAP : slots + (m + 1) * CAP].astype(BF)
            return carry

        lax.fori_loop(0, copies, column, 0)
        for move in moves:
            move.wait()

    return pl.pallas_call(
        kernel,
        out_shape=(
            jax.ShapeDtypeStruct(shape, F32),
            jax.ShapeDtypeStruct(shape, BF),
            jax.ShapeDtypeStruct((3, count, units), BF),
        ),
        in_specs=[IN_VMEM] * 5,
        out_specs=(IN_VMEM, IN_VMEM, IN_HBM),
        scratch_shapes=[pltpu.SemaphoreType.DMA((3,))],
        compiler_params=pltpu.CompilerParams(vmem_limit_bytes=24 << 20),
        cost_estimate=cost(4 * count * width * units, 4 * width * units + 6 * count * width),
        name="expert_rows",
    )(grad_gate, grad_up, hidden, gate, up)


def experts(gate, up, down, grads_both, copies, inputs_both):
    slots, width = grads_both[0].shape
    count = 2 * slots
    units = gate.shape[1]
    columns = width // copies
    halves_shape = (MICRO, copies, CAP, columns)
    square = (count, units)
    made = [(square, F32), (square, F32), (square, BF), (halves_shape, F32), (halves_shape, BF)]

    def kernel(*refs):
        grads_refs, (down_ref, gate_ref, up_ref), rows_refs = (refs[:2], refs[2:5], refs[5:7])
        slope_ref, silu_ref, hidden_ref, own_ref, par_ref, rows_hbm = refs[7:13]
        gg_ref, gu_ref, done = refs[13:]
        moves = [
            pltpu.make_async_copy(rows_refs[i], rows_hbm.at[pl.ds(i * slots, slots)], done.at[i])
            for i in range(2)
        ]
        for move in moves:
            move.start()

        def both(pair):
            return jnp.concatenate([pair[0][...], pair[1][...]])

        inputs = both(rows_refs)
        pre_gate = times(inputs, gate_ref[...])
        pre_up = times(inputs, up_ref[...])
        sigmoid = 1.0 / (1.0 + jnp.exp(-pre_gate))
        silu = pre_gate * sigmoid
        slope_ref[...] = pre_up * sigmoid * (1.0 + pre_gate * (1.0 - sigmoid))
        silu_ref[...] = silu
        hidden_ref[...] = (silu * pre_up).astype(BF)
        grad_hidden = times(both(grads_refs), down_ref[...], 1, 1)
        gg_ref[...] = (grad_hidden * slope_ref[...]).astype(BF)
        gu_ref[...] = (grad_hidden * silu_ref[...]).astype(BF)

        def column(c, carry):
            held = pl.ds(pl.multiple_of(c * columns, columns), columns)
            total = times(gg_ref[...], gate_ref[held, :], 1, 1)
            total = total + times(gu_ref[...], up_ref[held, :], 1, 1)
            for m in range(MICRO):
                own_ref[m, c] = total[m * CAP : (m + 1) * CAP]
                par_ref[m, c] = total[slots + m * CAP : slots + (m + 1) * CAP].astype(BF)
            return carry

        lax.fori_loop(0, copies, column, 0)
        for move in moves:
            move.wait()

    return pl.pallas_call(
        kernel,
        out_shape=(
            *[jax.ShapeDtypeStruct(*result) for result in made],
            jax.ShapeDtypeStruct((count, width), BF),
        ),
        in_specs=[IN_VMEM] * 7,
        out_specs=(*[IN_VMEM] * 5, IN_HBM),
        scratch_shapes=[
            pltpu.VMEM(square, BF),
            pltpu.VMEM(square, BF),
            pltpu.SemaphoreType.DMA((2,)),
        ],
        compiler_params=pltpu.CompilerParams(vmem_limit_bytes=30 << 20),
        cost_estimate=cost(10 * count * width * units, 2 * width * (3 * units + 4 * count)),
        name="experts_first",
    )(*grads_both, down, gate, up, *inputs_both)


def side_by_side(pieces):
    micro, copies, tokens, columns = pieces.shape

    def kernel(pieces_ref, out_ref):
        for c in range(copies):
            out_ref[:, :, c * columns : (c + 1) * columns] = pieces_ref[:, c]

    return pl.pallas_call(
        kernel,
        out_shape=jax.ShapeDtypeStruct((micro, tokens, copies * columns), pieces.dtype),
        compiler_params=pltpu.CompilerParams(vmem_limit_bytes=8 << 20),
        name="side_by_side",
    )(pieces)


def shards(saved_inputs, top_grad, routes, mix_weights, w_gate, w_up, w_down, q_prev):
    sections = lax.axis_size("pipe")
    last = lax.axis_index("pipe") == sections - 1
    peers = lax.axis_size("expert")
    expert_index = lax.axis_index("expert")
    replicas = lax.axis_size("dp")
    dp_index = lax.axis_index("dp")
    gate, up, down = (w_gate[0, 0, 0], w_up[0, 0, 0], w_down[0, 0, 0])
    right = q_prev[0, 0, 0].transpose(0, 2, 1)
    copies = peers // EXPERTS
    tokens = saved_inputs.shape[2]
    rows = MICRO * tokens
    slots = MICRO * CAP
    columns = D // copies
    major, minor = (expert_index // copies, expert_index % copies)

    own_inputs = saved_inputs[0].reshape(rows, D)
    top_rows = top_grad.reshape(rows, D)
    rank = slots_of(routes[0])
    part_ids = lax.dynamic_index_in_dim(routes[0] * CAP + rank, major, 0, keepdims=False)
    first, second = hit_table(part_ids, EXPERTS * CAP)
    deal_pick = (first | second).astype(BF)
    part_pick = deal_pick.reshape(EXPERTS, CAP, tokens).transpose(0, 2, 1)

    routes_by_choice = routes[0].transpose(0, 2, 1)
    own_slots = pick_slots(major, routes_by_choice, own_inputs)
    inputs_both = (own_slots, swap_cores(own_slots))
    own_grads, slot_weights = pick_slots(
        major, routes_by_choice, top_rows, mix_weights[0].transpose(0, 2, 1)
    )
    gate_first, up_first = fetch((gate, up))
    *forward, own_half, other_half, inputs = experts(
        gate_first, up_first, down, (own_grads, swap_cores(own_grads)), copies, inputs_both=inputs_both
    )

    def reduced(own_half, other_half, base, targets):
        other = swap_cores(other_half)
        mine = (own_half + other.astype(F32)).astype(BF)
        pieces = exchange(mine.reshape(peers, CAP, columns))
        return combine(
            pieces.reshape(EXPERTS, copies, CAP, columns), part_pick, base, targets
        )

    top_part = lax.dynamic_slice(
        top_grad, (major, 0, minor * columns), (1, tokens, columns)
    ).reshape(tokens, columns)
    part = reduced(own_half, other_half, top_part, 1)[0]
    incoming = lax.ppermute(part, "pipe", [(i, i - 1) for i in range(1, sections)])
    base, pieces = deal(last, top_part, incoming, deal_pick, copies)
    own_rows = exchange(pieces.reshape(peers, CAP, columns))
    own_grads = scale_rows(own_rows.reshape(MICRO, copies, CAP, columns), slot_weights)
    sums, grad_gate, grad_up, grad_rows = expert_slopes(
        down, (own_grads, swap_cores(own_grads)), forward, right
    )
    other_sums = swap_cores(sums)
    own_half, other_half, grads = expert_rows(
        gate, up, grad_gate, grad_up, forward[2], copies
    )
    parts = reduced(own_half, other_half, base, peers)
    produced = exchange(parts)
    produced = side_by_side(produced.reshape(MICRO, copies, tokens, columns))

    sums = sums.astype(F32) + jnp.concatenate([other_sums[slots:], other_sums[:slots]]).astype(F32)
    sums = add_copies(sums, copies)
    squares = (
        times(inputs, inputs, 1, 1),
        times(grad_rows, inputs, 1, 1),
        times(grad_rows, grad_rows, 1, 1),
    )
    q_next, basis = finish(
        dp_index,
        sums,
        squares,
        (inputs, grad_rows),
        grads,
        replicas * rows,
    )
    return (
        produced.reshape(1, MICRO, tokens, D),
        basis.T[None, None, None],
        q_next.transpose(0, 2, 1)[None, None, None],
    )


def solution(mesh):
    placed = (
        P("pipe", None, "dp", None),
        P(None, "dp", None),
        P("pipe", None, "dp", None),
        P("pipe", None, "dp", None),
        P("pipe", "expert", None, None, "dp"),
        P("pipe", "expert", None, None, "dp"),
        P("pipe", "expert", None, "dp", None),
        P("pipe", "expert", None, None, "dp", None),
    )
    return jax.shard_map(
        shards,
        mesh=mesh,
        in_specs=placed,
        out_specs=(
            P("pipe", None, "dp", None),
            P("pipe", "expert", None, "dp", None),
            P("pipe", "expert", None, None, "dp", None),
        ),
        check_vma=False,
    )
```

```python
import math

import jax
import jax.numpy as jnp
from jax import lax
from jax.experimental import pallas as pl
from jax.experimental.pallas import tpu as pltpu
from jax.sharding import PartitionSpec as P

D = 3072
EXPERTS = 4
R = 64
MICRO = 4
CAP = 48

BF = jnp.bfloat16
F32 = jnp.float32
IN_SMEM = pl.BlockSpec(memory_space=pltpu.SMEM)
IN_VMEM = pl.BlockSpec(memory_space=pltpu.VMEM)
IN_HBM = pl.BlockSpec(memory_space=pltpu.HBM)


def cost(flops, moved):
    return pl.CostEstimate(flops=int(flops), bytes_accessed=int(moved), transcendentals=0)


def swap_cores(value):
    return lax.ppermute(value, "dp", [(0, 1), (1, 0)])


def exchange(pieces):
    return lax.all_to_all(pieces, "expert", 0, 0, tiled=True)


def times(a, b, ca=1, cb=0, precision=None):
    return lax.dot_general(
        a, b, (((ca,), (cb,)), ((), ())), preferred_element_type=F32, precision=precision
    )


def slots_of(route_rows):
    flat = route_rows.reshape(MICRO, -1)
    count = flat.shape[1]
    earlier = lax.broadcasted_iota(jnp.int32, (count, count), 1) < lax.broadcasted_iota(
        jnp.int32, (count, count), 0
    )
    same = (flat[:, :, None] == flat[:, None, :]) & earlier[None]
    return jnp.sum(same.astype(jnp.int32), axis=2).reshape(route_rows.shape)


def hit_table(ids, count):
    rows = lax.broadcasted_iota(jnp.int32, (count, ids.shape[0]), 0)
    return rows == ids[None, :, 0], rows == ids[None, :, 1]


def add_copies(values, copies):
    def x_pair(i):
        return i ^ 1

    def y_pair(i):
        return i ^ 2

    def y_cross(i):
        y = i // 2 % 4
        return i + (((3 - y) % 4) - y) * 2

    for partner in (x_pair, y_pair, y_cross):
        route = [(i, partner(i)) for i in range(copies * EXPERTS)]
        rounded = values.astype(BF)
        other = lax.ppermute(rounded, "expert", route)
        values = rounded.astype(F32) + other.astype(F32)
    return rounded, other


def inverse_lower(gram):
    height = 8
    lanes = lax.broadcasted_iota(jnp.int32, (height, 2 * R), 1)
    depth = lax.broadcasted_iota(jnp.int32, (height, 2 * R), 0)
    blocks = []
    for b in range(R // height):
        rows = gram[b * height : (b + 1) * height, :]
        held = jnp.concatenate([jnp.zeros((height, R), F32), rows], 1)
        blocks.append(jnp.where(lanes == depth + b * height, 1.0, held))
    for k in range(R):
        at, row = divmod(k, height)
        pivot_row = blocks[at][row : row + 1, :]
        pivot_row = pivot_row * (1.0 / pivot_row[:, R + k : R + k + 1])
        for b in range((k + 1) // height, R // height):
            below = blocks[b] - blocks[b][:, R + k : R + k + 1] * pivot_row
            blocks[b] = jnp.where(depth + b * height > k, below, blocks[b]) if b == at else below
    for b in range(R // height):
        diagonal = jnp.where(lanes == depth + R + b * height, blocks[b], 0.0)
        pivots = jnp.sum(diagonal, axis=1, keepdims=True)
        blocks[b] = (blocks[b] * lax.rsqrt(pivots))[:, :R]
    return jnp.concatenate(blocks, axis=0)


def halves(value):
    high = value.astype(BF)
    return high, (value - high.astype(F32)).astype(BF)


def finish(dp_index, sums, squares, rows16, grads, token_total):
    count, wide = rows16[0].shape
    half = wide // 2
    units = grads.shape[2]

    def kernel(dp_ref, sums_ref, others_ref, *refs):
        squares_hbm, rows_hbm, grads_hbm = (refs[:3], refs[3:5], refs[5])
        q_ref, basis_ref, squares_ref, rows_ref, grads_ref, done = refs[6:]
        start = pl.multiple_of(dp_ref[0] * half, half)
        moves = [
            pltpu.make_async_copy(squares_hbm[i], squares_ref.at[i], done.at[i]) for i in range(3)
        ]
        moves.append(pltpu.make_async_copy(grads_hbm, grads_ref, done.at[3]))
        moves += [
            pltpu.make_async_copy(
                rows_hbm[i].at[:, pl.ds(start, half)],
                rows_ref.at[pl.ds(i * count, count)],
                done.at[4 + i],
            )
            for i in range(2)
        ]
        for move in moves:
            move.start()
        turned = (sums_ref[...].astype(F32) + others_ref[...].astype(F32)).T
        of_inputs, of_grads = (turned[:R].astype(BF), turned[R:].astype(BF))
        for move in moves[:3]:
            move.wait()

        def twice(left, right, cb):
            high, low = halves(right)
            return times(left, high, 1, cb) + times(left, low, 1, cb)

        inputs_inputs, grads_inputs, grads_grads = (squares_ref[i] for i in range(3))
        along_inputs = twice(of_inputs, inputs_inputs, 0) + twice(of_grads, grads_inputs, 0)
        along_grads = twice(of_inputs, grads_inputs, 1) + twice(of_grads, grads_grads, 0)
        gram = twice(of_inputs, along_inputs, 1) + twice(of_grads, along_grads, 1)
        inverse = inverse_lower(0.5 * (gram + gram.T))
        exact = lax.Precision.HIGHEST
        weights = jnp.concatenate(
            [
                times(inverse, of_inputs.astype(F32), 1, 0, exact),
                times(inverse, of_grads.astype(F32), 1, 0, exact),
            ],
            axis=1,
        ).astype(BF)
        scale = 1.0 / math.sqrt(float(token_total))
        along_inputs = times(inverse, along_inputs, 1, 0, exact).astype(BF)
        along_grads = times(inverse, along_grads, 1, 0, exact).astype(BF)
        for move in moves[3:]:
            move.wait()
        q_ref[0] = times(along_inputs, grads_ref[0]) * scale
        q_ref[1] = times(along_inputs, grads_ref[1]) * scale
        q_ref[2] = times(along_grads, grads_ref[2]) * scale
        basis_ref[...] = times(weights, rows_ref[...]) * math.sqrt(float(wide))

    return pl.pallas_call(
        kernel,
        out_shape=(
            jax.ShapeDtypeStruct((3, R, units), F32),
            jax.ShapeDtypeStruct((R, half), F32),
        ),
        in_specs=[IN_SMEM, IN_VMEM, IN_VMEM] + [IN_HBM] * 6,
        scratch_shapes=[
            pltpu.VMEM((3, count, count), F32),
            pltpu.VMEM((2 * count, half), BF),
            pltpu.VMEM((3, count, units), BF),
            pltpu.SemaphoreType.DMA((6,)),
        ],
        compiler_params=pltpu.CompilerParams(vmem_limit_bytes=61 << 20),
        cost_estimate=cost(4 * R * count * wide, 2 * count * (wide + 3 * units) + 12 * count**2),
        name="finish",
    )(dp_index.reshape(1), *sums, *squares, *rows16, grads)


def pick_slots(own_expert, routes, values, mix=None):
    micro, _, tokens = routes.shape
    width = values.shape[1]
    block = width // 4
    count = micro * CAP
    weighted = mix is not None

    def kernel(expert_ref, routes_ref, *refs):
        values_ref, slots_ref = (refs[weighted], refs[weighted + 1])
        expert = expert_ref[0]
        filler = jnp.zeros((8 - micro, tokens), F32)
        first = routes_ref[:, 0, :] == expert
        second = routes_ref[:, 1, :] == expert
        hit = jnp.where(first | second, 1.0, 0.0)
        earlier = lax.broadcasted_iota(jnp.int32, (tokens, tokens), 0) < lax.broadcasted_iota(
            jnp.int32, (tokens, tokens), 1
        )
        counted = jnp.concatenate([hit, filler]).astype(BF)
        rank = times(counted, jnp.where(earlier, 1.0, 0.0).astype(BF))[:micro]
        base = lax.broadcasted_iota(jnp.int32, (micro, tokens), 0).astype(F32) * CAP
        place = jnp.where(hit > 0.0, rank + base, -1.0)
        place = jnp.concatenate([place[m : m + 1] for m in range(micro)], axis=1)
        slot = lax.broadcasted_iota(jnp.int32, (count, micro * tokens), 0).astype(F32)
        chosen = slot == place
        pick = jnp.where(chosen, 1.0, 0.0).astype(BF)
        by_slot = 1.0
        if weighted:
            mix_ref, w_ref = (refs[0], refs[3])
            weight = jnp.where(first, mix_ref[:, 0, :], 0.0)
            weight = weight + jnp.where(second, mix_ref[:, 1, :], 0.0)
            weight = jnp.concatenate([weight[m : m + 1] for m in range(micro)], axis=1)
            by_slot = jnp.sum(jnp.where(chosen, weight, 0.0), axis=1, keepdims=True)
            w_ref[...] = jnp.broadcast_to(by_slot, (count, 128))
        for at in range(0, width, block):
            held = pl.ds(at, block)
            slots_ref[:, held] = (by_slot * times(pick, values_ref[:, held])).astype(BF)

    slots_shape = jax.ShapeDtypeStruct((count, width), BF)
    operands = (own_expert.reshape(1), routes, *([mix] if weighted else []), values)
    return pl.pallas_call(
        kernel,
        out_shape=(slots_shape, jax.ShapeDtypeStruct((count, 128), F32))
        if weighted
        else slots_shape,
        in_specs=[IN_SMEM] + [IN_VMEM] * (len(operands) - 1),
        compiler_params=pltpu.CompilerParams(vmem_limit_bytes=12 << 20),
        cost_estimate=cost(2 * count * micro * tokens * width, 2 * (count + micro * tokens) * width),
        name="pick_weighted" if weighted else "pick_slots",
    )(*operands)


def scale_rows(pieces, slot_weights):
    micro, copies, cap, columns = pieces.shape

    def kernel(pieces_ref, w_ref, out_ref):
        for m in range(micro):
            held = pl.ds(m * cap, cap)
            weight = w_ref[held, :1]
            for c in range(copies):
                scaled = weight * pieces_ref[m, c].astype(F32)
                out_ref[held, c * columns : (c + 1) * columns] = scaled.astype(BF)

    return pl.pallas_call(
        kernel,
        out_shape=jax.ShapeDtypeStruct((micro * cap, copies * columns), BF),
        compiler_params=pltpu.CompilerParams(vmem_limit_bytes=8 << 20),
        cost_estimate=cost(0, 8 * micro * cap * copies * columns),
        name="scale_rows",
    )(pieces, slot_weights)


def combine(pieces, pick, base, peers):
    experts_count, copies, _, columns = pieces.shape
    tokens = base.shape[0]

    def kernel(pieces_ref, pick_ref, base_ref, out_ref):
        share = base_ref[...].astype(F32)
        for e in range(experts_count):
            total = pieces_ref[e, 0].astype(F32)
            for c in range(1, copies):
                total = total + pieces_ref[e, c].astype(F32)
            for term in halves(total):
                share = share + times(pick_ref[e], term)
        part = share.astype(BF)
        for peer in range(peers):
            out_ref[peer] = part

    return pl.pallas_call(
        kernel,
        out_shape=jax.ShapeDtypeStruct((peers, tokens, columns), BF),
        compiler_params=pltpu.CompilerParams(vmem_limit_bytes=61 << 20),
        name="combine",
    )(pieces, pick, base)


def deal(last, top_part, incoming, pick, copies):
    tokens, columns = incoming.shape
    slots = pick.shape[0]
    cap = slots // EXPERTS

    def kernel(last_ref, top_ref, incoming_ref, pick_ref, base_ref, out_ref):
        base = jnp.where(last_ref[0] == 1, top_ref[...].astype(F32), incoming_ref[...].astype(F32))
        base = base.astype(BF)
        base_ref[...] = base
        listed = times(pick_ref[...], base).astype(BF)
        for e in range(EXPERTS):
            for c in range(copies):
                out_ref[e, c] = listed[e * cap : (e + 1) * cap]

    return pl.pallas_call(
        kernel,
        out_shape=(
            jax.ShapeDtypeStruct((tokens, columns), BF),
            jax.ShapeDtypeStruct((EXPERTS, copies, cap, columns), BF),
        ),
        in_specs=[IN_SMEM] + [IN_VMEM] * 3,
        compiler_params=pltpu.CompilerParams(vmem_limit_bytes=8 << 20),
        cost_estimate=cost(2 * slots * tokens * columns, 60 << 20),
        name="deal",
    )(last.astype(jnp.int32).reshape(1), top_part, incoming, pick)


def fetch(arrays):
    count = len(arrays)

    def kernel(*refs):
        done = refs[-1]
        moves = [
            pltpu.make_async_copy(refs[i], refs[count + i], done.at[i]) for i in range(count)
        ]
        for move in moves:
            move.start()
        for move in moves:
            move.wait()

    return pl.pallas_call(
        kernel,
        out_shape=tuple(jax.ShapeDtypeStruct(a.shape, a.dtype) for a in arrays),
        in_specs=[IN_HBM] * count,
        out_specs=(IN_VMEM,) * count,
        scratch_shapes=[pltpu.SemaphoreType.DMA((count,))],
        compiler_params=pltpu.CompilerParams(vmem_limit_bytes=12 << 20),
    )(*arrays)


def expert_slopes(down, grads_both, forward, right):
    slots, width = grads_both[0].shape
    count = 2 * slots
    units = right.shape[2]
    square = (count, units)

    def kernel(*refs):
        own_ref, partner_ref, down_ref, slope_ref, silu_ref, hidden_ref, right_ref = refs[:7]
        sums_ref, gg_ref, gu_ref, rows_hbm, done = refs[7:]
        moves = []

        def keep(source, target):
            move = pltpu.make_async_copy(source, target, done.at[len(moves)])
            move.start()
            moves.append(move)

        keep(own_ref, rows_hbm.at[pl.ds(0, slots)])
        keep(partner_ref, rows_hbm.at[pl.ds(slots, slots)])
        rows = jnp.concatenate([own_ref[...], partner_ref[...]])
        grad_hidden = times(rows, down_ref[...], 1, 1)
        gg_ref[...] = (grad_hidden * slope_ref[...]).astype(BF)
        gu_ref[...] = (grad_hidden * silu_ref[...]).astype(BF)
        right16 = right_ref[...].astype(BF)
        of_inputs = times(gg_ref[...], right16[0], 1, 1) + times(gu_ref[...], right16[1], 1, 1)
        of_grads = times(hidden_ref[...], right16[2], 1, 1)
        sums_ref[...] = jnp.concatenate([of_inputs, of_grads], axis=1).astype(BF)
        for move in moves:
            move.wait()

    return pl.pallas_call(
        kernel,
        out_shape=(
            jax.ShapeDtypeStruct((count, 2 * R), BF),
            jax.ShapeDtypeStruct(square, BF),
            jax.ShapeDtypeStruct(square, BF),
            jax.ShapeDtypeStruct((count, width), BF),
        ),
        in_specs=[IN_VMEM] * 7,
        out_specs=(*[IN_VMEM] * 3, IN_HBM),
        scratch_shapes=[pltpu.SemaphoreType.DMA((2,))],
        compiler_params=pltpu.CompilerParams(vmem_limit_bytes=20 << 20),
        cost_estimate=cost(
            2 * count * width * units, 2 * width * (units + 2 * count) + 12 * count * units
        ),
        name="expert_slopes",
    )(*grads_both, down, *forward, right)


def expert_rows(gate, up, grad_gate, grad_up, hidden, copies):
    width, units = gate.shape
    count = grad_gate.shape[0]
    slots = count // 2
    columns = width // copies
    shape = (MICRO, copies, CAP, columns)

    def kernel(gg_ref, gu_ref, hidden_ref, gate_ref, up_ref, own_ref, par_ref, grads_hbm, done):
        moves = [
            pltpu.make_async_copy(source, grads_hbm.at[i], done.at[i])
            for i, source in enumerate((gg_ref, gu_ref, hidden_ref))
        ]
        for move in moves:
            move.start()

        def column(c, carry):
            held = pl.ds(pl.multiple_of(c * columns, columns), columns)
            total = times(gg_ref[...], gate_ref[held, :], 1, 1)
            total = total + times(gu_ref[...], up_ref[held, :], 1, 1)
            for m in range(MICRO):
                own_ref[m, c] = total[m * CAP : (m + 1) * CAP]
                par_ref[m, c] = total[slots + m * CAP : slots + (m + 1) * CAP].astype(BF)
            return carry

        lax.fori_loop(0, copies, column, 0)
        for move in moves:
            move.wait()

    return pl.pallas_call(
        kernel,
        out_shape=(
            jax.ShapeDtypeStruct(shape, F32),
            jax.ShapeDtypeStruct(shape, BF),
            jax.ShapeDtypeStruct((3, count, units), BF),
        ),
        in_specs=[IN_VMEM] * 5,
        out_specs=(IN_VMEM, IN_VMEM, IN_HBM),
        scratch_shapes=[pltpu.SemaphoreType.DMA((3,))],
        compiler_params=pltpu.CompilerParams(vmem_limit_bytes=24 << 20),
        cost_estimate=cost(4 * count * width * units, 4 * width * units + 6 * count * width),
        name="expert_rows",
    )(grad_gate, grad_up, hidden, gate, up)


def experts(gate, up, down, grads_both, copies, inputs_both):
    slots, width = grads_both[0].shape
    count = 2 * slots
    units = gate.shape[1]
    columns = width // copies
    halves_shape = (MICRO, copies, CAP, columns)
    square = (count, units)
    made = [(square, F32), (square, F32), (square, BF), (halves_shape, F32), (halves_shape, BF)]

    def kernel(*refs):
        grads_refs, (down_ref, gate_ref, up_ref), rows_refs = (refs[:2], refs[2:5], refs[5:7])
        slope_ref, silu_ref, hidden_ref, own_ref, par_ref, rows_hbm = refs[7:13]
        gg_ref, gu_ref, done = refs[13:]
        moves = [
            pltpu.make_async_copy(rows_refs[i], rows_hbm.at[pl.ds(i * slots, slots)], done.at[i])
            for i in range(2)
        ]
        for move in moves:
            move.start()

        def both(pair):
            return jnp.concatenate([pair[0][...], pair[1][...]])

        inputs = both(rows_refs)
        pre_gate = times(inputs, gate_ref[...])
        pre_up = times(inputs, up_ref[...])
        sigmoid = 1.0 / (1.0 + jnp.exp(-pre_gate))
        silu = pre_gate * sigmoid
        slope_ref[...] = pre_up * sigmoid * (1.0 + pre_gate * (1.0 - sigmoid))
        silu_ref[...] = silu
        hidden_ref[...] = (silu * pre_up).astype(BF)
        grad_hidden = times(both(grads_refs), down_ref[...], 1, 1)
        gg_ref[...] = (grad_hidden * slope_ref[...]).astype(BF)
        gu_ref[...] = (grad_hidden * silu_ref[...]).astype(BF)

        def column(c, carry):
            held = pl.ds(pl.multiple_of(c * columns, columns), columns)
            total = times(gg_ref[...], gate_ref[held, :], 1, 1)
            total = total + times(gu_ref[...], up_ref[held, :], 1, 1)
            for m in range(MICRO):
                own_ref[m, c] = total[m * CAP : (m + 1) * CAP]
                par_ref[m, c] = total[slots + m * CAP : slots + (m + 1) * CAP].astype(BF)
            return carry

        lax.fori_loop(0, copies, column, 0)
        for move in moves:
            move.wait()

    return pl.pallas_call(
        kernel,
        out_shape=(
            *[jax.ShapeDtypeStruct(*result) for result in made],
            jax.ShapeDtypeStruct((count, width), BF),
        ),
        in_specs=[IN_VMEM] * 7,
        out_specs=(*[IN_VMEM] * 5, IN_HBM),
        scratch_shapes=[
            pltpu.VMEM(square, BF),
            pltpu.VMEM(square, BF),
            pltpu.SemaphoreType.DMA((2,)),
        ],
        compiler_params=pltpu.CompilerParams(vmem_limit_bytes=30 << 20),
        cost_estimate=cost(10 * count * width * units, 2 * width * (3 * units + 4 * count)),
        name="experts_first",
    )(*grads_both, down, gate, up, *inputs_both)


def side_by_side(pieces):
    micro, copies, tokens, columns = pieces.shape

    def kernel(pieces_ref, out_ref):
        for c in range(copies):
            out_ref[:, :, c * columns : (c + 1) * columns] = pieces_ref[:, c]

    return pl.pallas_call(
        kernel,
        out_shape=jax.ShapeDtypeStruct((micro, tokens, copies * columns), pieces.dtype),
        compiler_params=pltpu.CompilerParams(vmem_limit_bytes=8 << 20),
        name="side_by_side",
    )(pieces)


def shards(saved_inputs, top_grad, routes, mix_weights, w_gate, w_up, w_down, q_prev):
    sections = lax.axis_size("pipe")
    last = lax.axis_index("pipe") == sections - 1
    peers = lax.axis_size("expert")
    expert_index = lax.axis_index("expert")
    replicas = lax.axis_size("dp")
    dp_index = lax.axis_index("dp")
    gate, up, down = (w_gate[0, 0, 0], w_up[0, 0, 0], w_down[0, 0, 0])
    right = q_prev[0, 0, 0].transpose(0, 2, 1)
    copies = peers // EXPERTS
    tokens = saved_inputs.shape[2]
    rows = MICRO * tokens
    slots = MICRO * CAP
    columns = D // copies
    major, minor = (expert_index // copies, expert_index % copies)

    own_inputs = saved_inputs[0].reshape(rows, D)
    top_rows = top_grad.reshape(rows, D)
    rank = slots_of(routes[0])
    part_ids = lax.dynamic_index_in_dim(routes[0] * CAP + rank, major, 0, keepdims=False)
    first, second = hit_table(part_ids, EXPERTS * CAP)
    deal_pick = (first | second).astype(BF)
    part_pick = deal_pick.reshape(EXPERTS, CAP, tokens).transpose(0, 2, 1)

    routes_by_choice = routes[0].transpose(0, 2, 1)
    own_slots = pick_slots(major, routes_by_choice, own_inputs)
    inputs_both = (own_slots, swap_cores(own_slots))
    own_grads, slot_weights = pick_slots(
        major, routes_by_choice, top_rows, mix_weights[0].transpose(0, 2, 1)
    )
    gate_first, up_first = fetch((gate, up))
    *forward, own_half, other_half, inputs = experts(
        gate_first, up_first, down, (own_grads, swap_cores(own_grads)), copies, inputs_both=inputs_both
    )

    def reduced(own_half, other_half, base, targets):
        other = swap_cores(other_half)
        mine = (own_half + other.astype(F32)).astype(BF)
        pieces = exchange(mine.reshape(peers, CAP, columns))
        return combine(
            pieces.reshape(EXPERTS, copies, CAP, columns), part_pick, base, targets
        )

    top_part = lax.dynamic_slice(
        top_grad, (major, 0, minor * columns), (1, tokens, columns)
    ).reshape(tokens, columns)
    part = reduced(own_half, other_half, top_part, 1)[0]
    incoming = lax.ppermute(part, "pipe", [(i, i - 1) for i in range(1, sections)])
    base, pieces = deal(last, top_part, incoming, deal_pick, copies)
    own_rows = exchange(pieces.reshape(peers, CAP, columns))
    own_grads = scale_rows(own_rows.reshape(MICRO, copies, CAP, columns), slot_weights)
    sums, grad_gate, grad_up, grad_rows = expert_slopes(
        down, (own_grads, swap_cores(own_grads)), forward, right
    )
    other_sums = swap_cores(sums)
    own_half, other_half, grads = expert_rows(
        gate, up, grad_gate, grad_up, forward[2], copies
    )
    parts = reduced(own_half, other_half, base, peers)
    produced = exchange(parts)
    produced = side_by_side(produced.reshape(MICRO, copies, tokens, columns))

    sums = sums.astype(F32) + jnp.concatenate([other_sums[slots:], other_sums[:slots]]).astype(F32)
    sums = add_copies(sums, copies)
    squares = (
        times(inputs, inputs, 1, 1),
        times(grad_rows, inputs, 1, 1),
        times(grad_rows, grad_rows, 1, 1),
    )
    q_next, basis = finish(
        dp_index,
        sums,
        squares,
        (inputs, grad_rows),
        grads,
        replicas * rows,
    )
    return (
        produced.reshape(1, MICRO, tokens, D),
        basis.T[None, None, None],
        q_next.transpose(0, 2, 1)[None, None, None],
    )


def solution(mesh):
    placed = (
        P("pipe", None, "dp", None),
        P(None, "dp", None),
        P("pipe", None, "dp", None),
        P("pipe", None, "dp", None),
        P("pipe", "expert", None, None, "dp"),
        P("pipe", "expert", None, None, "dp"),
        P("pipe", "expert", None, "dp", None),
        P("pipe", "expert", None, None, "dp", None),
    )
    return jax.shard_map(
        shards,
        mesh=mesh,
        in_specs=placed,
        out_specs=(
            P("pipe", None, "dp", None),
            P("pipe", "expert", None, "dp", None),
            P("pipe", "expert", None, None, "dp", None),
        ),
        check_vma=False,
    )
```
